32 devices in a mesh: sky: 2 (over x), seg: 16 (over z, y, core).
Axes of the slice: x: 2, y: 2, z: 4, core: 2. Of those that a mesh axis runs over, the one named last changes fastest.
Arguments:
- strain_series: bfloat16 [32, 2, 65536], P(('sky', 'seg')), parts along dimension 0, may hold values from -6 to 6
- antenna: float32 [32, 2, 65536], P(('sky', 'seg')), parts along dimension 0, may hold values from -160 to 160, as said below
- drift: int32 [32, 6], P(('sky', 'seg')), parts along dimension 0, may hold values from -2 to 2
- tracks: int32 [64, 16], replicated, may hold values from 0 to 5
Outputs:
- track_stat: float32 [128, 65536], P('sky', 'seg'), parts along dimension 0
The draws below stay inside these ranges and needn't reach their ends.
There are 2 independent parts, one for each index of `sky`. The reference program is written for one: setup_inputs(seed, part) draws one part's arguments, and reference() takes and returns one part's arrays. A program takes and returns all parts, laid end to end along the dimension named above; an argument that names none is the same for every part. Nothing has to cross between parts.
Inputs may be any that keep to these rules, and one draw needn't show every extreme that they name: `antenna`: row 0 holds the a weights, row 1 the b weights of each segment.
All inputs are finite; a program needn't handle non-finite values.
Results may differ from the reference program's by a relative error of at most 0.0015.
Values sent between devices are 32-bit elements; how exact they have to be, the bound alone decides.
A program may use at most 192 MiB of HBM per device.

```python
import math
import jax
import jax.numpy as jnp
from jax import lax

NBIN = 65536
DFT_ROWS = 256
BLK = 128
DMAX = 2
KCOH = 6
NTRACK = 64
NSEG = 16


def draw_antenna(key, part):
    key_noise = jax.random.fold_in(key, 11)
    key_corr = jax.random.fold_in(key, 12)
    key_level = jax.random.fold_in(key, 13)
    noise = jnp.clip(jax.random.normal(key_noise, (NSEG, 2, NBIN), jnp.float32), -5.0, 5.0)
    levels = jax.random.uniform(key_level, (NSEG, 16), jnp.float32, 0.0, math.log(10.0))
    corr = jax.random.uniform(key_corr, (NSEG, 1), jnp.float32, -0.995, 0.995)
    envelope = jnp.repeat(jnp.exp(levels), NBIN // 16, axis=1)
    first = envelope * noise[:, 0]
    second = envelope * (corr * noise[:, 0] + jnp.sqrt(1.0 - corr * corr) * noise[:, 1])
    return jnp.stack([first, second], 1)


def plant(array, key, low, largest):
    longest = array.shape.index(max(array.shape))
    spots = []
    for shift in (0, 1):
        where = [jax.random.randint(jax.random.fold_in(key, axis), (), 0, length) for axis, length in enumerate(array.shape)]
        where[longest] = (where[longest] + shift) % array.shape[longest]
        spots.append(tuple(where))
    return array.at[spots[0]].set(low).at[spots[1]].set(largest)


def steps_of(stream_key, dims, shards, smallest, high):
    loudness, own = 1.0, jax.random.fold_in(stream_key, 6)
    for axis_at, shards_of in shards:
        heights = jnp.exp(jax.random.uniform(jax.random.fold_in(own, axis_at), (shards_of,), jnp.float32, smallest / len(shards), high / len(shards)))
        loudness = loudness * jnp.repeat(heights, dims[axis_at] // shards_of).reshape([-1 if axis == axis_at else 1 for axis in range(len(dims))])
    return loudness


def bell_draw(rng, dims, scale, most, cuts=(), kind=jnp.bfloat16):
    result = scale * jax.random.normal(rng, dims, jnp.float32)
    if cuts:
        result = result * steps_of(rng, dims, cuts, -0.22, 0.18)
    return jnp.clip(result, -most, most).astype(kind)


def setup_inputs(seed: int = 0, part: int = 0) -> dict:
    keys = jax.random.split(jax.random.key(seed), 5)
    part_splits = jax.random.split(jax.random.fold_in(keys[4], part), 5)
    strain_series = bell_draw(part_splits[0], (NSEG, 2, NBIN), 1.0, 6.0, ((0, 16),))
    antenna = draw_antenna(jax.random.fold_in(jax.random.fold_in(keys[4], part), 71), part)
    drift = plant(jax.random.randint(part_splits[2], (NSEG, KCOH), 0 - DMAX, DMAX + 1), jax.random.fold_in(part_splits[2], 1), 0 - DMAX, DMAX).astype(jnp.int32)
    tracks = plant(jax.random.randint(keys[3], (NTRACK, NSEG), 0, KCOH), jax.random.fold_in(keys[3], 1), 0, KCOH - 1).astype(jnp.int32)
    return {"strain_series": strain_series, "antenna": antenna, "drift": drift, "tracks": tracks}


chirp_step = 3.0
tiny_eps = 1e-6


def section_tables(points, first_rows):
    second_rows = points // first_rows
    outer_index = jnp.arange(first_rows, dtype=jnp.int32)
    inner_index = jnp.arange(second_rows, dtype=jnp.int32)
    first_angle = (2.0 * math.pi / first_rows) * ((outer_index[:, None] * outer_index[None, :]) % first_rows).astype(jnp.float32)
    cos_one, sin_one = jnp.cos(first_angle), jnp.sin(first_angle)
    left_table = jnp.stack([jnp.stack([cos_one, sin_one]), jnp.stack([-sin_one, cos_one])]).astype(jnp.bfloat16)
    second_angle = (2.0 * math.pi / second_rows) * ((inner_index[:, None] * inner_index[None, :]) % second_rows).astype(jnp.float32)
    cos_two, sin_two = jnp.cos(second_angle), jnp.sin(second_angle)
    right_table = jnp.stack([jnp.stack([cos_two, -sin_two]), jnp.stack([sin_two, cos_two])]).astype(jnp.bfloat16)
    twist_angle = (2.0 * math.pi / points) * ((outer_index[:, None] * inner_index[None, :]) % points).astype(jnp.float32)
    return left_table, right_table, jnp.cos(twist_angle), jnp.sin(twist_angle)


def coherent_stat(series, weights, left_table, right_table, twist_cos, twist_sin):
    seg_rows = series.shape[0]
    points = series.shape[2]
    first_rows = left_table.shape[2]
    second_rows = points // first_rows
    position = jnp.arange(points, dtype=jnp.float32) / points
    chirp_rate = (jnp.arange(KCOH, dtype=jnp.float32) - (KCOH - 1) / 2.0) * chirp_step
    phases = (2.0 * math.pi) * chirp_rate[:, None] * (position * position)[None, :]
    phase_cos, phase_sin = jnp.cos(phases), jnp.sin(phases)
    series_real = series[:, 0].astype(jnp.float32)[:, None, :]
    series_imag = series[:, 1].astype(jnp.float32)[:, None, :]
    demod_real = series_real * phase_cos + series_imag * phase_sin
    demod_imag = series_imag * phase_cos - series_real * phase_sin
    weight_a = weights[:, 0][:, None, :]
    weight_b = weights[:, 1][:, None, :]
    with_a = jnp.stack([weight_a * demod_real, weight_a * demod_imag], 2)
    with_b = jnp.stack([weight_b * demod_real, weight_b * demod_imag], 2)
    weighted = jnp.stack([with_a, with_b], 2).astype(jnp.bfloat16)
    weighted = weighted.reshape(seg_rows * KCOH * 2, 2, first_rows, second_rows)
    section_one = jnp.einsum('oikn,binm->bokm', left_table.astype(jnp.float32), weighted.astype(jnp.float32))
    one_real, one_imag = section_one[:, 0], section_one[:, 1]
    twisted_real = one_real * twist_cos + one_imag * twist_sin
    twisted_imag = one_imag * twist_cos - one_real * twist_sin
    middle = jnp.stack([twisted_real, twisted_imag], 1).astype(jnp.bfloat16)
    spectra = jnp.einsum('bikm,ioml->bolk', middle.astype(jnp.float32), right_table.astype(jnp.float32))
    spectra = spectra.reshape(seg_rows, KCOH, 2, 2, points)
    a_real, a_imag = spectra[:, :, 0, 0], spectra[:, :, 0, 1]
    b_real, b_imag = spectra[:, :, 1, 0], spectra[:, :, 1, 1]
    weight_aa = jnp.mean(weights[:, 0] * weights[:, 0], axis=-1) + tiny_eps
    weight_bb = jnp.mean(weights[:, 1] * weights[:, 1], axis=-1) + tiny_eps
    weight_ab = jnp.mean(weights[:, 0] * weights[:, 1], axis=-1)
    determinant = jnp.maximum(weight_aa * weight_bb - weight_ab * weight_ab, 0.1 * weight_aa * weight_bb)
    energy = (weight_bb[:, None, None] * (a_real * a_real + a_imag * a_imag)
              + weight_aa[:, None, None] * (b_real * b_real + b_imag * b_imag)
              - 2.0 * weight_ab[:, None, None] * (a_real * b_real + a_imag * b_imag))
    return energy / (points * determinant[:, None, None])


def drift_blocks(padded, offsets, extent, amount):
    summed = jnp.zeros(padded.shape[:-2] + (amount, padded.shape[-1]), padded.dtype)
    for offset in range(-extent, extent + 1):
        window = padded[..., extent - offset:extent - offset + amount, :]
        summed = summed + jnp.where((offsets == offset)[..., None, None], window, 0.0)
    return summed


def reference(strain_series, antenna, drift, tracks):
    left_table, right_table, twist_cos, twist_sin = section_tables(NBIN, DFT_ROWS)

    def one_segment(item):
        series, weights = item
        return coherent_stat(series[None], weights[None], left_table, right_table, twist_cos, twist_sin)[0]

    stats = lax.map(one_segment, (strain_series, antenna))
    blocks = stats.reshape(NSEG, KCOH, NBIN // BLK, BLK)
    padded = jnp.pad(blocks, ((0, 0), (0, 0), (DMAX, DMAX), (0, 0)))
    moved = drift_blocks(padded, drift, DMAX, NBIN // BLK).reshape(NSEG, KCOH, NBIN)
    levels = jnp.arange(KCOH, dtype=jnp.int32)
    pick = (tracks[:, :, None] == levels[None, None, :]).astype(jnp.float32)
    summed = jnp.einsum('jsk,skf->jf', pick, moved, precision=lax.Precision.HIGHEST)
    return summed / NSEG
```

```python
import functools
import math

import jax
import jax.numpy as jnp
import numpy as np
from jax import lax
from jax.experimental import pallas as pl
from jax.experimental.pallas import tpu as pltpu
from jax.sharding import PartitionSpec as P

DFT_ROWS = 256
BLK = 128
KCOH = 6
LEVELS = KCOH // 2
PAD = 8
HALO = 16
MESH = pl.DeviceIdType.MESH

chirp_step = 3.0
tiny_eps = 1e-06


def dft_table(rows):
    index = np.arange(rows, dtype=np.int64)
    angle = np.float32(2.0 * math.pi / rows) * (index[:, None] * index[None, :] % rows).astype(np.float32)
    cos, sin = np.cos(angle), np.sin(angle)
    return np.block([[cos, sin], [-sin, cos]]).astype(jnp.bfloat16)


def twist_table(points, first_rows):
    second_rows = points // first_rows
    outer = np.arange(first_rows, dtype=np.int64)
    inner = np.arange(second_rows, dtype=np.int64)
    angle = np.float32(2.0 * math.pi / points) * (outer[:, None] * inner[None, :] % points).astype(np.float32)
    return np.stack([np.cos(angle), np.sin(angle)]).astype(np.float32)


def chirp_table(points, first_rows):
    position = np.arange(points, dtype=np.float32) / np.float32(points)
    rate = (np.arange(LEVELS, KCOH, dtype=np.float32) - np.float32((KCOH - 1) / 2.0)) * np.float32(chirp_step)
    phases = (np.float32(2.0 * math.pi) * rate)[:, None] * (position * position)[None, :]
    both = np.stack([np.cos(phases), np.sin(phases)], 1).astype(np.float32)
    return both.reshape(LEVELS, 2, first_rows, points // first_rows)


def kernel(
    count, drift_hbm, series_hbm, antenna_hbm, chirp_hbm, twist_hbm, table_hbm, tracks_hbm, out_ref,
    drift, series_in, series, antenna, chirp, twist, table, tracks,
    strain, weights, weighted, spread, middle, spectra, padded,
    send, recv, gather, total_far, from_far,
    load_sem, chirp_sem, send_sem, far_sem, near_sem, gather_sem, total_sem,
):
    _, first_rows, second_rows = strain.shape
    rows = second_rows // count
    half_count = count // 2
    half_rows = second_rows // 2
    points = first_rows * second_rows
    halves = first_rows // BLK
    sky = lax.axis_index("sky")
    me = lax.axis_index("seg")
    side = lax.div(me, half_count)
    place_in = lax.rem(me, half_count)
    far = (1 - side) * half_count
    near = side * half_count
    mirror = far + place_in

    loads = [
        pltpu.make_async_copy(source, target, load_sem.at[index])
        for index, (source, target) in enumerate([
            (series_hbm, series_in), (antenna_hbm, antenna), (table_hbm, table), (twist_hbm, twist), (drift_hbm, drift),
            (tracks_hbm, tracks),
        ])
    ]
    chirp_load = lambda level: pltpu.make_async_copy(chirp_hbm.at[level], chirp.at[level], chirp_sem.at[level])
    loads[0].start()
    loads[1].start()
    chirp_load(0).start()
    for load in loads[2:]:
        load.start()

    barrier = pltpu.get_barrier_semaphore()

    def greet(step, carry):
        pl.semaphore_signal(barrier, inc=1, device_id=(sky, lax.rem(me + step, count)), device_id_type=MESH)
        return carry

    lax.fori_loop(1, count, greet, 0)

    for which in range(2):
        for half in range(halves):
            padded[which, half, :PAD] = jnp.zeros((PAD, BLK), jnp.float32)
            padded[which, half, PAD + second_rows :] = jnp.zeros((PAD, BLK), jnp.float32)
    send[1] = jnp.zeros(send.shape[1:], jnp.float32)

    loads[0].wait()
    series[...] = series_in[...].astype(jnp.float32)
    loads[1].wait()
    pieces = second_rows // BLK
    for which in range(2):
        for piece in range(pieces):
            lanes = slice(piece * BLK, (piece + 1) * BLK)
            lines = pl.ds(piece, first_rows, stride=pieces)
            strain[which, :, lanes] = series[lines, which, :]
            weights[which, :, lanes] = antenna[lines, which, :]

    weight_a, weight_b = weights[0], weights[1]
    total = lambda value: jnp.sum(jnp.sum(value, axis=0, keepdims=True), axis=1, keepdims=True)
    aa = total(weight_a * weight_a) / points + tiny_eps
    bb = total(weight_b * weight_b) / points + tiny_eps
    ab = total(weight_a * weight_b) / points
    scale = 1.0 / (points * jnp.maximum(aa * bb - ab * ab, 0.1 * aa * bb))
    coef_a, coef_b, coef_ab = bb * scale, aa * scale, 2.0 * ab * scale

    for load in loads[2:]:
        load.wait()
    for level in range(1, LEVELS):
        chirp_load(level).start()

    def second_stage(start, size):
        start = pl.multiple_of(start, HALO)
        for which in range(4):
            for part in range(2):
                spectra[which, part, :size] = lax.dot_general(
                    table[pl.ds(part * second_rows + start, size), :], middle[which], (((1,), (1,)), ((), ())),
                    preferred_element_type=jnp.float32,
                )
        for which in range(2):
            a_real, a_imag = spectra[2 * which, 0, :size], spectra[2 * which, 1, :size]
            b_real, b_imag = spectra[2 * which + 1, 0, :size], spectra[2 * which + 1, 1, :size]
            value = (
                coef_a * (a_real * a_real + a_imag * a_imag)
                + coef_b * (b_real * b_real + b_imag * b_imag)
                - coef_ab * (a_real * b_real + a_imag * b_imag)
            )
            for half in range(halves):
                padded[which, half, pl.ds(PAD + start, size), :] = value[:, half * BLK : (half + 1) * BLK]

    def place(level, first_device):
        for which in (1, 0):
            shift = drift[0, (LEVELS + level) if which == 0 else (LEVELS - 1 - level)]
            channel = 2 * level + which
            for half in range(halves):
                block = half - shift + halves * PAD
                source = lax.rem(block, halves)
                start = lax.div(block, halves)
                lanes = slice(half * BLK, (half + 1) * BLK)
                if rows % 8 == 0:
                    devices = pl.ds(first_device, half_count)
                    value = padded[which, source, pl.ds(start + first_device * rows, half_rows), :]
                    base = send[1, devices, :, lanes]
                    send[channel, devices, :, lanes] = value.reshape(half_count, rows, BLK) - base
                else:
                    def one(step, carry, which=which, channel=channel, source=source, start=start, lanes=lanes):
                        peer = first_device + step
                        value = padded[which, source, pl.ds(start + peer * rows, rows), :]
                        send[channel, peer, :, lanes] = value - send[1, peer, :, lanes]
                        return carry

                    lax.fori_loop(0, half_count, one, 0)

    def push(source, target, done, arrived, peer):
        pltpu.make_async_remote_copy(
            src_ref=source, dst_ref=target, send_sem=done, recv_sem=arrived, device_id=(sky, peer), device_id_type=MESH
        ).start()

    def ship_far(channel):
        def one(step, carry):
            peer = far + lax.rem(place_in + step, half_count)
            push(send.at[channel, peer], recv.at[channel, me], send_sem.at[channel], far_sem.at[channel], peer)
            return carry

        lax.fori_loop(0, half_count, one, 0)

    def ship_near(channel):
        def one(step, carry):
            peer = near + lax.rem(place_in + step, half_count)
            push(send.at[channel, peer], recv.at[channel, me], send_sem.at[channel], near_sem.at[channel], peer)
            return carry

        lax.fori_loop(1, half_count, one, 0)
        pltpu.make_async_copy(send.at[channel, me], recv.at[channel, me], near_sem.at[channel]).start()

    def ship_base():
        def one(step, carry):
            other = lax.rem(place_in + step, half_count)
            push(send.at[1, far + other], gather.at[place_in], send_sem.at[1], gather_sem, near + other)
            return carry

        lax.fori_loop(1, half_count, one, 0)
        pltpu.make_async_copy(send.at[1, mirror], gather.at[place_in], gather_sem).start()

    def one_level(level, carry):
        chirp_load(level).wait()
        chirp_cos, chirp_sin = chirp[level, 0], chirp[level, 1]
        real, imag = strain[0], strain[1]
        real_cos, imag_sin = real * chirp_cos, imag * chirp_sin
        imag_cos, real_sin = imag * chirp_cos, real * chirp_sin
        demods = ((real_cos + imag_sin, imag_cos - real_sin), (real_cos - imag_sin, imag_cos + real_sin))
        for which in range(4):
            weight = weights[which % 2]
            for part in range(2):
                lines = slice(part * first_rows, (part + 1) * first_rows)
                weighted[which, lines, :] = (weight * demods[which // 2][part]).astype(jnp.bfloat16)
        twist_cos, twist_sin = twist[0], twist[1]
        for which in range(4):
            spread[which] = jnp.dot(table[...], weighted[which], preferred_element_type=jnp.float32)
            one_real, one_imag = spread[which, :first_rows], spread[which, first_rows:]
            middle[which, :, :second_rows] = (one_real * twist_cos + one_imag * twist_sin).astype(jnp.bfloat16)
            middle[which, :, second_rows:] = (one_imag * twist_cos - one_real * twist_sin).astype(jnp.bfloat16)

        second_stage((1 - side) * (half_rows - HALO), half_rows + HALO)
        place(level, far)

        @pl.when(level == 0)
        def _():
            pl.semaphore_wait(barrier, count - 1)

        ship_far(2 * level)

        @pl.when(level > 0)
        def _():
            ship_far(2 * level + 1)

        second_stage(side * (half_rows + HALO), half_rows - HALO)
        place(level, near)

        @pl.when(level == 0)
        def _():
            ship_base()

        ship_near(2 * level + 1)
        ship_near(2 * level)

        @pl.when(level == LEVELS - 2)
        def _():
            pltpu.make_async_copy(gather, gather, gather_sem).wait()
            total_far[...] = jnp.sum(gather[...], axis=0)
            push(total_far, from_far, total_sem.at[0], total_sem.at[1], mirror)

        return carry

    lax.fori_loop(0, LEVELS, one_level, 0)

    out_ref[...] = jnp.zeros_like(out_ref)
    far_devices, near_devices = pl.ds(far, half_count), pl.ds(near, half_count)
    await_bytes = lambda part, arrived: pltpu.make_async_copy(part, part, arrived).wait()

    def collect(step, carry):
        channel = jnp.where(step == 0, 0, step + 1)

        @pl.when(step == KCOH - 2)
        def _():
            await_bytes(recv.at[1, near_devices], near_sem.at[1])
            await_bytes(from_far, total_sem.at[1])
            base = jnp.sum(recv[1, near_devices], axis=0) + from_far[...]
            for row in range(rows):
                columns = slice(row * first_rows, (row + 1) * first_rows)
                out_ref[:, columns] += base[row : row + 1, :]

        await_bytes(recv.at[channel, near_devices], near_sem.at[channel])
        await_bytes(recv.at[channel, far_devices], far_sem.at[channel])
        level = lax.div(channel, 2)
        rate = jnp.where(lax.rem(channel, 2) == 0, LEVELS + level, LEVELS - 1 - level)
        pick = jnp.where(tracks[...] == rate, 1.0, 0.0).astype(jnp.bfloat16)
        pick = jnp.concatenate([pick, pick], axis=0)
        for row in range(rows):
            value = recv[channel, :, row, :]
            high = value.astype(jnp.bfloat16)
            low = (value - high.astype(jnp.float32)).astype(jnp.bfloat16)
            columns = slice(row * first_rows, (row + 1) * first_rows)
            out_ref[:, columns] += lax.dot_general(
                pick, jnp.concatenate([high, low], axis=0), (((0,), (0,)), ((), ())), preferred_element_type=jnp.float32
            )
        return carry

    lax.fori_loop(0, KCOH - 1, collect, 0)

    for channel in range(KCOH):
        if channel == 1:
            part = send.at[1, pl.ds(0, 2 * (half_count - 1))]
        else:
            part = send.at[channel, pl.ds(0, count - 1)]
        await_bytes(part, send_sem.at[channel])
    await_bytes(total_far, total_sem.at[0])


def local(count, strain_series, antenna, drift, tracks):
    points = strain_series.shape[2]
    first_rows, second_rows = DFT_ROWS, points // DFT_ROWS
    segments = tracks.shape[1]
    rows = second_rows // count
    blocked = lambda array: array.reshape(2, points // BLK, BLK).transpose(1, 0, 2)
    hbm = pl.BlockSpec(memory_space=pl.ANY)
    chirps = chirp_table(points, first_rows)
    block = (points // BLK, 2, BLK)
    summed = pl.pallas_call(
        functools.partial(kernel, count),
        out_shape=pltpu.VMEM((tracks.shape[0], points // count), jnp.float32),
        in_specs=[hbm] * 7,
        out_specs=pl.BlockSpec(memory_space=pltpu.VMEM),
        scratch_shapes=[
            pltpu.SMEM(drift.shape, jnp.int32),
            pltpu.VMEM(block, jnp.bfloat16),
            pltpu.VMEM(block, jnp.float32),
            pltpu.VMEM(block, jnp.float32),
            pltpu.VMEM(chirps.shape, jnp.float32),
            pltpu.VMEM((2, first_rows, second_rows), jnp.float32),
            pltpu.VMEM((2 * first_rows, 2 * first_rows), jnp.bfloat16),
            pltpu.VMEM((segments, tracks.shape[0]), jnp.int32),
            pltpu.VMEM((2, first_rows, second_rows), jnp.float32),
            pltpu.VMEM((2, first_rows, second_rows), jnp.float32),
            pltpu.VMEM((4, 2 * first_rows, second_rows), jnp.bfloat16),
            pltpu.VMEM((4, 2 * first_rows, second_rows), jnp.float32),
            pltpu.VMEM((4, first_rows, 2 * second_rows), jnp.bfloat16),
            pltpu.VMEM((4, 2, second_rows // 2 + HALO, first_rows), jnp.float32),
            pltpu.VMEM((2, first_rows // BLK, second_rows + 2 * PAD, BLK), jnp.float32),
            pltpu.VMEM((KCOH, count, rows, first_rows), jnp.float32),
            pltpu.VMEM((KCOH, count, rows, first_rows), jnp.float32),
            pltpu.VMEM((count // 2, rows, first_rows), jnp.float32),
            pltpu.VMEM((rows, first_rows), jnp.float32),
            pltpu.VMEM((rows, first_rows), jnp.float32),
            pltpu.SemaphoreType.DMA((6,)),
            pltpu.SemaphoreType.DMA((LEVELS,)),
            pltpu.SemaphoreType.DMA((KCOH,)),
            pltpu.SemaphoreType.DMA((KCOH,)),
            pltpu.SemaphoreType.DMA((KCOH,)),
            pltpu.SemaphoreType.DMA,
            pltpu.SemaphoreType.DMA((2,)),
        ],
        compiler_params=pltpu.CompilerParams(
            collective_id=0, has_side_effects=True, vmem_limit_bytes=60 << 20
        ),
    )(
        drift,
        blocked(strain_series),
        blocked(antenna),
        jnp.asarray(chirps),
        jnp.asarray(twist_table(points, first_rows)),
        jnp.asarray(dft_table(first_rows)),
        tracks.T,
    )
    return summed / segments


def solution(mesh):
    return jax.shard_map(
        functools.partial(local, mesh.shape["seg"]),
        mesh=mesh,
        in_specs=(
            P(("sky", "seg"), None, None),
            P(("sky", "seg"), None, None),
            P(("sky", "seg"), None),
            P(),
        ),
        out_specs=P("sky", "seg"),
        check_vma=False,
    )
```

```python
import functools
import math

import jax
import jax.numpy as jnp
import numpy as np
from jax import lax
from jax.experimental import pallas as pl
from jax.experimental.pallas import tpu as pltpu
from jax.sharding import PartitionSpec as P

DFT_ROWS = 256
BLK = 128
KCOH = 6
LEVELS = KCOH // 2
PAD = 8
HALO = 16
MESH = pl.DeviceIdType.MESH

chirp_step = 3.0
tiny_eps = 1e-06


def dft_table(rows):
    index = np.arange(rows, dtype=np.int64)
    angle = np.float32(2.0 * math.pi / rows) * (index[:, None] * index[None, :] % rows).astype(np.float32)
    cos, sin = np.cos(angle), np.sin(angle)
    return np.block([[cos, sin], [-sin, cos]]).astype(jnp.bfloat16)


def twist_table(points, first_rows):
    second_rows = points // first_rows
    outer = np.arange(first_rows, dtype=np.int64)
    inner = np.arange(second_rows, dtype=np.int64)
    angle = np.float32(2.0 * math.pi / points) * (outer[:, None] * inner[None, :] % points).astype(np.float32)
    return np.stack([np.cos(angle), np.sin(angle)]).astype(np.float32)


def chirp_table(points, first_rows):
    position = np.arange(points, dtype=np.float32) / np.float32(points)
    rate = (np.arange(LEVELS, KCOH, dtype=np.float32) - np.float32((KCOH - 1) / 2.0)) * np.float32(chirp_step)
    phases = (np.float32(2.0 * math.pi) * rate)[:, None] * (position * position)[None, :]
    both = np.stack([np.cos(phases), np.sin(phases)], 1).astype(np.float32)
    return both.reshape(LEVELS, 2, first_rows, points // first_rows)


def kernel(
    count, drift_hbm, series_hbm, antenna_hbm, chirp_hbm, twist_hbm, table_hbm, tracks_hbm, out_ref,
    drift, series_in, series, antenna, chirp, twist, table, tracks,
    strain, weights, weighted, spread, middle, spectra, padded,
    send, recv, gather, total_far, from_far,
    load_sem, chirp_sem, send_sem, far_sem, near_sem, gather_sem, total_sem,
):
    _, first_rows, second_rows = strain.shape
    rows = second_rows // count
    half_count = count // 2
    half_rows = second_rows // 2
    points = first_rows * second_rows
    halves = first_rows // BLK
    sky = lax.axis_index("sky")
    me = lax.axis_index("seg")
    side = lax.div(me, half_count)
    place_in = lax.rem(me, half_count)
    far = (1 - side) * half_count
    near = side * half_count
    mirror = far + place_in

    loads = [
        pltpu.make_async_copy(source, target, load_sem.at[index])
        for index, (source, target) in enumerate([
            (series_hbm, series_in), (antenna_hbm, antenna), (table_hbm, table), (twist_hbm, twist), (drift_hbm, drift),
            (tracks_hbm, tracks),
        ])
    ]
    chirp_load = lambda level: pltpu.make_async_copy(chirp_hbm.at[level], chirp.at[level], chirp_sem.at[level])
    loads[0].start()
    loads[1].start()
    chirp_load(0).start()
    for load in loads[2:]:
        load.start()

    barrier = pltpu.get_barrier_semaphore()

    def greet(step, carry):
        pl.semaphore_signal(barrier, inc=1, device_id=(sky, lax.rem(me + step, count)), device_id_type=MESH)
        return carry

    lax.fori_loop(1, count, greet, 0)

    for which in range(2):
        for half in range(halves):
            padded[which, half, :PAD] = jnp.zeros((PAD, BLK), jnp.float32)
            padded[which, half, PAD + second_rows :] = jnp.zeros((PAD, BLK), jnp.float32)
    send[1] = jnp.zeros(send.shape[1:], jnp.float32)

    loads[0].wait()
    series[...] = series_in[...].astype(jnp.float32)
    loads[1].wait()
    pieces = second_rows // BLK
    for which in range(2):
        for piece in range(pieces):
            lanes = slice(piece * BLK, (piece + 1) * BLK)
            lines = pl.ds(piece, first_rows, stride=pieces)
            strain[which, :, lanes] = series[lines, which, :]
            weights[which, :, lanes] = antenna[lines, which, :]

    weight_a, weight_b = weights[0], weights[1]
    total = lambda value: jnp.sum(jnp.sum(value, axis=0, keepdims=True), axis=1, keepdims=True)
    aa = total(weight_a * weight_a) / points + tiny_eps
    bb = total(weight_b * weight_b) / points + tiny_eps
    ab = total(weight_a * weight_b) / points
    scale = 1.0 / (points * jnp.maximum(aa * bb - ab * ab, 0.1 * aa * bb))
    coef_a, coef_b, coef_ab = bb * scale, aa * scale, 2.0 * ab * scale

    for load in loads[2:]:
        load.wait()
    for level in range(1, LEVELS):
        chirp_load(level).start()

    def second_stage(start, size):
        start = pl.multiple_of(start, HALO)
        for which in range(4):
            for part in range(2):
                spectra[which, part, :size] = lax.dot_general(
                    table[pl.ds(part * second_rows + start, size), :], middle[which], (((1,), (1,)), ((), ())),
                    preferred_element_type=jnp.float32,
                )
        for which in range(2):
            a_real, a_imag = spectra[2 * which, 0, :size], spectra[2 * which, 1, :size]
            b_real, b_imag = spectra[2 * which + 1, 0, :size], spectra[2 * which + 1, 1, :size]
            value = (
                coef_a * (a_real * a_real + a_imag * a_imag)
                + coef_b * (b_real * b_real + b_imag * b_imag)
                - coef_ab * (a_real * b_real + a_imag * b_imag)
            )
            for half in range(halves):
                padded[which, half, pl.ds(PAD + start, size), :] = value[:, half * BLK : (half + 1) * BLK]

    def place(level, first_device):
        for which in (1, 0):
            shift = drift[0, (LEVELS + level) if which == 0 else (LEVELS - 1 - level)]
            channel = 2 * level + which
            for half in range(halves):
                block = half - shift + halves * PAD
                source = lax.rem(block, halves)
                start = lax.div(block, halves)
                lanes = slice(half * BLK, (half + 1) * BLK)
                if rows % 8 == 0:
                    devices = pl.ds(first_device, half_count)
                    value = padded[which, source, pl.ds(start + first_device * rows, half_rows), :]
                    base = send[1, devices, :, lanes]
                    send[channel, devices, :, lanes] = value.reshape(half_count, rows, BLK) - base
                else:
                    def one(step, carry, which=which, channel=channel, source=source, start=start, lanes=lanes):
                        peer = first_device + step
                        value = padded[which, source, pl.ds(start + peer * rows, rows), :]
                        send[channel, peer, :, lanes] = value - send[1, peer, :, lanes]
                        return carry

                    lax.fori_loop(0, half_count, one, 0)

    def push(source, target, done, arrived, peer):
        pltpu.make_async_remote_copy(
            src_ref=source, dst_ref=target, send_sem=done, recv_sem=arrived, device_id=(sky, peer), device_id_type=MESH
        ).start()

    def ship_far(channel):
        def one(step, carry):
            peer = jnp.where(side == 0, count - 1 - step, step)
            push(send.at[channel, peer], recv.at[channel, me], send_sem.at[channel], far_sem.at[channel], peer)
            return carry

        lax.fori_loop(0, half_count, one, 0)

    def ship_near(channel):
        def one(step, carry):
            peer = near + lax.rem(place_in + step, half_count)
            push(send.at[channel, peer], recv.at[channel, me], send_sem.at[channel], near_sem.at[channel], peer)
            return carry

        lax.fori_loop(1, half_count, one, 0)
        pltpu.make_async_copy(send.at[channel, me], recv.at[channel, me], near_sem.at[channel]).start()

    def ship_base():
        def one(step, carry):
            other = lax.rem(place_in + step, half_count)
            push(send.at[1, far + other], gather.at[place_in], send_sem.at[1], gather_sem, near + other)
            return carry

        lax.fori_loop(1, half_count, one, 0)
        pltpu.make_async_copy(send.at[1, mirror], gather.at[place_in], gather_sem).start()

    def one_level(level, carry):
        chirp_load(level).wait()
        chirp_cos, chirp_sin = chirp[level, 0], chirp[level, 1]
        real, imag = strain[0], strain[1]
        real_cos, imag_sin = real * chirp_cos, imag * chirp_sin
        imag_cos, real_sin = imag * chirp_cos, real * chirp_sin
        demods = ((real_cos + imag_sin, imag_cos - real_sin), (real_cos - imag_sin, imag_cos + real_sin))
        for which in range(4):
            weight = weights[which % 2]
            for part in range(2):
                lines = slice(part * first_rows, (part + 1) * first_rows)
                weighted[which, lines, :] = (weight * demods[which // 2][part]).astype(jnp.bfloat16)
        twist_cos, twist_sin = twist[0], twist[1]
        for which in range(4):
            spread[which] = jnp.dot(table[...], weighted[which], preferred_element_type=jnp.float32)
            one_real, one_imag = spread[which, :first_rows], spread[which, first_rows:]
            middle[which, :, :second_rows] = (one_real * twist_cos + one_imag * twist_sin).astype(jnp.bfloat16)
            middle[which, :, second_rows:] = (one_imag * twist_cos - one_real * twist_sin).astype(jnp.bfloat16)

        second_stage((1 - side) * (half_rows - HALO), half_rows + HALO)
        place(level, far)

        @pl.when(level == 0)
        def _():
            pl.semaphore_wait(barrier, count - 1)

        ship_far(2 * level)

        @pl.when(level > 0)
        def _():
            ship_far(2 * level + 1)

        second_stage(side * (half_rows + HALO), half_rows - HALO)
        place(level, near)

        @pl.when(level == 0)
        def _():
            ship_base()

        ship_near(2 * level + 1)
        ship_near(2 * level)

        @pl.when(level == LEVELS - 2)
        def _():
            pltpu.make_async_copy(gather, gather, gather_sem).wait()
            total_far[...] = jnp.sum(gather[...], axis=0)
            push(total_far, from_far, total_sem.at[0], total_sem.at[1], mirror)

        return carry

    lax.fori_loop(0, LEVELS, one_level, 0)

    out_ref[...] = jnp.zeros_like(out_ref)
    far_devices, near_devices = pl.ds(far, half_count), pl.ds(near, half_count)
    await_bytes = lambda part, arrived: pltpu.make_async_copy(part, part, arrived).wait()

    def collect(step, carry):
        channel = jnp.where(step == 0, 0, step + 1)

        @pl.when(step == KCOH - 2)
        def _():
            await_bytes(recv.at[1, near_devices], near_sem.at[1])
            await_bytes(from_far, total_sem.at[1])
            base = jnp.sum(recv[1, near_devices], axis=0) + from_far[...]
            for row in range(rows):
                columns = slice(row * first_rows, (row + 1) * first_rows)
                out_ref[:, columns] += base[row : row + 1, :]

        await_bytes(recv.at[channel, near_devices], near_sem.at[channel])
        await_bytes(recv.at[channel, far_devices], far_sem.at[channel])
        level = lax.div(channel, 2)
        rate = jnp.where(lax.rem(channel, 2) == 0, LEVELS + level, LEVELS - 1 - level)
        pick = jnp.where(tracks[...] == rate, 1.0, 0.0).astype(jnp.bfloat16)
        pick = jnp.concatenate([pick, pick], axis=0)
        for row in range(rows):
            value = recv[channel, :, row, :]
            high = value.astype(jnp.bfloat16)
            low = (value - high.astype(jnp.float32)).astype(jnp.bfloat16)
            columns = slice(row * first_rows, (row + 1) * first_rows)
            out_ref[:, columns] += lax.dot_general(
                pick, jnp.concatenate([high, low], axis=0), (((0,), (0,)), ((), ())), preferred_element_type=jnp.float32
            )
        return carry

    lax.fori_loop(0, KCOH - 1, collect, 0)

    for channel in range(KCOH):
        if channel == 1:
            part = send.at[1, pl.ds(0, 2 * (half_count - 1))]
        else:
            part = send.at[channel, pl.ds(0, count - 1)]
        await_bytes(part, send_sem.at[channel])
    await_bytes(total_far, total_sem.at[0])


def local(count, strain_series, antenna, drift, tracks):
    points = strain_series.shape[2]
    first_rows, second_rows = DFT_ROWS, points // DFT_ROWS
    segments = tracks.shape[1]
    rows = second_rows // count
    blocked = lambda array: array.reshape(2, points // BLK, BLK).transpose(1, 0, 2)
    hbm = pl.BlockSpec(memory_space=pl.ANY)
    chirps = chirp_table(points, first_rows)
    block = (points // BLK, 2, BLK)
    summed = pl.pallas_call(
        functools.partial(kernel, count),
        out_shape=pltpu.VMEM((tracks.shape[0], points // count), jnp.float32),
        in_specs=[hbm] * 7,
        out_specs=pl.BlockSpec(memory_space=pltpu.VMEM),
        scratch_shapes=[
            pltpu.SMEM(drift.shape, jnp.int32),
            pltpu.VMEM(block, jnp.bfloat16),
            pltpu.VMEM(block, jnp.float32),
            pltpu.VMEM(block, jnp.float32),
            pltpu.VMEM(chirps.shape, jnp.float32),
            pltpu.VMEM((2, first_rows, second_rows), jnp.float32),
            pltpu.VMEM((2 * first_rows, 2 * first_rows), jnp.bfloat16),
            pltpu.VMEM((segments, tracks.shape[0]), jnp.int32),
            pltpu.VMEM((2, first_rows, second_rows), jnp.float32),
            pltpu.VMEM((2, first_rows, second_rows), jnp.float32),
            pltpu.VMEM((4, 2 * first_rows, second_rows), jnp.bfloat16),
            pltpu.VMEM((4, 2 * first_rows, second_rows), jnp.float32),
            pltpu.VMEM((4, first_rows, 2 * second_rows), jnp.bfloat16),
            pltpu.VMEM((4, 2, second_rows // 2 + HALO, first_rows), jnp.float32),
            pltpu.VMEM((2, first_rows // BLK, second_rows + 2 * PAD, BLK), jnp.float32),
            pltpu.VMEM((KCOH, count, rows, first_rows), jnp.float32),
            pltpu.VMEM((KCOH, count, rows, first_rows), jnp.float32),
            pltpu.VMEM((count // 2, rows, first_rows), jnp.float32),
            pltpu.VMEM((rows, first_rows), jnp.float32),
            pltpu.VMEM((rows, first_rows), jnp.float32),
            pltpu.SemaphoreType.DMA((6,)),
            pltpu.SemaphoreType.DMA((LEVELS,)),
            pltpu.SemaphoreType.DMA((KCOH,)),
            pltpu.SemaphoreType.DMA((KCOH,)),
            pltpu.SemaphoreType.DMA((KCOH,)),
            pltpu.SemaphoreType.DMA,
            pltpu.SemaphoreType.DMA((2,)),
        ],
        compiler_params=pltpu.CompilerParams(
            collective_id=0, has_side_effects=True, vmem_limit_bytes=60 << 20
        ),
    )(
        drift,
        blocked(strain_series),
        blocked(antenna),
        jnp.asarray(chirps),
        jnp.asarray(twist_table(points, first_rows)),
        jnp.asarray(dft_table(first_rows)),
        tracks.T,
    )
    return summed / segments


def solution(mesh):
    return jax.shard_map(
        functools.partial(local, mesh.shape["seg"]),
        mesh=mesh,
        in_specs=(
            P(("sky", "seg"), None, None),
            P(("sky", "seg"), None, None),
            P(("sky", "seg"), None),
            P(),
        ),
        out_specs=P("sky", "seg"),
        check_vma=False,
    )
```

```python
import functools
import math

import jax
import jax.numpy as jnp
import numpy as np
from jax import lax
from jax.experimental import pallas as pl
from jax.experimental.pallas import tpu as pltpu
from jax.sharding import PartitionSpec as P

DFT_ROWS = 256
BLK = 128
KCOH = 6
LEVELS = KCOH // 2
PAD = 8
HALO = 16
MESH = pl.DeviceIdType.MESH

chirp_step = 3.0
tiny_eps = 1e-06


def dft_table(rows):
    index = np.arange(rows, dtype=np.int64)
    angle = np.float32(2.0 * math.pi / rows) * (index[:, None] * index[None, :] % rows).astype(np.float32)
    cos, sin = np.cos(angle), np.sin(angle)
    return np.block([[cos, sin], [-sin, cos]]).astype(jnp.bfloat16)


def twist_table(points, first_rows):
    second_rows = points // first_rows
    outer = np.arange(first_rows, dtype=np.int64)
    inner = np.arange(second_rows, dtype=np.int64)
    angle = np.float32(2.0 * math.pi / points) * (outer[:, None] * inner[None, :] % points).astype(np.float32)
    return np.stack([np.cos(angle), np.sin(angle)]).astype(np.float32)


def chirp_table(points, first_rows):
    position = np.arange(points, dtype=np.float32) / np.float32(points)
    rate = (np.arange(LEVELS, KCOH, dtype=np.float32) - np.float32((KCOH - 1) / 2.0)) * np.float32(chirp_step)
    phases = (np.float32(2.0 * math.pi) * rate)[:, None] * (position * position)[None, :]
    both = np.stack([np.cos(phases), np.sin(phases)], 1).astype(np.float32)
    return both.reshape(LEVELS, 2, first_rows, points // first_rows)


def kernel(
    count, drift_hbm, series_hbm, antenna_hbm, chirp_hbm, twist_hbm, table_hbm, tracks_hbm, out_ref,
    drift, series_in, series, antenna, chirp, twist, table, tracks,
    strain, weights, weighted, spread, middle, spectra, padded,
    send, recv, gather, total_far, from_far, picks, staged,
    load_sem, chirp_sem, send_sem, far_sem, near_sem, gather_sem, total_sem,
):
    _, first_rows, second_rows = strain.shape
    halves = first_rows // BLK
    blocks = second_rows * halves // count
    half_count = count // 2
    half_rows = second_rows // 2
    points = first_rows * second_rows
    sky = lax.axis_index("sky")
    me = lax.axis_index("seg")
    side = lax.div(me, half_count)
    place_in = lax.rem(me, half_count)
    far = (1 - side) * half_count
    near = side * half_count
    mirror = far + place_in

    loads = [
        pltpu.make_async_copy(source, target, load_sem.at[index])
        for index, (source, target) in enumerate([
            (series_hbm, series_in), (antenna_hbm, antenna), (table_hbm, table), (twist_hbm, twist), (drift_hbm, drift),
            (tracks_hbm, tracks),
        ])
    ]
    chirp_load = lambda level: pltpu.make_async_copy(chirp_hbm.at[level], chirp.at[level], chirp_sem.at[level])
    loads[0].start()
    loads[1].start()
    chirp_load(0).start()
    for load in loads[2:]:
        load.start()

    barrier = pltpu.get_barrier_semaphore()

    def greet(step, carry):
        pl.semaphore_signal(barrier, inc=1, device_id=(sky, lax.rem(me + step, count)), device_id_type=MESH)
        return carry

    lax.fori_loop(1, count, greet, 0)

    for which in range(2):
        padded[which, :PAD] = jnp.zeros((PAD, BLK), jnp.float32)
        padded[which, PAD + second_rows * halves :] = jnp.zeros((PAD, BLK), jnp.float32)
    send[1] = jnp.zeros(send.shape[1:], jnp.float32)

    loads[0].wait()
    series[...] = series_in[...].astype(jnp.float32)
    loads[1].wait()
    pieces = second_rows // BLK
    for which in range(2):
        for piece in range(pieces):
            lanes = slice(piece * BLK, (piece + 1) * BLK)
            lines = pl.ds(2 * piece + which, first_rows, stride=2 * pieces)
            strain[which, :, lanes] = series[lines, :]
            weights[which, :, lanes] = antenna[lines, :]

    weight_a, weight_b = weights[0], weights[1]
    total = lambda value: jnp.sum(jnp.sum(value, axis=0, keepdims=True), axis=1, keepdims=True)
    aa = total(weight_a * weight_a) / points + tiny_eps
    bb = total(weight_b * weight_b) / points + tiny_eps
    ab = total(weight_a * weight_b) / points
    scale = 1.0 / (points * jnp.maximum(aa * bb - ab * ab, 0.1 * aa * bb))
    coef_a, coef_b, coef_ab = bb * scale, aa * scale, 2.0 * ab * scale

    for load in loads[2:]:
        load.wait()
    for level in range(1, LEVELS):
        chirp_load(level).start()

    def second_stage(start, size):
        start = pl.multiple_of(start, HALO)
        for which in range(4):
            for part in range(2):
                spectra[which, part, :size] = lax.dot_general(
                    table[pl.ds(part * second_rows + start, size), :], middle[which], (((1,), (1,)), ((), ())),
                    preferred_element_type=jnp.float32,
                )
        for which in range(2):
            a_real, a_imag = spectra[2 * which, 0, :size], spectra[2 * which, 1, :size]
            b_real, b_imag = spectra[2 * which + 1, 0, :size], spectra[2 * which + 1, 1, :size]
            value = (
                coef_a * (a_real * a_real + a_imag * a_imag)
                + coef_b * (b_real * b_real + b_imag * b_imag)
                - coef_ab * (a_real * b_real + a_imag * b_imag)
            )
            for half in range(halves):
                lines = pl.ds(PAD + halves * start + half, size, stride=halves)
                padded[which, lines, :] = value[:, half * BLK : (half + 1) * BLK]

    def place(level, first_device):
        for which in (1, 0):
            shift = drift[0, (LEVELS + level) if which == 0 else (LEVELS - 1 - level)]
            channel = 2 * level + which
            if blocks % 8 == 0:
                devices = pl.ds(first_device, half_count)
                value = padded[which, pl.ds(PAD + first_device * blocks - shift, half_count * blocks), :]
                send[channel, devices] = value.reshape(half_count, blocks, BLK) - send[1, devices]
            else:
                def one(step, carry, which=which, channel=channel, shift=shift):
                    peer = first_device + step
                    value = padded[which, pl.ds(PAD + peer * blocks - shift, blocks), :]
                    send[channel, peer] = value - send[1, peer]
                    return carry

                lax.fori_loop(0, half_count, one, 0)

    def push(source, target, done, arrived, peer):
        pltpu.make_async_remote_copy(
            src_ref=source, dst_ref=target, send_sem=done, recv_sem=arrived, device_id=(sky, peer), device_id_type=MESH
        ).start()

    def ship_far(channel):
        def one(step, carry):
            peer = jnp.where(side == 0, count - 1 - step, step)
            push(send.at[channel, peer], recv.at[channel, me], send_sem.at[channel], far_sem.at[channel], peer)
            return carry

        lax.fori_loop(0, half_count, one, 0)

    def ship_near(channel):
        def one(step, carry):
            peer = near + lax.rem(place_in + step, half_count)
            push(send.at[channel, peer], recv.at[channel, me], send_sem.at[channel], near_sem.at[channel], peer)
            return carry

        lax.fori_loop(1, half_count, one, 0)
        pltpu.make_async_copy(send.at[channel, me], recv.at[channel, me], near_sem.at[channel]).start()

    def ship_base():
        def one(step, carry):
            other = lax.rem(place_in + step, half_count)
            push(send.at[1, far + other], gather.at[place_in], send_sem.at[1], gather_sem, near + other)
            return carry

        lax.fori_loop(1, half_count, one, 0)
        pltpu.make_async_copy(send.at[1, mirror], gather.at[place_in], gather_sem).start()

    def one_level(level, carry):
        chirp_load(level).wait()
        chirp_cos, chirp_sin = chirp[level, 0], chirp[level, 1]
        real, imag = strain[0], strain[1]
        real_cos, imag_sin = real * chirp_cos, imag * chirp_sin
        imag_cos, real_sin = imag * chirp_cos, real * chirp_sin
        demods = ((real_cos + imag_sin, imag_cos - real_sin), (real_cos - imag_sin, imag_cos + real_sin))
        for which in range(4):
            weight = weights[which % 2]
            for part in range(2):
                lines = slice(part * first_rows, (part + 1) * first_rows)
                weighted[which, lines, :] = (weight * demods[which // 2][part]).astype(jnp.bfloat16)
        twist_cos, twist_sin = twist[0], twist[1]
        for which in range(4):
            spread[which] = jnp.dot(table[...], weighted[which], preferred_element_type=jnp.float32)
            one_real, one_imag = spread[which, :first_rows], spread[which, first_rows:]
            middle[which, :, :second_rows] = (one_real * twist_cos + one_imag * twist_sin).astype(jnp.bfloat16)
            middle[which, :, second_rows:] = (one_imag * twist_cos - one_real * twist_sin).astype(jnp.bfloat16)

        second_stage((1 - side) * (half_rows - HALO), half_rows + HALO)
        place(level, far)

        @pl.when(level == 0)
        def _():
            pl.semaphore_wait(barrier, count - 1)

        ship_far(2 * level)

        @pl.when(level > 0)
        def _():
            ship_far(2 * level + 1)

        second_stage(side * (half_rows + HALO), half_rows - HALO)
        place(level, near)

        @pl.when(level == 0)
        def _():
            ship_base()

        ship_near(2 * level + 1)
        ship_near(2 * level)

        @pl.when(level == LEVELS - 2)
        def _():
            pltpu.make_async_copy(gather, gather, gather_sem).wait()
            total_far[...] = jnp.sum(gather[...], axis=0)
            push(total_far, from_far, total_sem.at[0], total_sem.at[1], mirror)

        return carry

    lax.fori_loop(0, LEVELS, one_level, 0)

    far_devices, near_devices = pl.ds(far, half_count), pl.ds(near, half_count)
    await_bytes = lambda part, arrived: pltpu.make_async_copy(part, part, arrived).wait()

    channels = [channel for channel in range(KCOH) if channel != 1]
    chosen = []
    for channel in channels:
        rate = LEVELS + channel // 2 if channel % 2 == 0 else LEVELS - 1 - channel // 2
        chosen += [jnp.where(tracks[...] == rate, 1.0, 0.0).astype(jnp.bfloat16)] * 2
    chosen = jnp.concatenate(chosen, axis=0)
    names = tracks.shape[1]
    same = lax.broadcasted_iota(jnp.int32, (names, names), 0) == lax.broadcasted_iota(jnp.int32, (names, names), 1)
    picks[...] = lax.dot_general(
        jnp.where(same, 1.0, 0.0).astype(jnp.bfloat16), chosen, (((1,), (1,)), ((), ())), preferred_element_type=jnp.float32
    ).astype(jnp.bfloat16)

    def stage(step, channel):
        await_bytes(recv.at[channel, near_devices], near_sem.at[channel])
        await_bytes(recv.at[channel, far_devices], far_sem.at[channel])
        line = step * 2 * count if isinstance(step, int) else pl.multiple_of(step * 2 * count, 2 * count)
        arrived = recv.at[channel].reshape(count * blocks, BLK) if blocks % 8 == 0 else None
        for block in range(blocks):
            if blocks % 8 == 0:
                value = arrived[pl.ds(block, count, stride=blocks), :]
            else:
                value = recv[channel, :, block, :]
            high = value.astype(jnp.bfloat16)
            lanes = slice(block * BLK, (block + 1) * BLK)
            staged[pl.ds(line, count), lanes] = high
            staged[pl.ds(line + count, count), lanes] = (value - high.astype(jnp.float32)).astype(jnp.bfloat16)

    def stage_one(step, carry):
        stage(step, jnp.where(step == 0, 0, step + 1))
        return carry

    lax.fori_loop(0, KCOH - 2, stage_one, 0)
    await_bytes(recv.at[1, near_devices], near_sem.at[1])
    await_bytes(from_far, total_sem.at[1])
    base = jnp.sum(recv[1, near_devices], axis=0) + from_far[...]
    early = (KCOH - 2) * 2 * count
    width = halves * BLK
    parts = blocks // halves
    for part in range(parts):
        columns = slice(part * width, (part + 1) * width)
        line = jnp.concatenate([base[part * halves + half : part * halves + half + 1, :] for half in range(halves)], axis=1)
        out_ref[:, columns] = line + jnp.dot(
            picks[:, :early], staged[:early, columns], preferred_element_type=jnp.float32
        )
    stage(KCOH - 2, channels[-1])
    for part in range(parts):
        columns = slice(part * width, (part + 1) * width)
        out_ref[:, columns] += jnp.dot(picks[:, early:], staged[early:, columns], preferred_element_type=jnp.float32)

    for channel in range(KCOH):
        if channel == 1:
            part = send.at[1, pl.ds(0, 2 * (half_count - 1))]
        else:
            part = send.at[channel, pl.ds(0, count - 1)]
        await_bytes(part, send_sem.at[channel])
    await_bytes(total_far, total_sem.at[0])


def local(count, strain_series, antenna, drift, tracks):
    points = strain_series.shape[2]
    first_rows, second_rows = DFT_ROWS, points // DFT_ROWS
    segments = tracks.shape[1]
    blocks = points // count // BLK
    blocked = lambda array: array.reshape(2, points // BLK, BLK).transpose(1, 0, 2).reshape(2 * points // BLK, BLK)
    hbm = pl.BlockSpec(memory_space=pl.ANY)
    chirps = chirp_table(points, first_rows)
    block = (2 * points // BLK, BLK)
    summed = pl.pallas_call(
        functools.partial(kernel, count),
        out_shape=pltpu.VMEM((tracks.shape[0], points // count), jnp.float32),
        in_specs=[hbm] * 7,
        out_specs=pl.BlockSpec(memory_space=pltpu.VMEM),
        scratch_shapes=[
            pltpu.SMEM(drift.shape, jnp.int32),
            pltpu.VMEM(block, jnp.bfloat16),
            pltpu.VMEM(block, jnp.float32),
            pltpu.VMEM(block, jnp.float32),
            pltpu.VMEM(chirps.shape, jnp.float32),
            pltpu.VMEM((2, first_rows, second_rows), jnp.float32),
            pltpu.VMEM((2 * first_rows, 2 * first_rows), jnp.bfloat16),
            pltpu.VMEM((segments, tracks.shape[0]), jnp.int32),
            pltpu.VMEM((2, first_rows, second_rows), jnp.float32),
            pltpu.VMEM((2, first_rows, second_rows), jnp.float32),
            pltpu.VMEM((4, 2 * first_rows, second_rows), jnp.bfloat16),
            pltpu.VMEM((4, 2 * first_rows, second_rows), jnp.float32),
            pltpu.VMEM((4, first_rows, 2 * second_rows), jnp.bfloat16),
            pltpu.VMEM((4, 2, second_rows // 2 + HALO, first_rows), jnp.float32),
            pltpu.VMEM((2, points // BLK + 2 * PAD, BLK), jnp.float32),
            pltpu.VMEM((KCOH, count, blocks, BLK), jnp.float32),
            pltpu.VMEM((KCOH, count, blocks, BLK), jnp.float32),
            pltpu.VMEM((count // 2, blocks, BLK), jnp.float32),
            pltpu.VMEM((blocks, BLK), jnp.float32),
            pltpu.VMEM((blocks, BLK), jnp.float32),
            pltpu.VMEM((tracks.shape[0], (KCOH - 1) * 2 * count), jnp.bfloat16),
            pltpu.VMEM(((KCOH - 1) * 2 * count, points // count), jnp.bfloat16),
            pltpu.SemaphoreType.DMA((6,)),
            pltpu.SemaphoreType.DMA((LEVELS,)),
            pltpu.SemaphoreType.DMA((KCOH,)),
            pltpu.SemaphoreType.DMA((KCOH,)),
            pltpu.SemaphoreType.DMA((KCOH,)),
            pltpu.SemaphoreType.DMA,
            pltpu.SemaphoreType.DMA((2,)),
        ],
        compiler_params=pltpu.CompilerParams(
            collective_id=0, has_side_effects=True, vmem_limit_bytes=60 << 20
        ),
    )(
        drift,
        blocked(strain_series),
        blocked(antenna),
        jnp.asarray(chirps),
        jnp.asarray(twist_table(points, first_rows)),
        jnp.asarray(dft_table(first_rows)),
        tracks.T,
    )
    return summed / segments


def solution(mesh):
    return jax.shard_map(
        functools.partial(local, mesh.shape["seg"]),
        mesh=mesh,
        in_specs=(
            P(("sky", "seg"), None, None),
            P(("sky", "seg"), None, None),
            P(("sky", "seg"), None),
            P(),
        ),
        out_specs=P("sky", "seg"),
        check_vma=False,
    )
```

```python
import functools
import math

import jax
import jax.numpy as jnp
import numpy as np
from jax import lax
from jax.experimental import pallas as pl
from jax.experimental.pallas import tpu as pltpu
from jax.sharding import PartitionSpec as P

DFT_ROWS = 256
BLK = 128
KCOH = 6
LEVELS = KCOH // 2
PAD = 8
HALO = 16
MESH = pl.DeviceIdType.MESH

chirp_step = 3.0
tiny_eps = 1e-06


def dft_table(rows):
    index = np.arange(rows, dtype=np.int64)
    angle = np.float32(2.0 * math.pi / rows) * (index[:, None] * index[None, :] % rows).astype(np.float32)
    cos, sin = np.cos(angle), np.sin(angle)
    return np.block([[cos, sin], [-sin, cos]]).astype(jnp.bfloat16)


def twist_table(points, first_rows):
    second_rows = points // first_rows
    outer = np.arange(first_rows, dtype=np.int64)
    inner = np.arange(second_rows, dtype=np.int64)
    angle = np.float32(2.0 * math.pi / points) * (outer[:, None] * inner[None, :] % points).astype(np.float32)
    return np.stack([np.cos(angle), np.sin(angle)]).astype(np.float32)


def chirp_table(points, first_rows):
    position = np.arange(points, dtype=np.float32) / np.float32(points)
    rate = (np.arange(LEVELS, KCOH, dtype=np.float32) - np.float32((KCOH - 1) / 2.0)) * np.float32(chirp_step)
    phases = (np.float32(2.0 * math.pi) * rate)[:, None] * (position * position)[None, :]
    both = np.stack([np.cos(phases), np.sin(phases)], 1).astype(np.float32)
    return both.reshape(LEVELS, 2, first_rows, points // first_rows)


def kernel(
    count, drift_hbm, series_hbm, antenna_hbm, chirp_hbm, twist_hbm, table_hbm, tracks_hbm, out_ref,
    drift, series_in, series, antenna, chirp, twist, table, tracks,
    strain, weights, weighted, spread, middle, spectra, padded,
    send, recv, gather, total_far, from_far, picks, staged,
    load_sem, chirp_sem, send_sem, far_sem, near_sem, gather_sem, total_sem, late_sem,
):
    _, first_rows, second_rows = strain.shape
    halves = first_rows // BLK
    blocks = second_rows * halves // count
    half_count = count // 2
    early_count = half_count + half_count // 2
    late_count = count - early_count
    flat = blocks % 8 == 0
    slot = lambda device: pl.ds(pl.multiple_of(device * blocks, blocks), blocks) if flat else device
    span = lambda device: pl.ds(pl.multiple_of(device * blocks, blocks), half_count * blocks) if flat else pl.ds(device, half_count)
    half_rows = second_rows // 2
    points = first_rows * second_rows
    sky = lax.axis_index("sky")
    me = lax.axis_index("seg")
    side = lax.div(me, half_count)
    place_in = lax.rem(me, half_count)
    far = (1 - side) * half_count
    near = side * half_count
    mirror = far + place_in

    loads = [
        pltpu.make_async_copy(source, target, load_sem.at[index])
        for index, (source, target) in enumerate([
            (series_hbm, series_in), (antenna_hbm, antenna), (table_hbm, table), (twist_hbm, twist), (drift_hbm, drift),
            (tracks_hbm, tracks),
        ])
    ]
    chirp_load = lambda level: pltpu.make_async_copy(chirp_hbm.at[level], chirp.at[level], chirp_sem.at[level])
    loads[0].start()
    loads[1].start()
    chirp_load(0).start()
    for load in loads[2:]:
        load.start()

    barrier = pltpu.get_barrier_semaphore()

    is_early = me < early_count

    def signal(semaphore, first, wide):
        def one(step, carry):
            peer = lax.rem(me + step, count) if wide else first + step
            pl.semaphore_signal(semaphore, inc=1, device_id=(sky, peer), device_id_type=MESH)
            return carry

        return one

    @pl.when(is_early)
    def _():
        lax.fori_loop(1, count, signal(barrier, 0, True), 0)

    @pl.when(jnp.logical_not(is_early))
    def _():
        lax.fori_loop(0, me - early_count, signal(barrier, early_count, False), 0)
        lax.fori_loop(me - early_count + 1, late_count, signal(barrier, early_count, False), 0)

    for which in range(2):
        padded[which, :PAD] = jnp.zeros((PAD, BLK), jnp.float32)
        padded[which, PAD + second_rows * halves :] = jnp.zeros((PAD, BLK), jnp.float32)
    send[1] = jnp.zeros(send.shape[1:], jnp.float32)

    @pl.when(jnp.logical_not(is_early))
    def _():
        pl.semaphore_wait(barrier, count - 1)
        lax.fori_loop(0, early_count, signal(late_sem, 0, False), 0)

    loads[0].wait()
    series[...] = series_in[...].astype(jnp.float32)
    loads[1].wait()
    pieces = second_rows // BLK
    for which in range(2):
        for piece in range(pieces):
            lanes = slice(piece * BLK, (piece + 1) * BLK)
            lines = pl.ds(2 * piece + which, first_rows, stride=2 * pieces)
            strain[which, :, lanes] = series[lines, :]
            weights[which, :, lanes] = antenna[lines, :]

    weight_a, weight_b = weights[0], weights[1]
    total = lambda value: jnp.sum(jnp.sum(value, axis=0, keepdims=True), axis=1, keepdims=True)
    aa = total(weight_a * weight_a) / points + tiny_eps
    bb = total(weight_b * weight_b) / points + tiny_eps
    ab = total(weight_a * weight_b) / points
    scale = 1.0 / (points * jnp.maximum(aa * bb - ab * ab, 0.1 * aa * bb))
    coef_a, coef_b, coef_ab = bb * scale, aa * scale, 2.0 * ab * scale

    for load in loads[2:]:
        load.wait()
    for level in range(1, LEVELS):
        chirp_load(level).start()

    def second_stage(start, size):
        start = pl.multiple_of(start, HALO)
        for which in range(4):
            for part in range(2):
                spectra[which, part, :size] = lax.dot_general(
                    table[pl.ds(part * second_rows + start, size), :], middle[which], (((1,), (1,)), ((), ())),
                    preferred_element_type=jnp.float32,
                )
        for which in range(2):
            a_real, a_imag = spectra[2 * which, 0, :size], spectra[2 * which, 1, :size]
            b_real, b_imag = spectra[2 * which + 1, 0, :size], spectra[2 * which + 1, 1, :size]
            value = (
                coef_a * (a_real * a_real + a_imag * a_imag)
                + coef_b * (b_real * b_real + b_imag * b_imag)
                - coef_ab * (a_real * b_real + a_imag * b_imag)
            )
            for half in range(halves):
                lines = pl.ds(PAD + halves * start + half, size, stride=halves)
                padded[which, lines, :] = value[:, half * BLK : (half + 1) * BLK]

    def place(level, first_device):
        for which in (1, 0):
            shift = drift[0, (LEVELS + level) if which == 0 else (LEVELS - 1 - level)]
            channel = 2 * level + which
            if flat:
                devices = pl.ds(first_device, half_count)
                value = padded[which, pl.ds(PAD + first_device * blocks - shift, half_count * blocks), :]
                send[channel, devices] = value.reshape(half_count, blocks, BLK) - send[1, devices]
            else:
                def one(step, carry, which=which, channel=channel, shift=shift):
                    peer = first_device + step
                    value = padded[which, pl.ds(PAD + peer * blocks - shift, blocks), :]
                    send[channel, peer] = value - send[1, peer]
                    return carry

                lax.fori_loop(0, half_count, one, 0)

    def push(source, target, done, arrived, peer):
        pltpu.make_async_remote_copy(
            src_ref=source, dst_ref=target, send_sem=done, recv_sem=arrived, device_id=(sky, peer), device_id_type=MESH
        ).start()

    def ship_far(channel, first=0, last=half_count, ascending=False):
        def one(step, carry):
            peer = jnp.where(side == 0, half_count + step if ascending else count - 1 - step, step)
            push(send.at[channel, peer], recv.at[channel, slot(me)], send_sem.at[channel], far_sem.at[channel], peer)
            return carry

        lax.fori_loop(first, last, one, 0)

    def ship_near(channel):
        def one(step, carry):
            peer = near + lax.rem(place_in + step, half_count)
            push(send.at[channel, peer], recv.at[channel, slot(me)], send_sem.at[channel], near_sem.at[channel], peer)
            return carry

        lax.fori_loop(1, half_count, one, 0)
        pltpu.make_async_copy(send.at[channel, me], recv.at[channel, slot(me)], near_sem.at[channel]).start()

    def ship_base():
        def one(step, carry):
            other = lax.rem(place_in + step, half_count)
            push(send.at[1, far + other], gather.at[place_in], send_sem.at[1], gather_sem, near + other)
            return carry

        lax.fori_loop(1, half_count, one, 0)
        pltpu.make_async_copy(send.at[1, mirror], gather.at[place_in], gather_sem).start()

    def one_level(level, carry):
        chirp_load(level).wait()
        chirp_cos, chirp_sin = chirp[level, 0], chirp[level, 1]
        real, imag = strain[0], strain[1]
        real_cos, imag_sin = real * chirp_cos, imag * chirp_sin
        imag_cos, real_sin = imag * chirp_cos, real * chirp_sin
        demods = ((real_cos + imag_sin, imag_cos - real_sin), (real_cos - imag_sin, imag_cos + real_sin))
        for which in range(4):
            weight = weights[which % 2]
            for part in range(2):
                lines = slice(part * first_rows, (part + 1) * first_rows)
                weighted[which, lines, :] = (weight * demods[which // 2][part]).astype(jnp.bfloat16)
        twist_cos, twist_sin = twist[0], twist[1]
        for which in range(4):
            spread[which] = jnp.dot(table[...], weighted[which], preferred_element_type=jnp.float32)
            one_real, one_imag = spread[which, :first_rows], spread[which, first_rows:]
            middle[which, :, :second_rows] = (one_real * twist_cos + one_imag * twist_sin).astype(jnp.bfloat16)
            middle[which, :, second_rows:] = (one_imag * twist_cos - one_real * twist_sin).astype(jnp.bfloat16)

        second_stage((1 - side) * (half_rows - HALO), half_rows + HALO)
        place(level, far)

        @pl.when(jnp.logical_and(level == 0, is_early))
        def _():
            pl.semaphore_wait(barrier, early_count - 1)

        @pl.when(level == 0)
        def _():
            ship_far(0, 0, half_count // 2, ascending=True)

        @pl.when(jnp.logical_and(level == 0, side == 0))
        def _():
            pl.semaphore_wait(late_sem, late_count)

        @pl.when(level == 0)
        def _():
            ship_far(0, half_count // 2, half_count, ascending=True)

        @pl.when(jnp.logical_and(level == 0, jnp.logical_and(side == 1, is_early)))
        def _():
            pl.semaphore_wait(late_sem, late_count)

        @pl.when(level > 0)
        def _():
            ship_far(2 * level)
            ship_far(2 * level + 1)

        second_stage(side * (half_rows + HALO), half_rows - HALO)
        place(level, near)

        @pl.when(level == 0)
        def _():
            ship_base()

        ship_near(2 * level + 1)
        ship_near(2 * level)

        @pl.when(level == LEVELS - 2)
        def _():
            pltpu.make_async_copy(gather, gather, gather_sem).wait()
            total_far[...] = jnp.sum(gather[...], axis=0)
            push(total_far, from_far, total_sem.at[0], total_sem.at[1], mirror)

        return carry

    lax.fori_loop(0, LEVELS, one_level, 0)

    far_devices, near_devices = span(far), span(near)
    await_bytes = lambda part, arrived: pltpu.make_async_copy(part, part, arrived).wait()

    channels = [channel for channel in range(KCOH) if channel != 1]
    chosen = []
    for channel in channels:
        rate = LEVELS + channel // 2 if channel % 2 == 0 else LEVELS - 1 - channel // 2
        chosen += [jnp.where(tracks[...] == rate, 1.0, 0.0).astype(jnp.bfloat16)] * 2
    chosen = jnp.concatenate(chosen, axis=0)
    names = tracks.shape[1]
    same = lax.broadcasted_iota(jnp.int32, (names, names), 0) == lax.broadcasted_iota(jnp.int32, (names, names), 1)
    picks[...] = lax.dot_general(
        jnp.where(same, 1.0, 0.0).astype(jnp.bfloat16), chosen, (((1,), (1,)), ((), ())), preferred_element_type=jnp.float32
    ).astype(jnp.bfloat16)

    def stage(step, channel):
        await_bytes(recv.at[channel, near_devices], near_sem.at[channel])
        await_bytes(recv.at[channel, far_devices], far_sem.at[channel])
        line = step * 2 * count if isinstance(step, int) else pl.multiple_of(step * 2 * count, 2 * count)
        for block in range(blocks):
            if flat:
                value = recv[channel, pl.ds(block, count, stride=blocks), :]
            else:
                value = recv[channel, :, block, :]
            high = value.astype(jnp.bfloat16)
            lanes = slice(block * BLK, (block + 1) * BLK)
            staged[pl.ds(line, count), lanes] = high
            staged[pl.ds(line + count, count), lanes] = (value - high.astype(jnp.float32)).astype(jnp.bfloat16)

    def stage_one(step, carry):
        stage(step, jnp.where(step == 0, 0, step + 1))
        return carry

    lax.fori_loop(0, KCOH - 2, stage_one, 0)
    await_bytes(recv.at[1, near_devices], near_sem.at[1])
    await_bytes(from_far, total_sem.at[1])
    base = jnp.sum(recv[1, near_devices].reshape(half_count, blocks, BLK), axis=0) + from_far[...]
    early = (KCOH - 2) * 2 * count
    width = halves * BLK
    parts = blocks // halves
    for part in range(parts):
        columns = slice(part * width, (part + 1) * width)
        line = jnp.concatenate([base[part * halves + half : part * halves + half + 1, :] for half in range(halves)], axis=1)
        out_ref[:, columns] = line + jnp.dot(
            picks[:, :early], staged[:early, columns], preferred_element_type=jnp.float32
        )
    stage(KCOH - 2, channels[-1])
    for part in range(parts):
        columns = slice(part * width, (part + 1) * width)
        out_ref[:, columns] += jnp.dot(picks[:, early:], staged[early:, columns], preferred_element_type=jnp.float32)

    for channel in range(KCOH):
        if channel == 1:
            part = send.at[1, pl.ds(0, 2 * (half_count - 1))]
        else:
            part = send.at[channel, pl.ds(0, count - 1)]
        await_bytes(part, send_sem.at[channel])
    await_bytes(total_far, total_sem.at[0])


def local(count, strain_series, antenna, drift, tracks):
    points = strain_series.shape[2]
    first_rows, second_rows = DFT_ROWS, points // DFT_ROWS
    segments = tracks.shape[1]
    blocks = points // count // BLK
    blocked = lambda array: array.reshape(2, points // BLK, BLK).transpose(1, 0, 2).reshape(2 * points // BLK, BLK)
    hbm = pl.BlockSpec(memory_space=pl.ANY)
    chirps = chirp_table(points, first_rows)
    block = (2 * points // BLK, BLK)
    summed = pl.pallas_call(
        functools.partial(kernel, count),
        out_shape=pltpu.VMEM((tracks.shape[0], points // count), jnp.float32),
        in_specs=[hbm] * 7,
        out_specs=pl.BlockSpec(memory_space=pltpu.VMEM),
        scratch_shapes=[
            pltpu.SMEM(drift.shape, jnp.int32),
            pltpu.VMEM(block, jnp.bfloat16),
            pltpu.VMEM(block, jnp.float32),
            pltpu.VMEM(block, jnp.float32),
            pltpu.VMEM(chirps.shape, jnp.float32),
            pltpu.VMEM((2, first_rows, second_rows), jnp.float32),
            pltpu.VMEM((2 * first_rows, 2 * first_rows), jnp.bfloat16),
            pltpu.VMEM((segments, tracks.shape[0]), jnp.int32),
            pltpu.VMEM((2, first_rows, second_rows), jnp.float32),
            pltpu.VMEM((2, first_rows, second_rows), jnp.float32),
            pltpu.VMEM((4, 2 * first_rows, second_rows), jnp.bfloat16),
            pltpu.VMEM((4, 2 * first_rows, second_rows), jnp.float32),
            pltpu.VMEM((4, first_rows, 2 * second_rows), jnp.bfloat16),
            pltpu.VMEM((4, 2, second_rows // 2 + HALO, first_rows), jnp.float32),
            pltpu.VMEM((2, points // BLK + 2 * PAD, BLK), jnp.float32),
            pltpu.VMEM((KCOH, count, blocks, BLK), jnp.float32),
            pltpu.VMEM((KCOH, count * blocks, BLK) if blocks % 8 == 0 else (KCOH, count, blocks, BLK), jnp.float32),
            pltpu.VMEM((count // 2, blocks, BLK), jnp.float32),
            pltpu.VMEM((blocks, BLK), jnp.float32),
            pltpu.VMEM((blocks, BLK), jnp.float32),
            pltpu.VMEM((tracks.shape[0], (KCOH - 1) * 2 * count), jnp.bfloat16),
            pltpu.VMEM(((KCOH - 1) * 2 * count, points // count), jnp.bfloat16),
            pltpu.SemaphoreType.DMA((6,)),
            pltpu.SemaphoreType.DMA((LEVELS,)),
            pltpu.SemaphoreType.DMA((KCOH,)),
            pltpu.SemaphoreType.DMA((KCOH,)),
            pltpu.SemaphoreType.DMA((KCOH,)),
            pltpu.SemaphoreType.DMA,
            pltpu.SemaphoreType.DMA((2,)),
            pltpu.SemaphoreType.REGULAR,
        ],
        compiler_params=pltpu.CompilerParams(
            collective_id=0, has_side_effects=True, vmem_limit_bytes=60 << 20
        ),
    )(
        drift,
        blocked(strain_series),
        blocked(antenna),
        jnp.asarray(chirps),
        jnp.asarray(twist_table(points, first_rows)),
        jnp.asarray(dft_table(first_rows)),
        tracks.T,
    )
    return summed / segments


def solution(mesh):
    return jax.shard_map(
        functools.partial(local, mesh.shape["seg"]),
        mesh=mesh,
        in_specs=(
            P(("sky", "seg"), None, None),
            P(("sky", "seg"), None, None),
            P(("sky", "seg"), None),
            P(),
        ),
        out_specs=P("sky", "seg"),
        check_vma=False,
    )
```

```python
import functools
import math

import jax
import jax.numpy as jnp
import numpy as np
from jax import lax
from jax.experimental import pallas as pl
from jax.experimental.pallas import tpu as pltpu
from jax.sharding import PartitionSpec as P

DFT_ROWS = 256
BLK = 128
KCOH = 6
LEVELS = KCOH // 2
PAD = 8
HALO = 16
MESH = pl.DeviceIdType.MESH

chirp_step = 3.0
tiny_eps = 1e-06


def dft_table(rows):
    index = np.arange(rows, dtype=np.int64)
    angle = np.float32(2.0 * math.pi / rows) * (index[:, None] * index[None, :] % rows).astype(np.float32)
    cos, sin = np.cos(angle), np.sin(angle)
    return np.block([[cos, sin], [-sin, cos]]).astype(jnp.bfloat16)


def twist_table(points, first_rows):
    second_rows = points // first_rows
    outer = np.arange(first_rows, dtype=np.int64)
    inner = np.arange(second_rows, dtype=np.int64)
    angle = np.float32(2.0 * math.pi / points) * (inner[:, None] * outer[None, :] % points).astype(np.float32)
    return np.stack([np.cos(angle), np.sin(angle)]).astype(np.float32)


def chirp_table(points, first_rows):
    position = np.arange(points, dtype=np.float32) / np.float32(points)
    rate = (np.arange(LEVELS, KCOH, dtype=np.float32) - np.float32((KCOH - 1) / 2.0)) * np.float32(chirp_step)
    phases = (np.float32(2.0 * math.pi) * rate)[:, None] * (position * position)[None, :]
    both = np.stack([np.cos(phases), np.sin(phases)], 1).astype(np.float32)
    return np.swapaxes(both.reshape(LEVELS, 2, first_rows, points // first_rows), 2, 3).copy()


def kernel(
    count, drift_hbm, series_hbm, antenna_hbm, chirp_hbm, twist_hbm, table_hbm, tracks_hbm, out_ref,
    drift, series_in, series, antenna, chirp, twist, table, tracks,
    strain, weights, weighted, spread, middle, spectra, padded,
    send, recv, gather, total_far, from_far, picks, staged,
    load_sem, chirp_sem, send_sem, far_sem, near_sem, gather_sem, total_sem, late_sem,
):
    _, second_rows, first_rows = strain.shape
    halves = first_rows // BLK
    blocks = second_rows * halves // count
    half_count = count // 2
    early_count = half_count + half_count // 2
    late_count = count - early_count
    half_rows = second_rows // 2
    points = first_rows * second_rows
    sky = lax.axis_index("sky")
    me = lax.axis_index("seg")
    side = lax.div(me, half_count)
    place_in = lax.rem(me, half_count)
    far = (1 - side) * half_count
    near = side * half_count
    mirror = far + place_in

    loads = [
        pltpu.make_async_copy(source, target, load_sem.at[index])
        for index, (source, target) in enumerate([
            (series_hbm, series_in), (antenna_hbm, antenna), (table_hbm, table), (twist_hbm, twist), (drift_hbm, drift),
            (tracks_hbm, tracks),
        ])
    ]
    chirp_load = lambda level: pltpu.make_async_copy(chirp_hbm.at[level], chirp.at[level], chirp_sem.at[level])
    loads[0].start()
    loads[1].start()
    chirp_load(0).start()
    for load in loads[2:]:
        load.start()

    barrier = pltpu.get_barrier_semaphore()

    is_early = me < early_count

    def signal(semaphore, first, wide):
        def one(step, carry):
            peer = lax.rem(me + step, count) if wide else first + step
            pl.semaphore_signal(semaphore, inc=1, device_id=(sky, peer), device_id_type=MESH)
            return carry

        return one

    @pl.when(is_early)
    def _():
        lax.fori_loop(1, count, signal(barrier, 0, True), 0)

    @pl.when(jnp.logical_not(is_early))
    def _():
        lax.fori_loop(0, me - early_count, signal(barrier, early_count, False), 0)
        lax.fori_loop(me - early_count + 1, late_count, signal(barrier, early_count, False), 0)

    for which in range(2):
        padded[which, :PAD] = jnp.zeros((PAD, BLK), jnp.float32)
        padded[which, PAD + second_rows * halves :] = jnp.zeros((PAD, BLK), jnp.float32)
    send[1] = jnp.zeros(send.shape[1:], jnp.float32)

    @pl.when(jnp.logical_not(is_early))
    def _():
        pl.semaphore_wait(barrier, count - 1)
        lax.fori_loop(0, early_count, signal(late_sem, 0, False), 0)

    pieces = second_rows // BLK

    def turned(source, target):
        for which in range(2):
            for piece in range(pieces):
                lines = pl.ds(2 * piece + which, first_rows, stride=2 * pieces)
                target[which, piece * BLK : (piece + 1) * BLK, :] = source[lines, :].T

    def demodulate(level):
        for first in range(0, second_rows, HALO):
            rows = slice(first, first + HALO)
            chirp_cos, chirp_sin = chirp[level, 0, rows, :], chirp[level, 1, rows, :]
            real, imag = strain[0, rows, :], strain[1, rows, :]
            real_cos, imag_sin = real * chirp_cos, imag * chirp_sin
            imag_cos, real_sin = imag * chirp_cos, real * chirp_sin
            demods = ((real_cos + imag_sin, imag_cos - real_sin), (real_cos - imag_sin, imag_cos + real_sin))
            for kind in range(2):
                weight = weights[kind, rows, :]
                for upper in range(2):
                    start = (2 * upper + kind) * second_rows + first
                    for part in range(2):
                        lanes = slice((1 - part) * first_rows, (2 - part) * first_rows)
                        weighted[start : start + HALO, lanes] = (weight * demods[upper][part]).astype(jnp.bfloat16)

    loads[0].wait()
    series[...] = series_in[...].astype(jnp.float32)
    turned(series, strain)
    loads[1].wait()
    turned(antenna, weights)
    chirp_load(0).wait()
    demodulate(0)

    def coefficients():
        sums = [0.0, 0.0, 0.0]
        for first in range(0, second_rows, HALO):
            rows = slice(first, first + HALO)
            weight_a, weight_b = weights[0, rows, :], weights[1, rows, :]
            sums = [held + value for held, value in zip(sums, (weight_a * weight_a, weight_b * weight_b, weight_a * weight_b))]
        aa, bb, ab = [jnp.sum(jnp.sum(held, axis=0, keepdims=True), axis=1, keepdims=True) / points for held in sums]
        aa, bb = aa + tiny_eps, bb + tiny_eps
        scale = 1.0 / (points * jnp.maximum(aa * bb - ab * ab, 0.1 * aa * bb))
        return bb * scale, aa * scale, 2.0 * ab * scale

    for load in loads[2:]:
        load.wait()
    for level in range(1, LEVELS):
        chirp_load(level).start()

    def second_stage(coefs, start, size):
        coef_a, coef_b, coef_ab = coefs
        start = pl.multiple_of(start, HALO)
        lines = jnp.concatenate([table[pl.ds(start, size), :], table[pl.ds(second_rows + start, size), :]], axis=0)
        for which in range(4):
            spectra[which, : 2 * size] = jnp.dot(lines, middle[which], preferred_element_type=jnp.float32)
        for which in range(2):
            for first in range(0, size, HALO):
                real_rows, imag_rows = slice(first, first + HALO), slice(size + first, size + first + HALO)
                a_real, a_imag = spectra[2 * which, real_rows, :], spectra[2 * which, imag_rows, :]
                b_real, b_imag = spectra[2 * which + 1, real_rows, :], spectra[2 * which + 1, imag_rows, :]
                value = (
                    coef_a * (a_real * a_real + a_imag * a_imag)
                    + coef_b * (b_real * b_real + b_imag * b_imag)
                    - coef_ab * (a_real * b_real + a_imag * b_imag)
                )
                for half in range(halves):
                    lines = pl.ds(PAD + halves * (start + first) + half, HALO, stride=halves)
                    padded[which, lines, :] = value[:, half * BLK : (half + 1) * BLK]

    def place(level, first_device):
        for which in (1, 0):
            shift = drift[0, (LEVELS + level) if which == 0 else (LEVELS - 1 - level)]
            channel = 2 * level + which
            if blocks % 8 == 0:
                devices = pl.ds(first_device, half_count)
                value = padded[which, pl.ds(PAD + first_device * blocks - shift, half_count * blocks), :]
                send[channel, devices] = value.reshape(half_count, blocks, BLK) - send[1, devices]
            else:
                def one(step, carry, which=which, channel=channel, shift=shift):
                    peer = first_device + step
                    value = padded[which, pl.ds(PAD + peer * blocks - shift, blocks), :]
                    send[channel, peer] = value - send[1, peer]
                    return carry

                lax.fori_loop(0, half_count, one, 0)

    def push(source, target, done, arrived, peer):
        pltpu.make_async_remote_copy(
            src_ref=source, dst_ref=target, send_sem=done, recv_sem=arrived, device_id=(sky, peer), device_id_type=MESH
        ).start()

    def ship_far(channel, first=0, last=half_count, ascending=False):
        def one(step, carry):
            peer = jnp.where(side == 0, half_count + step if ascending else count - 1 - step, step)
            push(send.at[channel, peer], recv.at[channel, :, me], send_sem.at[channel], far_sem.at[channel], peer)
            return carry

        lax.fori_loop(first, last, one, 0)

    def ship_near(channel):
        def one(step, carry):
            peer = near + lax.rem(place_in + step, half_count)
            push(send.at[channel, peer], recv.at[channel, :, me], send_sem.at[channel], near_sem.at[channel], peer)
            return carry

        lax.fori_loop(1, half_count, one, 0)
        pltpu.make_async_copy(send.at[channel, me], recv.at[channel, :, me], near_sem.at[channel]).start()

    def ship_base():
        def one(step, carry):
            other = lax.rem(place_in + step, half_count)
            push(send.at[1, far + other], gather.at[place_in], send_sem.at[1], gather_sem, near + other)
            return carry

        lax.fori_loop(1, half_count, one, 0)
        pltpu.make_async_copy(send.at[1, mirror], gather.at[place_in], gather_sem).start()

    def one_level(level, carry):
        spread[...] = jnp.dot(weighted[...], table[...], preferred_element_type=jnp.float32)
        coefs = coefficients()
        for which in range(4):
            for first in range(0, second_rows, HALO):
                rows = slice(first, first + HALO)
                lines = slice(which * second_rows + first, which * second_rows + first + HALO)
                twist_cos, twist_sin = twist[0, rows, :], twist[1, rows, :]
                one_imag, one_real = spread[lines, :first_rows], spread[lines, first_rows:]
                middle[which, first : first + HALO, :] = (one_real * twist_cos + one_imag * twist_sin).astype(jnp.bfloat16)
                middle[which, second_rows + first : second_rows + first + HALO, :] = (
                    one_imag * twist_cos - one_real * twist_sin
                ).astype(jnp.bfloat16)

        second_stage(coefs, (1 - side) * (half_rows - HALO), half_rows + HALO)
        place(level, far)

        @pl.when(jnp.logical_and(level == 0, is_early))
        def _():
            pl.semaphore_wait(barrier, early_count - 1)

        @pl.when(level == 0)
        def _():
            ship_far(0, 0, half_count // 2, ascending=True)

        @pl.when(jnp.logical_and(level == 0, side == 0))
        def _():
            pl.semaphore_wait(late_sem, late_count)

        @pl.when(level == 0)
        def _():
            ship_far(0, half_count // 2, half_count, ascending=True)

        @pl.when(jnp.logical_and(level == 0, jnp.logical_and(side == 1, is_early)))
        def _():
            pl.semaphore_wait(late_sem, late_count)

        @pl.when(level > 0)
        def _():
            ship_far(2 * level)
            ship_far(2 * level + 1)

        second_stage(coefs, side * (half_rows + HALO), half_rows - HALO)
        place(level, near)

        @pl.when(level == 0)
        def _():
            ship_base()

        ship_near(2 * level + 1)
        ship_near(2 * level)

        @pl.when(level == LEVELS - 2)
        def _():
            pltpu.make_async_copy(gather, gather, gather_sem).wait()
            total_far[...] = jnp.sum(gather[...], axis=0)
            push(total_far, from_far, total_sem.at[0], total_sem.at[1], mirror)

        @pl.when(level < LEVELS - 1)
        def _():
            chirp_load(level + 1).wait()
            demodulate(level + 1)

        return carry

    lax.fori_loop(0, LEVELS, one_level, 0)

    far_devices, near_devices = pl.ds(pl.multiple_of(far, half_count), half_count), pl.ds(pl.multiple_of(near, half_count), half_count)
    await_bytes = lambda part, arrived: pltpu.make_async_copy(part, part, arrived).wait()

    channels = [channel for channel in range(KCOH) if channel != 1]
    chosen = []
    for channel in channels:
        rate = LEVELS + channel // 2 if channel % 2 == 0 else LEVELS - 1 - channel // 2
        chosen += [jnp.where(tracks[...] == rate, 1.0, 0.0).astype(jnp.bfloat16)] * 2
    chosen = jnp.concatenate(chosen, axis=0)
    names = tracks.shape[1]
    same = lax.broadcasted_iota(jnp.int32, (names, names), 0) == lax.broadcasted_iota(jnp.int32, (names, names), 1)
    picks[...] = lax.dot_general(
        jnp.where(same, 1.0, 0.0).astype(jnp.bfloat16), chosen, (((1,), (1,)), ((), ())), preferred_element_type=jnp.float32
    ).astype(jnp.bfloat16)

    def stage(step, channel):
        await_bytes(recv.at[channel, :, near_devices], near_sem.at[channel])
        await_bytes(recv.at[channel, :, far_devices], far_sem.at[channel])
        line = step * 2 * count if isinstance(step, int) else pl.multiple_of(step * 2 * count, 2 * count)
        for block in range(blocks):
            value = recv[channel, block]
            high = value.astype(jnp.bfloat16)
            lanes = slice(block * BLK, (block + 1) * BLK)
            staged[pl.ds(line, count), lanes] = high
            staged[pl.ds(line + count, count), lanes] = (value - high.astype(jnp.float32)).astype(jnp.bfloat16)

    def stage_one(step, carry):
        stage(step, jnp.where(step == 0, 0, step + 1))
        return carry

    lax.fori_loop(0, KCOH - 2, stage_one, 0)
    await_bytes(recv.at[1, :, near_devices], near_sem.at[1])
    await_bytes(from_far, total_sem.at[1])
    base = jnp.sum(recv[1, :, near_devices], axis=1) + from_far[...]
    early = (KCOH - 2) * 2 * count
    width = halves * BLK
    parts = blocks // halves
    for part in range(parts):
        columns = slice(part * width, (part + 1) * width)
        line = jnp.concatenate([base[part * halves + half : part * halves + half + 1, :] for half in range(halves)], axis=1)
        out_ref[:, columns] = line + jnp.dot(
            picks[:, :early], staged[:early, columns], preferred_element_type=jnp.float32
        )
    stage(KCOH - 2, channels[-1])
    for part in range(parts):
        columns = slice(part * width, (part + 1) * width)
        out_ref[:, columns] += jnp.dot(picks[:, early:], staged[early:, columns], preferred_element_type=jnp.float32)

    for channel in range(KCOH):
        if channel == 1:
            part = send.at[1, pl.ds(0, 2 * (half_count - 1))]
        else:
            part = send.at[channel, pl.ds(0, count - 1)]
        await_bytes(part, send_sem.at[channel])
    await_bytes(total_far, total_sem.at[0])


def local(count, strain_series, antenna, drift, tracks):
    points = strain_series.shape[2]
    first_rows, second_rows = DFT_ROWS, points // DFT_ROWS
    segments = tracks.shape[1]
    blocks = points // count // BLK
    blocked = lambda array: array.reshape(2, points // BLK, BLK).transpose(1, 0, 2).reshape(2 * points // BLK, BLK)
    hbm = pl.BlockSpec(memory_space=pl.ANY)
    chirps = chirp_table(points, first_rows)
    block = (2 * points // BLK, BLK)
    summed = pl.pallas_call(
        functools.partial(kernel, count),
        out_shape=pltpu.VMEM((tracks.shape[0], points // count), jnp.float32),
        in_specs=[hbm] * 7,
        out_specs=pl.BlockSpec(memory_space=pltpu.VMEM),
        scratch_shapes=[
            pltpu.SMEM(drift.shape, jnp.int32),
            pltpu.VMEM(block, jnp.bfloat16),
            pltpu.VMEM(block, jnp.float32),
            pltpu.VMEM(block, jnp.float32),
            pltpu.VMEM(chirps.shape, jnp.float32),
            pltpu.VMEM((2, second_rows, first_rows), jnp.float32),
            pltpu.VMEM((2 * first_rows, 2 * first_rows), jnp.bfloat16),
            pltpu.VMEM((segments, tracks.shape[0]), jnp.int32),
            pltpu.VMEM((2, second_rows, first_rows), jnp.float32),
            pltpu.VMEM((2, second_rows, first_rows), jnp.float32),
            pltpu.VMEM((4 * second_rows, 2 * first_rows), jnp.bfloat16),
            pltpu.VMEM((4 * second_rows, 2 * first_rows), jnp.float32),
            pltpu.VMEM((4, 2 * second_rows, first_rows), jnp.bfloat16),
            pltpu.VMEM((4, second_rows + 2 * HALO, first_rows), jnp.float32),
            pltpu.VMEM((2, points // BLK + 2 * PAD, BLK), jnp.float32),
            pltpu.VMEM((KCOH, count, blocks, BLK), jnp.float32),
            pltpu.VMEM((KCOH, blocks, count, BLK), jnp.float32),
            pltpu.VMEM((count // 2, blocks, BLK), jnp.float32),
            pltpu.VMEM((blocks, BLK), jnp.float32),
            pltpu.VMEM((blocks, BLK), jnp.float32),
            pltpu.VMEM((tracks.shape[0], (KCOH - 1) * 2 * count), jnp.bfloat16),
            pltpu.VMEM(((KCOH - 1) * 2 * count, points // count), jnp.bfloat16),
            pltpu.SemaphoreType.DMA((6,)),
            pltpu.SemaphoreType.DMA((LEVELS,)),
            pltpu.SemaphoreType.DMA((KCOH,)),
            pltpu.SemaphoreType.DMA((KCOH,)),
            pltpu.SemaphoreType.DMA((KCOH,)),
            pltpu.SemaphoreType.DMA,
            pltpu.SemaphoreType.DMA((2,)),
            pltpu.SemaphoreType.REGULAR,
        ],
        compiler_params=pltpu.CompilerParams(
            collective_id=0, has_side_effects=True, vmem_limit_bytes=60 << 20
        ),
    )(
        drift,
        blocked(strain_series),
        blocked(antenna),
        jnp.asarray(chirps),
        jnp.asarray(twist_table(points, first_rows)),
        jnp.asarray(dft_table(first_rows)),
        tracks.T,
    )
    return summed / segments


def solution(mesh):
    return jax.shard_map(
        functools.partial(local, mesh.shape["seg"]),
        mesh=mesh,
        in_specs=(
            P(("sky", "seg"), None, None),
            P(("sky", "seg"), None, None),
            P(("sky", "seg"), None),
            P(),
        ),
        out_specs=P("sky", "seg"),
        check_vma=False,
    )
```

```python
import functools
import math

import jax
import jax.numpy as jnp
import numpy as np
from jax import lax
from jax.experimental import pallas as pl
from jax.experimental.pallas import tpu as pltpu
from jax.sharding import PartitionSpec as P

DFT_ROWS = 256
BLK = 128
KCOH = 6
LEVELS = KCOH // 2
PAD = 8
HALO = 16
MESH = pl.DeviceIdType.MESH

chirp_step = 3.0
tiny_eps = 1e-06


def dft_table(rows):
    index = np.arange(rows, dtype=np.int64)
    angle = np.float32(2.0 * math.pi / rows) * (index[:, None] * index[None, :] % rows).astype(np.float32)
    cos, sin = np.cos(angle), np.sin(angle)
    return np.block([[cos, sin], [-sin, cos]]).astype(jnp.bfloat16)


def twist_table(points, first_rows):
    second_rows = points // first_rows
    outer = np.arange(first_rows, dtype=np.int64)
    inner = np.arange(second_rows, dtype=np.int64)
    angle = np.float32(2.0 * math.pi / points) * (inner[:, None] * outer[None, :] % points).astype(np.float32)
    return np.stack([np.cos(angle), np.sin(angle)]).astype(np.float32)


def chirp_table(points, first_rows):
    position = np.arange(points, dtype=np.float32) / np.float32(points)
    rate = (np.arange(LEVELS, KCOH, dtype=np.float32) - np.float32((KCOH - 1) / 2.0)) * np.float32(chirp_step)
    phases = (np.float32(2.0 * math.pi) * rate)[:, None] * (position * position)[None, :]
    both = np.stack([np.cos(phases), np.sin(phases)], 1).astype(np.float32)
    return np.swapaxes(both.reshape(LEVELS, 2, first_rows, points // first_rows), 2, 3).copy()


def kernel(
    count, drift_hbm, series_hbm, antenna_hbm, chirp_hbm, twist_hbm, table_hbm, tracks_hbm, out_ref,
    drift, series_in, series, antenna, chirp, twist, table, tracks,
    strain, weights, weighted, spread, middle, spectra, padded,
    send, recv, gather, total_far, from_far, picks, staged,
    load_sem, chirp_sem, send_sem, far_sem, near_sem, gather_sem, total_sem, late_sem,
):
    _, second_rows, first_rows = strain.shape
    halves = first_rows // BLK
    blocks = second_rows * halves // count
    half_count = count // 2
    early_count = half_count + half_count // 2
    late_count = count - early_count
    half_rows = second_rows // 2
    points = first_rows * second_rows
    sky = lax.axis_index("sky")
    me = lax.axis_index("seg")
    side = lax.div(me, half_count)
    place_in = lax.rem(me, half_count)
    far = (1 - side) * half_count
    near = side * half_count
    mirror = far + place_in

    loads = [
        pltpu.make_async_copy(source, target, load_sem.at[index])
        for index, (source, target) in enumerate([
            (series_hbm, series_in), (antenna_hbm, antenna), (table_hbm, table), (twist_hbm, twist), (drift_hbm, drift),
            (tracks_hbm, tracks),
        ])
    ]
    chirp_load = lambda level: pltpu.make_async_copy(chirp_hbm.at[level], chirp.at[level], chirp_sem.at[level])
    loads[0].start()
    loads[1].start()
    chirp_load(0).start()
    for load in loads[2:]:
        load.start()

    barrier = pltpu.get_barrier_semaphore()

    is_early = me < early_count

    def signal(semaphore, first, wide):
        def one(step, carry):
            peer = lax.rem(me + step, count) if wide else first + step
            pl.semaphore_signal(semaphore, inc=1, device_id=(sky, peer), device_id_type=MESH)
            return carry

        return one

    @pl.when(is_early)
    def _():
        lax.fori_loop(1, count, signal(barrier, 0, True), 0)

    @pl.when(jnp.logical_not(is_early))
    def _():
        lax.fori_loop(0, me - early_count, signal(barrier, early_count, False), 0)
        lax.fori_loop(me - early_count + 1, late_count, signal(barrier, early_count, False), 0)

    for which in range(2):
        padded[which, :PAD] = jnp.zeros((PAD, BLK), jnp.float32)
        padded[which, PAD + second_rows * halves :] = jnp.zeros((PAD, BLK), jnp.float32)
    send[1] = jnp.zeros(send.shape[1:], jnp.float32)

    @pl.when(jnp.logical_not(is_early))
    def _():
        pl.semaphore_wait(barrier, count - 1)
        lax.fori_loop(0, early_count, signal(late_sem, 0, False), 0)

    pieces = second_rows // BLK

    def turned(source, target):
        for which in range(2):
            for piece in range(pieces):
                lines = pl.ds(2 * piece + which, first_rows, stride=2 * pieces)
                target[which, piece * BLK : (piece + 1) * BLK, :] = source[lines, :].T

    def demodulate(level):
        for first in range(0, second_rows, HALO):
            rows = slice(first, first + HALO)
            chirp_cos, chirp_sin = chirp[level, 0, rows, :], chirp[level, 1, rows, :]
            real, imag = strain[0, rows, :], strain[1, rows, :]
            real_cos, imag_sin = real * chirp_cos, imag * chirp_sin
            imag_cos, real_sin = imag * chirp_cos, real * chirp_sin
            demods = ((real_cos + imag_sin, imag_cos - real_sin), (real_cos - imag_sin, imag_cos + real_sin))
            for kind in range(2):
                weight = weights[kind, rows, :]
                for upper in range(2):
                    start = (2 * upper + kind) * second_rows + first
                    for part in range(2):
                        lanes = slice((1 - part) * first_rows, (2 - part) * first_rows)
                        weighted[start : start + HALO, lanes] = (weight * demods[upper][part]).astype(jnp.bfloat16)

    loads[0].wait()
    series[...] = series_in[...].astype(jnp.float32)
    turned(series, strain)
    loads[1].wait()
    turned(antenna, weights)
    chirp_load(0).wait()
    demodulate(0)

    def coefficients():
        sums = [0.0, 0.0, 0.0]
        for first in range(0, second_rows, HALO):
            rows = slice(first, first + HALO)
            weight_a, weight_b = weights[0, rows, :], weights[1, rows, :]
            sums = [held + value for held, value in zip(sums, (weight_a * weight_a, weight_b * weight_b, weight_a * weight_b))]
        aa, bb, ab = [jnp.sum(jnp.sum(held, axis=0, keepdims=True), axis=1, keepdims=True) / points for held in sums]
        aa, bb = aa + tiny_eps, bb + tiny_eps
        scale = 1.0 / (points * jnp.maximum(aa * bb - ab * ab, 0.1 * aa * bb))
        return bb * scale, aa * scale, 2.0 * ab * scale

    for load in loads[2:]:
        load.wait()
    for level in range(1, LEVELS):
        chirp_load(level).start()

    def second_stage(coefs, start, size):
        coef_a, coef_b, coef_ab = coefs
        start = pl.multiple_of(start, HALO)
        lines = jnp.concatenate([table[pl.ds(start, size), :], table[pl.ds(second_rows + start, size), :]], axis=0)
        for which in range(4):
            spectra[which, : 2 * size] = jnp.dot(lines, middle[which], preferred_element_type=jnp.float32)
        for which in range(2):
            for first in range(0, size, HALO):
                real_rows, imag_rows = slice(first, first + HALO), slice(size + first, size + first + HALO)
                a_real, a_imag = spectra[2 * which, real_rows, :], spectra[2 * which, imag_rows, :]
                b_real, b_imag = spectra[2 * which + 1, real_rows, :], spectra[2 * which + 1, imag_rows, :]
                value = (
                    coef_a * (a_real * a_real + a_imag * a_imag)
                    + coef_b * (b_real * b_real + b_imag * b_imag)
                    - coef_ab * (a_real * b_real + a_imag * b_imag)
                )
                for half in range(halves):
                    lines = pl.ds(PAD + halves * (start + first) + half, HALO, stride=halves)
                    padded[which, lines, :] = value[:, half * BLK : (half + 1) * BLK]

    def place(level, first_device):
        for which in (1, 0):
            shift = drift[0, (LEVELS + level) if which == 0 else (LEVELS - 1 - level)]
            channel = 2 * level + which
            if blocks % 8 == 0:
                devices = pl.ds(first_device, half_count)
                value = padded[which, pl.ds(PAD + first_device * blocks - shift, half_count * blocks), :]
                send[channel, devices] = value.reshape(half_count, blocks, BLK) - send[1, devices]
            else:
                def one(step, carry, which=which, channel=channel, shift=shift):
                    peer = first_device + step
                    value = padded[which, pl.ds(PAD + peer * blocks - shift, blocks), :]
                    send[channel, peer] = value - send[1, peer]
                    return carry

                lax.fori_loop(0, half_count, one, 0)

    def push(source, target, done, arrived, peer):
        pltpu.make_async_remote_copy(
            src_ref=source, dst_ref=target, send_sem=done, recv_sem=arrived, device_id=(sky, peer), device_id_type=MESH
        ).start()

    def ship_far(channel, first=0, last=half_count, ascending=False):
        def one(step, carry):
            peer = jnp.where(side == 0, half_count + step if ascending else count - 1 - step, step)
            push(send.at[channel, peer], recv.at[channel, :, me], send_sem.at[channel], far_sem.at[channel], peer)
            return carry

        lax.fori_loop(first, last, one, 0)

    def ship_near(channel):
        def one(step, carry):
            peer = near + lax.rem(place_in + step, half_count)
            push(send.at[channel, peer], recv.at[channel, :, me], send_sem.at[channel], near_sem.at[channel], peer)
            return carry

        lax.fori_loop(1, half_count, one, 0)
        pltpu.make_async_copy(send.at[channel, me], recv.at[channel, :, me], near_sem.at[channel]).start()

    def ship_base():
        def one(step, carry):
            other = lax.rem(place_in + step, half_count)
            push(send.at[1, far + other], gather.at[place_in], send_sem.at[1], gather_sem, near + other)
            return carry

        lax.fori_loop(1, half_count, one, 0)
        pltpu.make_async_copy(send.at[1, mirror], gather.at[place_in], gather_sem).start()

    def one_level(level, carry):
        spread[...] = jnp.dot(weighted[...], table[...], preferred_element_type=jnp.float32)
        coefs = coefficients()
        for which in range(4):
            for first in range(0, second_rows, HALO):
                rows = slice(first, first + HALO)
                lines = slice(which * second_rows + first, which * second_rows + first + HALO)
                twist_cos, twist_sin = twist[0, rows, :], twist[1, rows, :]
                one_imag, one_real = spread[lines, :first_rows], spread[lines, first_rows:]
                middle[which, first : first + HALO, :] = (one_real * twist_cos + one_imag * twist_sin).astype(jnp.bfloat16)
                middle[which, second_rows + first : second_rows + first + HALO, :] = (
                    one_imag * twist_cos - one_real * twist_sin
                ).astype(jnp.bfloat16)

        second_stage(coefs, (1 - side) * (half_rows - HALO), half_rows + HALO)
        place(level, far)

        @pl.when(jnp.logical_and(level == 0, is_early))
        def _():
            pl.semaphore_wait(barrier, early_count - 1)

        @pl.when(level == 0)
        def _():
            ship_far(0, 0, half_count // 2, ascending=True)

        @pl.when(jnp.logical_and(level == 0, side == 0))
        def _():
            pl.semaphore_wait(late_sem, late_count)

        @pl.when(level == 0)
        def _():
            ship_far(0, half_count // 2, half_count, ascending=True)

        @pl.when(jnp.logical_and(level == 0, jnp.logical_and(side == 1, is_early)))
        def _():
            pl.semaphore_wait(late_sem, late_count)

        second_stage(coefs, side * (half_rows + HALO), half_rows - HALO)
        place(level, near)

        @pl.when(level == 0)
        def _():
            ship_base()

        ship_near(2 * level + 1)
        ship_near(2 * level)

        @pl.when(level > 0)
        def _():
            ship_far(2 * level)
            ship_far(2 * level + 1)

        @pl.when(level == LEVELS - 2)
        def _():
            pltpu.make_async_copy(gather, gather, gather_sem).wait()
            total_far[...] = jnp.sum(gather[...], axis=0)
            push(total_far, from_far, total_sem.at[0], total_sem.at[1], mirror)

        @pl.when(level < LEVELS - 1)
        def _():
            chirp_load(level + 1).wait()
            demodulate(level + 1)

        return carry

    lax.fori_loop(0, LEVELS, one_level, 0)

    far_devices, near_devices = pl.ds(pl.multiple_of(far, half_count), half_count), pl.ds(pl.multiple_of(near, half_count), half_count)
    await_bytes = lambda part, arrived: pltpu.make_async_copy(part, part, arrived).wait()

    channels = [channel for channel in range(KCOH) if channel != 1]
    chosen = []
    for channel in channels:
        rate = LEVELS + channel // 2 if channel % 2 == 0 else LEVELS - 1 - channel // 2
        chosen += [jnp.where(tracks[...] == rate, 1.0, 0.0).astype(jnp.bfloat16)] * 2
    chosen = jnp.concatenate(chosen, axis=0)
    names = tracks.shape[1]
    same = lax.broadcasted_iota(jnp.int32, (names, names), 0) == lax.broadcasted_iota(jnp.int32, (names, names), 1)
    picks[...] = lax.dot_general(
        jnp.where(same, 1.0, 0.0).astype(jnp.bfloat16), chosen, (((1,), (1,)), ((), ())), preferred_element_type=jnp.float32
    ).astype(jnp.bfloat16)

    def stage(step, channel):
        await_bytes(recv.at[channel, :, near_devices], near_sem.at[channel])
        await_bytes(recv.at[channel, :, far_devices], far_sem.at[channel])
        line = step * 2 * count if isinstance(step, int) else pl.multiple_of(step * 2 * count, 2 * count)
        for block in range(blocks):
            value = recv[channel, block]
            high = value.astype(jnp.bfloat16)
            lanes = slice(block * BLK, (block + 1) * BLK)
            staged[pl.ds(line, count), lanes] = high
            staged[pl.ds(line + count, count), lanes] = (value - high.astype(jnp.float32)).astype(jnp.bfloat16)

    def stage_one(step, carry):
        stage(step, jnp.where(step == 0, 0, step + 1))
        return carry

    lax.fori_loop(0, KCOH - 2, stage_one, 0)
    await_bytes(recv.at[1, :, near_devices], near_sem.at[1])
    await_bytes(from_far, total_sem.at[1])
    base = jnp.sum(recv[1, :, near_devices], axis=1) + from_far[...]
    early = (KCOH - 2) * 2 * count
    width = halves * BLK
    parts = blocks // halves
    for part in range(parts):
        columns = slice(part * width, (part + 1) * width)
        line = jnp.concatenate([base[part * halves + half : part * halves + half + 1, :] for half in range(halves)], axis=1)
        out_ref[:, columns] = line + jnp.dot(
            picks[:, :early], staged[:early, columns], preferred_element_type=jnp.float32
        )
    stage(KCOH - 2, channels[-1])
    for part in range(parts):
        columns = slice(part * width, (part + 1) * width)
        out_ref[:, columns] += jnp.dot(picks[:, early:], staged[early:, columns], preferred_element_type=jnp.float32)

    for channel in range(KCOH):
        if channel == 1:
            part = send.at[1, pl.ds(0, 2 * (half_count - 1))]
        else:
            part = send.at[channel, pl.ds(0, count - 1)]
        await_bytes(part, send_sem.at[channel])
    await_bytes(total_far, total_sem.at[0])


def local(count, strain_series, antenna, drift, tracks):
    points = strain_series.shape[2]
    first_rows, second_rows = DFT_ROWS, points // DFT_ROWS
    segments = tracks.shape[1]
    blocks = points // count // BLK
    blocked = lambda array: array.reshape(2, points // BLK, BLK).transpose(1, 0, 2).reshape(2 * points // BLK, BLK)
    hbm = pl.BlockSpec(memory_space=pl.ANY)
    chirps = chirp_table(points, first_rows)
    block = (2 * points // BLK, BLK)
    summed = pl.pallas_call(
        functools.partial(kernel, count),
        out_shape=pltpu.VMEM((tracks.shape[0], points // count), jnp.float32),
        in_specs=[hbm] * 7,
        out_specs=pl.BlockSpec(memory_space=pltpu.VMEM),
        scratch_shapes=[
            pltpu.SMEM(drift.shape, jnp.int32),
            pltpu.VMEM(block, jnp.bfloat16),
            pltpu.VMEM(block, jnp.float32),
            pltpu.VMEM(block, jnp.float32),
            pltpu.VMEM(chirps.shape, jnp.float32),
            pltpu.VMEM((2, second_rows, first_rows), jnp.float32),
            pltpu.VMEM((2 * first_rows, 2 * first_rows), jnp.bfloat16),
            pltpu.VMEM((segments, tracks.shape[0]), jnp.int32),
            pltpu.VMEM((2, second_rows, first_rows), jnp.float32),
            pltpu.VMEM((2, second_rows, first_rows), jnp.float32),
            pltpu.VMEM((4 * second_rows, 2 * first_rows), jnp.bfloat16),
            pltpu.VMEM((4 * second_rows, 2 * first_rows), jnp.float32),
            pltpu.VMEM((4, 2 * second_rows, first_rows), jnp.bfloat16),
            pltpu.VMEM((4, second_rows + 2 * HALO, first_rows), jnp.float32),
            pltpu.VMEM((2, points // BLK + 2 * PAD, BLK), jnp.float32),
            pltpu.VMEM((KCOH, count, blocks, BLK), jnp.float32),
            pltpu.VMEM((KCOH, blocks, count, BLK), jnp.float32),
            pltpu.VMEM((count // 2, blocks, BLK), jnp.float32),
            pltpu.VMEM((blocks, BLK), jnp.float32),
            pltpu.VMEM((blocks, BLK), jnp.float32),
            pltpu.VMEM((tracks.shape[0], (KCOH - 1) * 2 * count), jnp.bfloat16),
            pltpu.VMEM(((KCOH - 1) * 2 * count, points // count), jnp.bfloat16),
            pltpu.SemaphoreType.DMA((6,)),
            pltpu.SemaphoreType.DMA((LEVELS,)),
            pltpu.SemaphoreType.DMA((KCOH,)),
            pltpu.SemaphoreType.DMA((KCOH,)),
            pltpu.SemaphoreType.DMA((KCOH,)),
            pltpu.SemaphoreType.DMA,
            pltpu.SemaphoreType.DMA((2,)),
            pltpu.SemaphoreType.REGULAR,
        ],
        compiler_params=pltpu.CompilerParams(
            collective_id=0, has_side_effects=True, vmem_limit_bytes=60 << 20
        ),
    )(
        drift,
        blocked(strain_series),
        blocked(antenna),
        jnp.asarray(chirps),
        jnp.asarray(twist_table(points, first_rows)),
        jnp.asarray(dft_table(first_rows)),
        tracks.T,
    )
    return summed / segments


def solution(mesh):
    return jax.shard_map(
        functools.partial(local, mesh.shape["seg"]),
        mesh=mesh,
        in_specs=(
            P(("sky", "seg"), None, None),
            P(("sky", "seg"), None, None),
            P(("sky", "seg"), None),
            P(),
        ),
        out_specs=P("sky", "seg"),
        check_vma=False,
    )
```

```python
import functools
import math

import jax
import jax.numpy as jnp
import numpy as np
from jax import lax
from jax.experimental import pallas as pl
from jax.experimental.pallas import tpu as pltpu
from jax.sharding import PartitionSpec as P

DFT_ROWS = 256
BLK = 128
KCOH = 6
LEVELS = KCOH // 2
PAD = 8
HALO = 16
MESH = pl.DeviceIdType.MESH

chirp_step = 3.0
tiny_eps = 1e-06


def dft_table(rows):
    index = np.arange(rows, dtype=np.int64)
    angle = np.float32(2.0 * math.pi / rows) * (index[:, None] * index[None, :] % rows).astype(np.float32)
    cos, sin = np.cos(angle), np.sin(angle)
    return np.block([[cos, sin], [-sin, cos]]).astype(jnp.bfloat16)


def twist_table(points, first_rows):
    second_rows = points // first_rows
    outer = np.arange(first_rows, dtype=np.int64)
    inner = np.arange(second_rows, dtype=np.int64)
    angle = np.float32(2.0 * math.pi / points) * (inner[:, None] * outer[None, :] % points).astype(np.float32)
    return np.stack([np.cos(angle), np.sin(angle)]).astype(np.float32)


def chirp_table(points, first_rows):
    position = np.arange(points, dtype=np.float32) / np.float32(points)
    rate = (np.arange(LEVELS, KCOH, dtype=np.float32) - np.float32((KCOH - 1) / 2.0)) * np.float32(chirp_step)
    phases = (np.float32(2.0 * math.pi) * rate)[:, None] * (position * position)[None, :]
    both = np.stack([np.cos(phases), np.sin(phases)], 1).astype(np.float32)
    return np.swapaxes(both.reshape(LEVELS, 2, first_rows, points // first_rows), 2, 3).copy()


def kernel(
    count, drift_hbm, series_hbm, antenna_hbm, chirp_hbm, twist_hbm, table_hbm, tracks_hbm, out_ref,
    drift, series_in, series, antenna, chirp, twist, table, tracks,
    strain, weights, weighted, spread, middle, spectra, padded,
    send, recv, gather, total_far, from_far, picks, staged,
    load_sem, chirp_sem, send_sem, far_sem, near_sem, gather_sem, total_sem, late_sem,
):
    _, second_rows, first_rows = strain.shape
    halves = first_rows // BLK
    blocks = second_rows * halves // count
    half_count = count // 2
    early_count = half_count + half_count // 2
    late_count = count - early_count
    half_rows = second_rows // 2
    points = first_rows * second_rows
    sky = lax.axis_index("sky")
    me = lax.axis_index("seg")
    side = lax.div(me, half_count)
    place_in = lax.rem(me, half_count)
    far = (1 - side) * half_count
    near = side * half_count
    mirror = far + place_in

    loads = [
        pltpu.make_async_copy(source, target, load_sem.at[index])
        for index, (source, target) in enumerate([
            (series_hbm, series_in), (antenna_hbm, antenna), (table_hbm, table), (twist_hbm, twist), (drift_hbm, drift),
            (tracks_hbm, tracks),
        ])
    ]
    chirp_load = lambda level: pltpu.make_async_copy(chirp_hbm.at[level], chirp.at[level], chirp_sem.at[level])
    loads[0].start()
    loads[1].start()
    chirp_load(0).start()
    for load in loads[2:]:
        load.start()

    barrier = pltpu.get_barrier_semaphore()

    is_early = me < early_count

    def signal(semaphore, first, wide):
        def one(step, carry):
            peer = lax.rem(me + step, count) if wide else first + step
            pl.semaphore_signal(semaphore, inc=1, device_id=(sky, peer), device_id_type=MESH)
            return carry

        return one

    @pl.when(is_early)
    def _():
        lax.fori_loop(1, count, signal(barrier, 0, True), 0)

    @pl.when(jnp.logical_not(is_early))
    def _():
        lax.fori_loop(0, me - early_count, signal(barrier, early_count, False), 0)
        lax.fori_loop(me - early_count + 1, late_count, signal(barrier, early_count, False), 0)

    for which in range(2):
        padded[which, :PAD] = jnp.zeros((PAD, BLK), jnp.float32)
        padded[which, PAD + second_rows * halves :] = jnp.zeros((PAD, BLK), jnp.float32)
    send[1] = jnp.zeros(send.shape[1:], jnp.float32)

    @pl.when(jnp.logical_not(is_early))
    def _():
        pl.semaphore_wait(barrier, count - 1)
        lax.fori_loop(0, early_count, signal(late_sem, 0, False), 0)

    pieces = second_rows // BLK

    def turned(source, target):
        for which in range(2):
            for piece in range(pieces):
                lines = pl.ds(2 * piece + which, first_rows, stride=2 * pieces)
                target[which, piece * BLK : (piece + 1) * BLK, :] = source[lines, :].T

    def demodulate(level):
        for first in range(0, second_rows, HALO):
            rows = slice(first, first + HALO)
            chirp_cos, chirp_sin = chirp[level, 0, rows, :], chirp[level, 1, rows, :]
            real, imag = strain[0, rows, :], strain[1, rows, :]
            real_cos, imag_sin = real * chirp_cos, imag * chirp_sin
            imag_cos, real_sin = imag * chirp_cos, real * chirp_sin
            demods = ((real_cos + imag_sin, imag_cos - real_sin), (real_cos - imag_sin, imag_cos + real_sin))
            for kind in range(2):
                weight = weights[kind, rows, :]
                for upper in range(2):
                    start = (2 * upper + kind) * second_rows + first
                    for part in range(2):
                        lanes = slice((1 - part) * first_rows, (2 - part) * first_rows)
                        weighted[start : start + HALO, lanes] = (weight * demods[upper][part]).astype(jnp.bfloat16)

    loads[0].wait()
    series[...] = series_in[...].astype(jnp.float32)
    turned(series, strain)
    loads[1].wait()
    turned(antenna, weights)
    chirp_load(0).wait()
    demodulate(0)

    def coefficients():
        sums = [0.0, 0.0, 0.0]
        for first in range(0, second_rows, HALO):
            rows = slice(first, first + HALO)
            weight_a, weight_b = weights[0, rows, :], weights[1, rows, :]
            sums = [held + value for held, value in zip(sums, (weight_a * weight_a, weight_b * weight_b, weight_a * weight_b))]
        aa, bb, ab = [jnp.sum(jnp.sum(held, axis=0, keepdims=True), axis=1, keepdims=True) / points for held in sums]
        aa, bb = aa + tiny_eps, bb + tiny_eps
        scale = 1.0 / (points * jnp.maximum(aa * bb - ab * ab, 0.1 * aa * bb))
        return bb * scale, aa * scale, 2.0 * ab * scale

    for load in loads[2:]:
        load.wait()
    for level in range(1, LEVELS):
        chirp_load(level).start()

    def second_stage(coefs, start, size):
        coef_a, coef_b, coef_ab = coefs
        start = pl.multiple_of(start, HALO)
        lines = jnp.concatenate([table[pl.ds(start, size), :], table[pl.ds(second_rows + start, size), :]], axis=0)
        for which in range(4):
            spectra[which, : 2 * size] = jnp.dot(lines, middle[which], preferred_element_type=jnp.float32)
        for which in range(2):
            for first in range(0, size, HALO):
                real_rows, imag_rows = slice(first, first + HALO), slice(size + first, size + first + HALO)
                a_real, a_imag = spectra[2 * which, real_rows, :], spectra[2 * which, imag_rows, :]
                b_real, b_imag = spectra[2 * which + 1, real_rows, :], spectra[2 * which + 1, imag_rows, :]
                value = (
                    coef_a * (a_real * a_real + a_imag * a_imag)
                    + coef_b * (b_real * b_real + b_imag * b_imag)
                    - coef_ab * (a_real * b_real + a_imag * b_imag)
                )
                for half in range(halves):
                    lines = pl.ds(PAD + halves * (start + first) + half, HALO, stride=halves)
                    padded[which, lines, :] = value[:, half * BLK : (half + 1) * BLK]

    def place(level, first_device):
        for which in (1, 0):
            shift = drift[0, (LEVELS + level) if which == 0 else (LEVELS - 1 - level)]
            channel = 2 * level + which
            if blocks % 8 == 0:
                devices = pl.ds(first_device, half_count)
                value = padded[which, pl.ds(PAD + first_device * blocks - shift, half_count * blocks), :]
                send[channel, devices] = value.reshape(half_count, blocks, BLK) - send[1, devices]
            else:
                def one(step, carry, which=which, channel=channel, shift=shift):
                    peer = first_device + step
                    value = padded[which, pl.ds(PAD + peer * blocks - shift, blocks), :]
                    send[channel, peer] = value - send[1, peer]
                    return carry

                lax.fori_loop(0, half_count, one, 0)

    def push(source, target, done, arrived, peer):
        pltpu.make_async_remote_copy(
            src_ref=source, dst_ref=target, send_sem=done, recv_sem=arrived, device_id=(sky, peer), device_id_type=MESH
        ).start()

    def ship_far(level, channels, first=0, last=half_count, ascending=False):
        def one(step, carry):
            peer = jnp.where(side == 0, half_count + step if ascending else count - 1 - step, step)
            push(send.at[channels, peer], recv.at[channels, :, me], send_sem.at[level], far_sem.at[level], peer)
            return carry

        lax.fori_loop(first, last, one, 0)

    def ship_near(level):
        channels = pl.ds(2 * level, 2)

        def one(step, carry):
            peer = near + lax.rem(place_in + step, half_count)
            push(send.at[channels, peer], recv.at[channels, :, me], send_sem.at[LEVELS + level], near_sem.at[level], peer)
            return carry

        lax.fori_loop(1, half_count, one, 0)
        pltpu.make_async_copy(send.at[channels, me], recv.at[channels, :, me], near_sem.at[level]).start()

    def ship_base():
        def one(step, carry):
            other = lax.rem(place_in + step, half_count)
            push(send.at[1, far + other], gather.at[place_in], send_sem.at[2 * LEVELS], gather_sem, near + other)
            return carry

        lax.fori_loop(1, half_count, one, 0)
        pltpu.make_async_copy(send.at[1, mirror], gather.at[place_in], gather_sem).start()

    def one_level(level, carry):
        spread[...] = jnp.dot(weighted[...], table[...], preferred_element_type=jnp.float32)
        coefs = coefficients()
        for which in range(4):
            for first in range(0, second_rows, HALO):
                rows = slice(first, first + HALO)
                lines = slice(which * second_rows + first, which * second_rows + first + HALO)
                twist_cos, twist_sin = twist[0, rows, :], twist[1, rows, :]
                one_imag, one_real = spread[lines, :first_rows], spread[lines, first_rows:]
                middle[which, first : first + HALO, :] = (one_real * twist_cos + one_imag * twist_sin).astype(jnp.bfloat16)
                middle[which, second_rows + first : second_rows + first + HALO, :] = (
                    one_imag * twist_cos - one_real * twist_sin
                ).astype(jnp.bfloat16)

        second_stage(coefs, (1 - side) * (half_rows - HALO), half_rows + HALO)
        place(level, far)

        @pl.when(jnp.logical_and(level == 0, is_early))
        def _():
            pl.semaphore_wait(barrier, early_count - 1)

        @pl.when(level == 0)
        def _():
            ship_far(0, pl.ds(0, 1), 0, half_count // 2, ascending=True)

        @pl.when(jnp.logical_and(level == 0, side == 0))
        def _():
            pl.semaphore_wait(late_sem, late_count)

        @pl.when(level == 0)
        def _():
            ship_far(0, pl.ds(0, 1), half_count // 2, half_count, ascending=True)

        @pl.when(jnp.logical_and(level == 0, jnp.logical_and(side == 1, is_early)))
        def _():
            pl.semaphore_wait(late_sem, late_count)

        second_stage(coefs, side * (half_rows + HALO), half_rows - HALO)
        place(level, near)

        @pl.when(level == 0)
        def _():
            ship_base()

        ship_near(level)

        @pl.when(level > 0)
        def _():
            ship_far(level, pl.ds(2 * level, 2))

        @pl.when(level == LEVELS - 2)
        def _():
            pltpu.make_async_copy(gather, gather, gather_sem).wait()
            total_far[...] = jnp.sum(gather[...], axis=0)
            push(total_far, from_far, total_sem.at[0], total_sem.at[1], mirror)

        @pl.when(level < LEVELS - 1)
        def _():
            chirp_load(level + 1).wait()
            demodulate(level + 1)

        return carry

    lax.fori_loop(0, LEVELS, one_level, 0)

    far_devices, near_devices = pl.ds(pl.multiple_of(far, half_count), half_count), pl.ds(pl.multiple_of(near, half_count), half_count)
    await_bytes = lambda part, arrived: pltpu.make_async_copy(part, part, arrived).wait()

    channels = [channel for channel in range(KCOH) if channel != 1]
    chosen = []
    for channel in channels:
        rate = LEVELS + channel // 2 if channel % 2 == 0 else LEVELS - 1 - channel // 2
        chosen += [jnp.where(tracks[...] == rate, 1.0, 0.0).astype(jnp.bfloat16)] * 2
    chosen = jnp.concatenate(chosen, axis=0)
    names = tracks.shape[1]
    same = lax.broadcasted_iota(jnp.int32, (names, names), 0) == lax.broadcasted_iota(jnp.int32, (names, names), 1)
    picks[...] = lax.dot_general(
        jnp.where(same, 1.0, 0.0).astype(jnp.bfloat16), chosen, (((1,), (1,)), ((), ())), preferred_element_type=jnp.float32
    ).astype(jnp.bfloat16)

    def arrive(level):
        pair = pl.ds(2 * level, 2)
        await_bytes(recv.at[pair, :, near_devices], near_sem.at[level])
        await_bytes(recv.at[pair if level else pl.ds(0, 1), :, far_devices], far_sem.at[level])

    def stage(step, channel):
        line = step * 2 * count
        for block in range(blocks):
            value = recv[channel, block]
            high = value.astype(jnp.bfloat16)
            lanes = slice(block * BLK, (block + 1) * BLK)
            staged[line : line + count, lanes] = high
            staged[line + count : line + 2 * count, lanes] = (value - high.astype(jnp.float32)).astype(jnp.bfloat16)

    for level in range(LEVELS - 1):
        arrive(level)
        for step, channel in enumerate(channels):
            if channel // 2 == level:
                stage(step, channel)
    await_bytes(from_far, total_sem.at[1])
    base = jnp.sum(recv[1, :, near_devices], axis=1) + from_far[...]
    early = (KCOH - 3) * 2 * count
    width = halves * BLK
    parts = blocks // halves
    for part in range(parts):
        columns = slice(part * width, (part + 1) * width)
        line = jnp.concatenate([base[part * halves + half : part * halves + half + 1, :] for half in range(halves)], axis=1)
        out_ref[:, columns] = line + jnp.dot(
            picks[:, :early], staged[:early, columns], preferred_element_type=jnp.float32
        )
    arrive(LEVELS - 1)
    for step in (KCOH - 3, KCOH - 2):
        stage(step, channels[step])
    for part in range(parts):
        columns = slice(part * width, (part + 1) * width)
        out_ref[:, columns] += jnp.dot(picks[:, early:], staged[early:, columns], preferred_element_type=jnp.float32)

    for level in range(LEVELS):
        pair = pl.ds(2 * level, 2)
        await_bytes(send.at[pair if level else pl.ds(0, 1), pl.ds(0, half_count)], send_sem.at[level])
        await_bytes(send.at[pair, pl.ds(0, half_count - 1)], send_sem.at[LEVELS + level])
    await_bytes(send.at[1, pl.ds(0, half_count - 1)], send_sem.at[2 * LEVELS])
    await_bytes(total_far, total_sem.at[0])


def local(count, strain_series, antenna, drift, tracks):
    points = strain_series.shape[2]
    first_rows, second_rows = DFT_ROWS, points // DFT_ROWS
    segments = tracks.shape[1]
    blocks = points // count // BLK
    blocked = lambda array: array.reshape(2, points // BLK, BLK).transpose(1, 0, 2).reshape(2 * points // BLK, BLK)
    hbm = pl.BlockSpec(memory_space=pl.ANY)
    chirps = chirp_table(points, first_rows)
    block = (2 * points // BLK, BLK)
    summed = pl.pallas_call(
        functools.partial(kernel, count),
        out_shape=pltpu.VMEM((tracks.shape[0], points // count), jnp.float32),
        in_specs=[hbm] * 7,
        out_specs=pl.BlockSpec(memory_space=pltpu.VMEM),
        scratch_shapes=[
            pltpu.SMEM(drift.shape, jnp.int32),
            pltpu.VMEM(block, jnp.bfloat16),
            pltpu.VMEM(block, jnp.float32),
            pltpu.VMEM(block, jnp.float32),
            pltpu.VMEM(chirps.shape, jnp.float32),
            pltpu.VMEM((2, second_rows, first_rows), jnp.float32),
            pltpu.VMEM((2 * first_rows, 2 * first_rows), jnp.bfloat16),
            pltpu.VMEM((segments, tracks.shape[0]), jnp.int32),
            pltpu.VMEM((2, second_rows, first_rows), jnp.float32),
            pltpu.VMEM((2, second_rows, first_rows), jnp.float32),
            pltpu.VMEM((4 * second_rows, 2 * first_rows), jnp.bfloat16),
            pltpu.VMEM((4 * second_rows, 2 * first_rows), jnp.float32),
            pltpu.VMEM((4, 2 * second_rows, first_rows), jnp.bfloat16),
            pltpu.VMEM((4, second_rows + 2 * HALO, first_rows), jnp.float32),
            pltpu.VMEM((2, points // BLK + 2 * PAD, BLK), jnp.float32),
            pltpu.VMEM((KCOH, count, blocks, BLK), jnp.float32),
            pltpu.VMEM((KCOH, blocks, count, BLK), jnp.float32),
            pltpu.VMEM((count // 2, blocks, BLK), jnp.float32),
            pltpu.VMEM((blocks, BLK), jnp.float32),
            pltpu.VMEM((blocks, BLK), jnp.float32),
            pltpu.VMEM((tracks.shape[0], (KCOH - 1) * 2 * count), jnp.bfloat16),
            pltpu.VMEM(((KCOH - 1) * 2 * count, points // count), jnp.bfloat16),
            pltpu.SemaphoreType.DMA((6,)),
            pltpu.SemaphoreType.DMA((LEVELS,)),
            pltpu.SemaphoreType.DMA((2 * LEVELS + 1,)),
            pltpu.SemaphoreType.DMA((LEVELS,)),
            pltpu.SemaphoreType.DMA((LEVELS,)),
            pltpu.SemaphoreType.DMA,
            pltpu.SemaphoreType.DMA((2,)),
            pltpu.SemaphoreType.REGULAR,
        ],
        compiler_params=pltpu.CompilerParams(
            collective_id=0, has_side_effects=True, vmem_limit_bytes=60 << 20
        ),
    )(
        drift,
        blocked(strain_series),
        blocked(antenna),
        jnp.asarray(chirps),
        jnp.asarray(twist_table(points, first_rows)),
        jnp.asarray(dft_table(first_rows)),
        tracks.T,
    )
    return summed / segments


def solution(mesh):
    return jax.shard_map(
        functools.partial(local, mesh.shape["seg"]),
        mesh=mesh,
        in_specs=(
            P(("sky", "seg"), None, None),
            P(("sky", "seg"), None, None),
            P(("sky", "seg"), None),
            P(),
        ),
        out_specs=P("sky", "seg"),
        check_vma=False,
    )
```

```python
import functools
import math

import jax
import jax.numpy as jnp
import numpy as np
from jax import lax
from jax.experimental import pallas as pl
from jax.experimental.pallas import tpu as pltpu
from jax.sharding import PartitionSpec as P

DFT_ROWS = 256
BLK = 128
KCOH = 6
LEVELS = KCOH // 2
PAD = 8
HALO = 16
MESH = pl.DeviceIdType.MESH

chirp_step = 3.0
tiny_eps = 1e-06


def dft_table(rows):
    index = np.arange(rows, dtype=np.int64)
    angle = np.float32(2.0 * math.pi / rows) * (index[:, None] * index[None, :] % rows).astype(np.float32)
    cos, sin = np.cos(angle), np.sin(angle)
    return np.block([[cos, sin], [-sin, cos]]).astype(jnp.bfloat16)


def twist_table(points, first_rows):
    second_rows = points // first_rows
    outer = np.arange(first_rows, dtype=np.int64)
    inner = np.arange(second_rows, dtype=np.int64)
    angle = np.float32(2.0 * math.pi / points) * (inner[:, None] * outer[None, :] % points).astype(np.float32)
    return np.stack([np.cos(angle), np.sin(angle)]).astype(np.float32)


def chirp_table(points, first_rows):
    position = np.arange(points, dtype=np.float32) / np.float32(points)
    rate = (np.arange(LEVELS, KCOH, dtype=np.float32) - np.float32((KCOH - 1) / 2.0)) * np.float32(chirp_step)
    phases = (np.float32(2.0 * math.pi) * rate)[:, None] * (position * position)[None, :]
    both = np.stack([np.cos(phases), np.sin(phases)], 1).astype(np.float32)
    return np.swapaxes(both.reshape(LEVELS, 2, first_rows, points // first_rows), 2, 3).copy()


def kernel(
    count, drift_hbm, series_hbm, antenna_hbm, chirp_hbm, twist_hbm, table_hbm, tracks_hbm, out_ref,
    drift, series_in, series, antenna, chirp, twist, table, tracks,
    strain, weights, weighted, spread, middle, spectra, padded,
    send, recv, gather, total_far, from_far, picks, staged,
    load_sem, chirp_sem, send_sem, far_sem, near_sem, gather_sem, total_sem, late_sem,
):
    _, second_rows, first_rows = strain.shape
    halves = first_rows // BLK
    blocks = second_rows * halves // count
    half_count = count // 2
    early_count = half_count + half_count // 2
    late_count = count - early_count
    half_rows = second_rows // 2
    points = first_rows * second_rows
    sky = lax.axis_index("sky")
    me = lax.axis_index("seg")
    side = lax.div(me, half_count)
    place_in = lax.rem(me, half_count)
    far = (1 - side) * half_count
    near = side * half_count
    mirror = far + place_in

    loads = [
        pltpu.make_async_copy(source, target, load_sem.at[index])
        for index, (source, target) in enumerate([
            (series_hbm, series_in), (antenna_hbm, antenna), (table_hbm, table), (twist_hbm, twist), (drift_hbm, drift),
            (tracks_hbm, tracks),
        ])
    ]
    chirp_load = lambda level: pltpu.make_async_copy(chirp_hbm.at[level], chirp.at[level], chirp_sem.at[level])
    loads[0].start()
    loads[1].start()
    chirp_load(0).start()
    for load in loads[2:]:
        load.start()

    barrier = pltpu.get_barrier_semaphore()

    is_early = me < early_count

    def signal(semaphore, first, wide):
        def one(step, carry):
            peer = lax.rem(me + step, count) if wide else first + step
            pl.semaphore_signal(semaphore, inc=1, device_id=(sky, peer), device_id_type=MESH)
            return carry

        return one

    @pl.when(is_early)
    def _():
        lax.fori_loop(1, count, signal(barrier, 0, True), 0)

    @pl.when(jnp.logical_not(is_early))
    def _():
        lax.fori_loop(0, me - early_count, signal(barrier, early_count, False), 0)
        lax.fori_loop(me - early_count + 1, late_count, signal(barrier, early_count, False), 0)

    for which in range(2):
        padded[which, :PAD] = jnp.zeros((PAD, BLK), jnp.float32)
        padded[which, PAD + second_rows * halves :] = jnp.zeros((PAD, BLK), jnp.float32)
    send[1] = jnp.zeros(send.shape[1:], jnp.float32)

    @pl.when(jnp.logical_not(is_early))
    def _():
        pl.semaphore_wait(barrier, count - 1)
        lax.fori_loop(0, early_count, signal(late_sem, 0, False), 0)

    pieces = second_rows // BLK

    def turned(source, target):
        for which in range(2):
            for piece in range(pieces):
                lines = pl.ds(2 * piece + which, first_rows, stride=2 * pieces)
                target[which, piece * BLK : (piece + 1) * BLK, :] = source[lines, :].T

    def demodulate(level):
        for first in range(0, second_rows, HALO):
            rows = slice(first, first + HALO)
            chirp_cos, chirp_sin = chirp[level, 0, rows, :], chirp[level, 1, rows, :]
            real, imag = strain[0, rows, :], strain[1, rows, :]
            real_cos, imag_sin = real * chirp_cos, imag * chirp_sin
            imag_cos, real_sin = imag * chirp_cos, real * chirp_sin
            demods = ((real_cos + imag_sin, imag_cos - real_sin), (real_cos - imag_sin, imag_cos + real_sin))
            for kind in range(2):
                weight = weights[kind, rows, :]
                for upper in range(2):
                    start = (2 * upper + kind) * second_rows + first
                    for part in range(2):
                        lanes = slice((1 - part) * first_rows, (2 - part) * first_rows)
                        weighted[start : start + HALO, lanes] = (weight * demods[upper][part]).astype(jnp.bfloat16)

    loads[0].wait()
    series[...] = series_in[...].astype(jnp.float32)
    turned(series, strain)
    loads[1].wait()
    turned(antenna, weights)
    chirp_load(0).wait()
    demodulate(0)

    def coefficients():
        sums = [0.0, 0.0, 0.0]
        for first in range(0, second_rows, HALO):
            rows = slice(first, first + HALO)
            weight_a, weight_b = weights[0, rows, :], weights[1, rows, :]
            sums = [held + value for held, value in zip(sums, (weight_a * weight_a, weight_b * weight_b, weight_a * weight_b))]
        aa, bb, ab = [jnp.sum(jnp.sum(held, axis=0, keepdims=True), axis=1, keepdims=True) / points for held in sums]
        aa, bb = aa + tiny_eps, bb + tiny_eps
        scale = 1.0 / (points * jnp.maximum(aa * bb - ab * ab, 0.1 * aa * bb))
        return bb * scale, aa * scale, 2.0 * ab * scale

    for load in loads[2:]:
        load.wait()
    for level in range(1, LEVELS):
        chirp_load(level).start()

    def second_stage(coefs, start, size):
        coef_a, coef_b, coef_ab = coefs
        start = pl.multiple_of(start, HALO)
        lines = jnp.concatenate([table[pl.ds(start, size), :], table[pl.ds(second_rows + start, size), :]], axis=0)
        for which in range(4):
            spectra[which, : 2 * size] = jnp.dot(lines, middle[which], preferred_element_type=jnp.float32)
        for which in range(2):
            for first in range(0, size, HALO):
                real_rows, imag_rows = slice(first, first + HALO), slice(size + first, size + first + HALO)
                a_real, a_imag = spectra[2 * which, real_rows, :], spectra[2 * which, imag_rows, :]
                b_real, b_imag = spectra[2 * which + 1, real_rows, :], spectra[2 * which + 1, imag_rows, :]
                value = (
                    coef_a * (a_real * a_real + a_imag * a_imag)
                    + coef_b * (b_real * b_real + b_imag * b_imag)
                    - coef_ab * (a_real * b_real + a_imag * b_imag)
                )
                for half in range(halves):
                    lines = pl.ds(PAD + halves * (start + first) + half, HALO, stride=halves)
                    padded[which, lines, :] = value[:, half * BLK : (half + 1) * BLK]

    def place(level, first_device, devices_here):
        for which in (1, 0):
            shift = drift[0, (LEVELS + level) if which == 0 else (LEVELS - 1 - level)]
            channel = 2 * level + which
            if blocks % 8 == 0:
                devices = pl.ds(first_device, devices_here)
                value = padded[which, pl.ds(PAD + first_device * blocks - shift, devices_here * blocks), :]
                send[channel, devices] = value.reshape(devices_here, blocks, BLK) - send[1, devices]
            else:
                def one(step, carry, which=which, channel=channel, shift=shift):
                    peer = first_device + step
                    value = padded[which, pl.ds(PAD + peer * blocks - shift, blocks), :]
                    send[channel, peer] = value - send[1, peer]
                    return carry

                lax.fori_loop(0, devices_here, one, 0)

    def push(source, target, done, arrived, peer):
        pltpu.make_async_remote_copy(
            src_ref=source, dst_ref=target, send_sem=done, recv_sem=arrived, device_id=(sky, peer), device_id_type=MESH
        ).start()

    def ship_far(level, channels, first=0, last=half_count, ascending=False):
        def one(step, carry):
            peer = jnp.where(side == 0, half_count + (step if ascending else lax.rem(step + half_count // 2, half_count)), step)
            push(send.at[channels, peer], recv.at[channels, :, me], send_sem.at[level], far_sem.at[level], peer)
            return carry

        lax.fori_loop(first, last, one, 0)

    def ship_near(level):
        channels = pl.ds(2 * level, 2)

        def one(step, carry):
            peer = near + lax.rem(place_in + step, half_count)
            push(send.at[channels, peer], recv.at[channels, :, me], send_sem.at[LEVELS + level], near_sem.at[level], peer)
            return carry

        lax.fori_loop(1, half_count, one, 0)
        pltpu.make_async_copy(send.at[channels, me], recv.at[channels, :, me], near_sem.at[level]).start()

    def ship_base():
        def one(step, carry):
            other = lax.rem(place_in + step, half_count)
            push(send.at[1, far + other], gather.at[place_in], send_sem.at[2 * LEVELS], gather_sem, near + other)
            return carry

        lax.fori_loop(1, half_count, one, 0)
        pltpu.make_async_copy(send.at[1, mirror], gather.at[place_in], gather_sem).start()

    def one_level(level, carry):
        spread[...] = jnp.dot(weighted[...], table[...], preferred_element_type=jnp.float32)
        coefs = coefficients()
        for which in range(4):
            for first in range(0, second_rows, HALO):
                rows = slice(first, first + HALO)
                lines = slice(which * second_rows + first, which * second_rows + first + HALO)
                twist_cos, twist_sin = twist[0, rows, :], twist[1, rows, :]
                one_imag, one_real = spread[lines, :first_rows], spread[lines, first_rows:]
                middle[which, first : first + HALO, :] = (one_real * twist_cos + one_imag * twist_sin).astype(jnp.bfloat16)
                middle[which, second_rows + first : second_rows + first + HALO, :] = (
                    one_imag * twist_cos - one_real * twist_sin
                ).astype(jnp.bfloat16)

        first_row = (1 - side) * (half_rows - HALO)
        first_size = half_rows // 2 + 2 * HALO
        second_stage(coefs, first_row, first_size)
        place(level, far, half_count // 2)

        @pl.when(jnp.logical_and(level == 0, is_early))
        def _():
            pl.semaphore_wait(barrier, early_count - 1)

        @pl.when(level == 0)
        def _():
            ship_far(0, pl.ds(0, 1), 0, half_count // 2, ascending=True)

        second_stage(coefs, first_row + first_size, half_rows + HALO - first_size)
        place(level, far + half_count // 2, half_count // 2)

        @pl.when(jnp.logical_and(level == 0, side == 0))
        def _():
            pl.semaphore_wait(late_sem, late_count)

        @pl.when(level == 0)
        def _():
            ship_far(0, pl.ds(0, 1), half_count // 2, half_count, ascending=True)

        @pl.when(jnp.logical_and(level == 0, jnp.logical_and(side == 1, is_early)))
        def _():
            pl.semaphore_wait(late_sem, late_count)

        second_stage(coefs, side * (half_rows + HALO), half_rows - HALO)
        place(level, near, half_count)

        @pl.when(level == 0)
        def _():
            ship_base()

        ship_near(level)

        @pl.when(level > 0)
        def _():
            ship_far(level, pl.ds(2 * level, 2))

        @pl.when(level == LEVELS - 2)
        def _():
            pltpu.make_async_copy(gather, gather, gather_sem).wait()
            total_far[...] = jnp.sum(gather[...], axis=0)
            push(total_far, from_far, total_sem.at[0], total_sem.at[1], mirror)

        @pl.when(level < LEVELS - 1)
        def _():
            chirp_load(level + 1).wait()
            demodulate(level + 1)

        return carry

    lax.fori_loop(0, LEVELS, one_level, 0)

    far_devices, near_devices = pl.ds(pl.multiple_of(far, half_count), half_count), pl.ds(pl.multiple_of(near, half_count), half_count)
    await_bytes = lambda part, arrived: pltpu.make_async_copy(part, part, arrived).wait()

    channels = [channel for channel in range(KCOH) if channel != 1]
    chosen = []
    for channel in channels:
        rate = LEVELS + channel // 2 if channel % 2 == 0 else LEVELS - 1 - channel // 2
        chosen += [jnp.where(tracks[...] == rate, 1.0, 0.0).astype(jnp.bfloat16)] * 2
    chosen = jnp.concatenate(chosen, axis=0)
    names = tracks.shape[1]
    same = lax.broadcasted_iota(jnp.int32, (names, names), 0) == lax.broadcasted_iota(jnp.int32, (names, names), 1)
    picks[...] = lax.dot_general(
        jnp.where(same, 1.0, 0.0).astype(jnp.bfloat16), chosen, (((1,), (1,)), ((), ())), preferred_element_type=jnp.float32
    ).astype(jnp.bfloat16)

    def arrive(level):
        pair = pl.ds(2 * level, 2)
        await_bytes(recv.at[pair, :, near_devices], near_sem.at[level])
        await_bytes(recv.at[pair if level else pl.ds(0, 1), :, far_devices], far_sem.at[level])

    def stage(step, channel):
        line = step * 2 * count
        for block in range(blocks):
            value = recv[channel, block]
            high = value.astype(jnp.bfloat16)
            lanes = slice(block * BLK, (block + 1) * BLK)
            staged[line : line + count, lanes] = high
            staged[line + count : line + 2 * count, lanes] = (value - high.astype(jnp.float32)).astype(jnp.bfloat16)

    for level in range(LEVELS - 1):
        arrive(level)
        for step, channel in enumerate(channels):
            if channel // 2 == level:
                stage(step, channel)
    await_bytes(from_far, total_sem.at[1])
    base = jnp.sum(recv[1, :, near_devices], axis=1) + from_far[...]
    early = (KCOH - 3) * 2 * count
    width = halves * BLK
    parts = blocks // halves
    for part in range(parts):
        columns = slice(part * width, (part + 1) * width)
        line = jnp.concatenate([base[part * halves + half : part * halves + half + 1, :] for half in range(halves)], axis=1)
        out_ref[:, columns] = line + jnp.dot(
            picks[:, :early], staged[:early, columns], preferred_element_type=jnp.float32
        )
    arrive(LEVELS - 1)
    for part in range(parts):
        columns = slice(part * width, (part + 1) * width)
        lines = []
        for channel in channels[-2:]:
            value = jnp.concatenate([recv[channel, part * halves + half] for half in range(halves)], axis=1)
            high = value.astype(jnp.bfloat16)
            lines += [high, (value - high.astype(jnp.float32)).astype(jnp.bfloat16)]
        out_ref[:, columns] += jnp.dot(
            picks[:, early:], jnp.concatenate(lines, axis=0), preferred_element_type=jnp.float32
        )

    for level in range(LEVELS):
        pair = pl.ds(2 * level, 2)
        await_bytes(send.at[pair if level else pl.ds(0, 1), pl.ds(0, half_count)], send_sem.at[level])
        await_bytes(send.at[pair, pl.ds(0, half_count - 1)], send_sem.at[LEVELS + level])
    await_bytes(send.at[1, pl.ds(0, half_count - 1)], send_sem.at[2 * LEVELS])
    await_bytes(total_far, total_sem.at[0])


def local(count, strain_series, antenna, drift, tracks):
    points = strain_series.shape[2]
    first_rows, second_rows = DFT_ROWS, points // DFT_ROWS
    segments = tracks.shape[1]
    blocks = points // count // BLK
    blocked = lambda array: array.reshape(2, points // BLK, BLK).transpose(1, 0, 2).reshape(2 * points // BLK, BLK)
    hbm = pl.BlockSpec(memory_space=pl.ANY)
    chirps = chirp_table(points, first_rows)
    block = (2 * points // BLK, BLK)
    summed = pl.pallas_call(
        functools.partial(kernel, count),
        out_shape=pltpu.VMEM((tracks.shape[0], points // count), jnp.float32),
        in_specs=[hbm] * 7,
        out_specs=pl.BlockSpec(memory_space=pltpu.VMEM),
        scratch_shapes=[
            pltpu.SMEM(drift.shape, jnp.int32),
            pltpu.VMEM(block, jnp.bfloat16),
            pltpu.VMEM(block, jnp.float32),
            pltpu.VMEM(block, jnp.float32),
            pltpu.VMEM(chirps.shape, jnp.float32),
            pltpu.VMEM((2, second_rows, first_rows), jnp.float32),
            pltpu.VMEM((2 * first_rows, 2 * first_rows), jnp.bfloat16),
            pltpu.VMEM((segments, tracks.shape[0]), jnp.int32),
            pltpu.VMEM((2, second_rows, first_rows), jnp.float32),
            pltpu.VMEM((2, second_rows, first_rows), jnp.float32),
            pltpu.VMEM((4 * second_rows, 2 * first_rows), jnp.bfloat16),
            pltpu.VMEM((4 * second_rows, 2 * first_rows), jnp.float32),
            pltpu.VMEM((4, 2 * second_rows, first_rows), jnp.bfloat16),
            pltpu.VMEM((4, second_rows + 2 * HALO, first_rows), jnp.float32),
            pltpu.VMEM((2, points // BLK + 2 * PAD, BLK), jnp.float32),
            pltpu.VMEM((KCOH, count, blocks, BLK), jnp.float32),
            pltpu.VMEM((KCOH, blocks, count, BLK), jnp.float32),
            pltpu.VMEM((count // 2, blocks, BLK), jnp.float32),
            pltpu.VMEM((blocks, BLK), jnp.float32),
            pltpu.VMEM((blocks, BLK), jnp.float32),
            pltpu.VMEM((tracks.shape[0], (KCOH - 1) * 2 * count), jnp.bfloat16),
            pltpu.VMEM(((KCOH - 3) * 2 * count, points // count), jnp.bfloat16),
            pltpu.SemaphoreType.DMA((6,)),
            pltpu.SemaphoreType.DMA((LEVELS,)),
            pltpu.SemaphoreType.DMA((2 * LEVELS + 1,)),
            pltpu.SemaphoreType.DMA((LEVELS,)),
            pltpu.SemaphoreType.DMA((LEVELS,)),
            pltpu.SemaphoreType.DMA,
            pltpu.SemaphoreType.DMA((2,)),
            pltpu.SemaphoreType.REGULAR,
        ],
        compiler_params=pltpu.CompilerParams(
            collective_id=0, has_side_effects=True, vmem_limit_bytes=60 << 20
        ),
    )(
        drift,
        blocked(strain_series),
        blocked(antenna),
        jnp.asarray(chirps),
        jnp.asarray(twist_table(points, first_rows)),
        jnp.asarray(dft_table(first_rows)),
        tracks.T,
    )
    return summed / segments


def solution(mesh):
    return jax.shard_map(
        functools.partial(local, mesh.shape["seg"]),
        mesh=mesh,
        in_specs=(
            P(("sky", "seg"), None, None),
            P(("sky", "seg"), None, None),
            P(("sky", "seg"), None),
            P(),
        ),
        out_specs=P("sky", "seg"),
        check_vma=False,
    )
```

```python
import functools
import math

import jax
import jax.numpy as jnp
import numpy as np
from jax import lax
from jax.experimental import pallas as pl
from jax.experimental.pallas import tpu as pltpu
from jax.sharding import PartitionSpec as P

DFT_ROWS = 256
BLK = 128
KCOH = 6
LEVELS = KCOH // 2
PAD = 8
HALO = 16
SUB = 8
MESH = pl.DeviceIdType.MESH

chirp_step = 3.0
tiny_eps = 1e-06


def dft_table(rows):
    index = np.arange(rows, dtype=np.int64)
    angle = np.float32(2.0 * math.pi / rows) * (index[:, None] * index[None, :] % rows).astype(np.float32)
    cos, sin = np.cos(angle), np.sin(angle)
    return np.block([[cos, sin], [-sin, cos]]).astype(jnp.bfloat16)


def twist_factors(points, first_rows):
    second_rows = points // first_rows
    inner = np.concatenate([SUB * np.arange(second_rows // SUB, dtype=np.int64), np.arange(SUB, dtype=np.int64)])
    outer = np.arange(first_rows, dtype=np.int64)
    angle = (2.0 * math.pi / points) * (inner[:, None] * outer[None, :] % points).astype(np.float64)
    return np.stack([np.cos(angle), np.sin(angle)]).astype(np.float32)


def chirp_table(points, first_rows):
    position = np.arange(points, dtype=np.float32) / np.float32(points)
    rate = (np.arange(LEVELS, KCOH, dtype=np.float32) - np.float32((KCOH - 1) / 2.0)) * np.float32(chirp_step)
    phases = (np.float32(2.0 * math.pi) * rate)[:, None] * (position * position)[None, :]
    both = np.stack([np.cos(phases), np.sin(phases)], 1).astype(np.float32)
    return np.swapaxes(both.reshape(LEVELS, 2, first_rows, points // first_rows), 2, 3).copy()


def kernel(
    count, drift_hbm, series_hbm, antenna_hbm, chirp_hbm, factors_hbm, table_hbm, tracks_hbm, out_ref,
    drift, series_in, series, antenna, chirp, factors, twist, table, tracks,
    strain, weights, weighted, spread, middle, spectra, padded,
    send, recv, gather, total_far, from_far, picks, last_picks, staged,
    load_sem, chirp_sem, send_sem, far_sem, near_sem, gather_sem, total_sem, late_sem,
):
    _, second_rows, first_rows = strain.shape
    halves = first_rows // BLK
    blocks = second_rows * halves // count
    half_count = count // 2
    early_count = half_count + half_count // 2
    late_count = count - early_count
    half_rows = second_rows // 2
    points = first_rows * second_rows
    sky = lax.axis_index("sky")
    me = lax.axis_index("seg")
    side = lax.div(me, half_count)
    place_in = lax.rem(me, half_count)
    far = (1 - side) * half_count
    near = side * half_count
    mirror = far + place_in

    loads = [
        pltpu.make_async_copy(source, target, load_sem.at[index])
        for index, (source, target) in enumerate([
            (series_hbm, series_in), (antenna_hbm, antenna), (table_hbm, table), (factors_hbm, factors), (drift_hbm, drift),
            (tracks_hbm, tracks),
        ])
    ]
    chirp_load = lambda level: pltpu.make_async_copy(chirp_hbm.at[level], chirp.at[level], chirp_sem.at[level])
    loads[0].start()
    loads[3].start()
    loads[1].start()
    chirp_load(0).start()
    for index in (4, 2, 5):
        loads[index].start()

    barrier = pltpu.get_barrier_semaphore()

    is_early = me < early_count

    def signal(semaphore, first, wide):
        def one(step, carry):
            peer = lax.rem(me + step, count) if wide else first + step
            pl.semaphore_signal(semaphore, inc=1, device_id=(sky, peer), device_id_type=MESH)
            return carry

        return one

    @pl.when(is_early)
    def _():
        lax.fori_loop(1, count, signal(barrier, 0, True), 0)

    @pl.when(jnp.logical_not(is_early))
    def _():
        lax.fori_loop(0, me - early_count, signal(barrier, early_count, False), 0)
        lax.fori_loop(me - early_count + 1, late_count, signal(barrier, early_count, False), 0)

    for which in range(2):
        padded[which, :PAD] = jnp.zeros((PAD, BLK), jnp.float32)
        padded[which, PAD + second_rows * halves :] = jnp.zeros((PAD, BLK), jnp.float32)
    send[1] = jnp.zeros(send.shape[1:], jnp.float32)

    @pl.when(jnp.logical_not(is_early))
    def _():
        pl.semaphore_wait(barrier, count - 1)
        lax.fori_loop(0, early_count, signal(late_sem, 0, False), 0)

    pieces = second_rows // BLK

    def turned(source, target):
        for which in range(2):
            for piece in range(pieces):
                lines = pl.ds(2 * piece + which, first_rows, stride=2 * pieces)
                target[which, piece * BLK : (piece + 1) * BLK, :] = source[lines, :].T

    def demodulate(level):
        for first in range(0, second_rows, HALO):
            rows = slice(first, first + HALO)
            chirp_cos, chirp_sin = chirp[level, 0, rows, :], chirp[level, 1, rows, :]
            real, imag = strain[0, rows, :], strain[1, rows, :]
            real_cos, imag_sin = real * chirp_cos, imag * chirp_sin
            imag_cos, real_sin = imag * chirp_cos, real * chirp_sin
            demods = ((real_cos + imag_sin, imag_cos - real_sin), (real_cos - imag_sin, imag_cos + real_sin))
            for kind in range(2):
                weight = weights[kind, rows, :]
                for upper in range(2):
                    start = (2 * upper + kind) * second_rows + first
                    for part in range(2):
                        lanes = slice((1 - part) * first_rows, (2 - part) * first_rows)
                        weighted[start : start + HALO, lanes] = (weight * demods[upper][part]).astype(jnp.bfloat16)

    loads[0].wait()
    series[...] = series_in[...].astype(jnp.float32)
    loads[3].wait()
    turned(series, strain)
    steps = second_rows // SUB
    step_cos, step_sin = factors[0, steps:, :], factors[1, steps:, :]
    for step in range(steps):
        base_cos, base_sin = factors[0, step : step + 1, :], factors[1, step : step + 1, :]
        twist[0, step * SUB : (step + 1) * SUB, :] = base_cos * step_cos - base_sin * step_sin
        twist[1, step * SUB : (step + 1) * SUB, :] = base_sin * step_cos + base_cos * step_sin
    loads[1].wait()
    turned(antenna, weights)
    chirp_load(0).wait()
    demodulate(0)

    def coefficients():
        sums = [0.0, 0.0, 0.0]
        for first in range(0, second_rows, HALO):
            rows = slice(first, first + HALO)
            weight_a, weight_b = weights[0, rows, :], weights[1, rows, :]
            sums = [held + value for held, value in zip(sums, (weight_a * weight_a, weight_b * weight_b, weight_a * weight_b))]
        aa, bb, ab = [jnp.sum(jnp.sum(held, axis=0, keepdims=True), axis=1, keepdims=True) / points for held in sums]
        aa, bb = aa + tiny_eps, bb + tiny_eps
        scale = 1.0 / (points * jnp.maximum(aa * bb - ab * ab, 0.1 * aa * bb))
        return bb * scale, aa * scale, 2.0 * ab * scale

    loads[4].wait()
    loads[2].wait()
    for level in range(1, LEVELS):
        chirp_load(level).start()

    def second_stage(coefs, start, size):
        coef_a, coef_b, coef_ab = coefs
        start = pl.multiple_of(start, HALO)
        lines = jnp.concatenate([table[pl.ds(start, size), :], table[pl.ds(second_rows + start, size), :]], axis=0)
        for which in range(4):
            spectra[which, : 2 * size] = jnp.dot(lines, middle[which], preferred_element_type=jnp.float32)
        for which in range(2):
            for first in range(0, size, HALO):
                real_rows, imag_rows = slice(first, first + HALO), slice(size + first, size + first + HALO)
                a_real, a_imag = spectra[2 * which, real_rows, :], spectra[2 * which, imag_rows, :]
                b_real, b_imag = spectra[2 * which + 1, real_rows, :], spectra[2 * which + 1, imag_rows, :]
                value = (
                    coef_a * (a_real * a_real + a_imag * a_imag)
                    + coef_b * (b_real * b_real + b_imag * b_imag)
                    - coef_ab * (a_real * b_real + a_imag * b_imag)
                )
                for half in range(halves):
                    lines = pl.ds(PAD + halves * (start + first) + half, HALO, stride=halves)
                    padded[which, lines, :] = value[:, half * BLK : (half + 1) * BLK]

    def place(level, first_device, devices_here):
        for which in (1, 0):
            shift = drift[0, (LEVELS + level) if which == 0 else (LEVELS - 1 - level)]
            channel = 2 * level + which
            if blocks % 8 == 0:
                devices = pl.ds(first_device, devices_here)
                value = padded[which, pl.ds(PAD + first_device * blocks - shift, devices_here * blocks), :]
                send[channel, devices] = value.reshape(devices_here, blocks, BLK) - send[1, devices]
            else:
                def one(step, carry, which=which, channel=channel, shift=shift):
                    peer = first_device + step
                    value = padded[which, pl.ds(PAD + peer * blocks - shift, blocks), :]
                    send[channel, peer] = value - send[1, peer]
                    return carry

                lax.fori_loop(0, devices_here, one, 0)

    def push(source, target, done, arrived, peer):
        pltpu.make_async_remote_copy(
            src_ref=source, dst_ref=target, send_sem=done, recv_sem=arrived, device_id=(sky, peer), device_id_type=MESH
        ).start()

    def ship_far(level, channels, first=0, last=half_count, ascending=False):
        def one(step, carry):
            peer = jnp.where(side == 0, half_count + (step if ascending else lax.rem(step + half_count // 2, half_count)), step)
            push(send.at[channels, peer], recv.at[channels, :, me], send_sem.at[level], far_sem.at[level], peer)
            return carry

        lax.fori_loop(first, last, one, 0)

    def ship_near(level):
        channels = pl.ds(2 * level, 2)

        def one(step, carry):
            peer = near + lax.rem(place_in + step, half_count)
            push(send.at[channels, peer], recv.at[channels, :, me], send_sem.at[LEVELS + level], near_sem.at[level], peer)
            return carry

        lax.fori_loop(1, half_count, one, 0)
        pltpu.make_async_copy(send.at[channels, me], recv.at[channels, :, me], near_sem.at[level]).start()

    def ship_base():
        def one(step, carry):
            other = lax.rem(place_in + step, half_count)
            push(send.at[1, far + other], gather.at[place_in], send_sem.at[2 * LEVELS], gather_sem, near + other)
            return carry

        lax.fori_loop(1, half_count, one, 0)
        pltpu.make_async_copy(send.at[1, mirror], gather.at[place_in], gather_sem).start()

    def one_level(level, carry):
        spread[...] = jnp.dot(weighted[...], table[...], preferred_element_type=jnp.float32)
        coefs = coefficients()
        for which in range(4):
            for first in range(0, second_rows, HALO):
                rows = slice(first, first + HALO)
                lines = slice(which * second_rows + first, which * second_rows + first + HALO)
                twist_cos, twist_sin = twist[0, rows, :], twist[1, rows, :]
                one_imag, one_real = spread[lines, :first_rows], spread[lines, first_rows:]
                middle[which, first : first + HALO, :] = (one_real * twist_cos + one_imag * twist_sin).astype(jnp.bfloat16)
                middle[which, second_rows + first : second_rows + first + HALO, :] = (
                    one_imag * twist_cos - one_real * twist_sin
                ).astype(jnp.bfloat16)

        first_row = (1 - side) * (half_rows - HALO)
        first_size = half_rows // 2 + 2 * HALO
        second_stage(coefs, first_row, first_size)
        place(level, far, half_count // 2)

        @pl.when(jnp.logical_and(level == 0, is_early))
        def _():
            pl.semaphore_wait(barrier, early_count - 1)

        @pl.when(level == 0)
        def _():
            ship_far(0, pl.ds(0, 1), 0, half_count // 2, ascending=True)

        second_stage(coefs, first_row + first_size, half_rows + HALO - first_size)
        place(level, far + half_count // 2, half_count // 2)

        @pl.when(jnp.logical_and(level == 0, side == 0))
        def _():
            pl.semaphore_wait(late_sem, late_count)

        @pl.when(level == 0)
        def _():
            ship_far(0, pl.ds(0, 1), half_count // 2, half_count, ascending=True)

        @pl.when(jnp.logical_and(level == 0, jnp.logical_and(side == 1, is_early)))
        def _():
            pl.semaphore_wait(late_sem, late_count)

        second_stage(coefs, side * (half_rows + HALO), half_rows - HALO)
        place(level, near, half_count)

        @pl.when(level == 0)
        def _():
            ship_base()

        ship_near(level)

        @pl.when(level > 0)
        def _():
            ship_far(level, pl.ds(2 * level, 2))

        @pl.when(level == LEVELS - 2)
        def _():
            pltpu.make_async_copy(gather, gather, gather_sem).wait()
            total_far[...] = jnp.sum(gather[...], axis=0)
            push(total_far, from_far, total_sem.at[0], total_sem.at[1], mirror)

        @pl.when(level < LEVELS - 1)
        def _():
            chirp_load(level + 1).wait()
            demodulate(level + 1)

        return carry

    lax.fori_loop(0, LEVELS, one_level, 0)

    far_devices, near_devices = pl.ds(pl.multiple_of(far, half_count), half_count), pl.ds(pl.multiple_of(near, half_count), half_count)
    await_bytes = lambda part, arrived: pltpu.make_async_copy(part, part, arrived).wait()

    channels = [channel for channel in range(KCOH) if channel != 1]
    names = tracks.shape[1]
    same = lax.broadcasted_iota(jnp.int32, (names, names), 0) == lax.broadcasted_iota(jnp.int32, (names, names), 1)
    loads[5].wait()
    for target, group in ((picks, channels[:-2]), (last_picks, channels[-2:])):
        chosen = []
        for channel in group:
            rate = LEVELS + channel // 2 if channel % 2 == 0 else LEVELS - 1 - channel // 2
            chosen += [jnp.where(tracks[...] == rate, 1.0, 0.0).astype(jnp.bfloat16)] * 2
        target[...] = lax.dot_general(
            jnp.where(same, 1.0, 0.0).astype(jnp.bfloat16), jnp.concatenate(chosen, axis=0), (((1,), (1,)), ((), ())),
            preferred_element_type=jnp.float32,
        ).astype(jnp.bfloat16)

    def arrive(level):
        pair = pl.ds(2 * level, 2)
        await_bytes(recv.at[pair, :, near_devices], near_sem.at[level])
        await_bytes(recv.at[pair if level else pl.ds(0, 1), :, far_devices], far_sem.at[level])

    def stage(step, channel):
        line = step * 2 * count
        for block in range(blocks):
            value = recv[channel, block]
            high = value.astype(jnp.bfloat16)
            lanes = slice(block * BLK, (block + 1) * BLK)
            staged[line : line + count, lanes] = high
            staged[line + count : line + 2 * count, lanes] = (value - high.astype(jnp.float32)).astype(jnp.bfloat16)

    for level in range(LEVELS - 1):
        arrive(level)
        for step, channel in enumerate(channels):
            if channel // 2 == level:
                stage(step, channel)
    await_bytes(from_far, total_sem.at[1])
    base = jnp.sum(recv[1, :, near_devices], axis=1) + from_far[...]
    width = halves * BLK
    parts = blocks // halves
    for part in range(parts):
        columns = slice(part * width, (part + 1) * width)
        line = jnp.concatenate([base[part * halves + half : part * halves + half + 1, :] for half in range(halves)], axis=1)
        out_ref[:, columns] = line + jnp.dot(
            picks[...], staged[:, columns], preferred_element_type=jnp.float32
        )
    arrive(LEVELS - 1)
    for part in range(parts):
        columns = slice(part * width, (part + 1) * width)
        lines = []
        for channel in channels[-2:]:
            value = jnp.concatenate([recv[channel, part * halves + half] for half in range(halves)], axis=1)
            high = value.astype(jnp.bfloat16)
            lines += [high, (value - high.astype(jnp.float32)).astype(jnp.bfloat16)]
        out_ref[:, columns] += jnp.dot(
            last_picks[...], jnp.concatenate(lines, axis=0), preferred_element_type=jnp.float32
        )

    for level in range(LEVELS):
        pair = pl.ds(2 * level, 2)
        await_bytes(send.at[pair if level else pl.ds(0, 1), pl.ds(0, half_count)], send_sem.at[level])
        await_bytes(send.at[pair, pl.ds(0, half_count - 1)], send_sem.at[LEVELS + level])
    await_bytes(send.at[1, pl.ds(0, half_count - 1)], send_sem.at[2 * LEVELS])
    await_bytes(total_far, total_sem.at[0])


def local(count, strain_series, antenna, drift, tracks):
    points = strain_series.shape[2]
    first_rows, second_rows = DFT_ROWS, points // DFT_ROWS
    segments = tracks.shape[1]
    blocks = points // count // BLK
    blocked = lambda array: array.reshape(2, points // BLK, BLK).transpose(1, 0, 2).reshape(2 * points // BLK, BLK)
    hbm = pl.BlockSpec(memory_space=pl.ANY)
    chirps = chirp_table(points, first_rows)
    factors = twist_factors(points, first_rows)
    block = (2 * points // BLK, BLK)
    summed = pl.pallas_call(
        functools.partial(kernel, count),
        out_shape=pltpu.VMEM((tracks.shape[0], points // count), jnp.float32),
        in_specs=[hbm] * 7,
        out_specs=pl.BlockSpec(memory_space=pltpu.VMEM),
        scratch_shapes=[
            pltpu.SMEM(drift.shape, jnp.int32),
            pltpu.VMEM(block, jnp.bfloat16),
            pltpu.VMEM(block, jnp.float32),
            pltpu.VMEM(block, jnp.float32),
            pltpu.VMEM(chirps.shape, jnp.float32),
            pltpu.VMEM(factors.shape, jnp.float32),
            pltpu.VMEM((2, second_rows, first_rows), jnp.float32),
            pltpu.VMEM((2 * first_rows, 2 * first_rows), jnp.bfloat16),
            pltpu.VMEM((segments, tracks.shape[0]), jnp.int32),
            pltpu.VMEM((2, second_rows, first_rows), jnp.float32),
            pltpu.VMEM((2, second_rows, first_rows), jnp.float32),
            pltpu.VMEM((4 * second_rows, 2 * first_rows), jnp.bfloat16),
            pltpu.VMEM((4 * second_rows, 2 * first_rows), jnp.float32),
            pltpu.VMEM((4, 2 * second_rows, first_rows), jnp.bfloat16),
            pltpu.VMEM((4, second_rows + 2 * HALO, first_rows), jnp.float32),
            pltpu.VMEM((2, points // BLK + 2 * PAD, BLK), jnp.float32),
            pltpu.VMEM((KCOH, count, blocks, BLK), jnp.float32),
            pltpu.VMEM((KCOH, blocks, count, BLK), jnp.float32),
            pltpu.VMEM((count // 2, blocks, BLK), jnp.float32),
            pltpu.VMEM((blocks, BLK), jnp.float32),
            pltpu.VMEM((blocks, BLK), jnp.float32),
            pltpu.VMEM((tracks.shape[0], (KCOH - 3) * 2 * count), jnp.bfloat16),
            pltpu.VMEM((tracks.shape[0], 4 * count), jnp.bfloat16),
            pltpu.VMEM(((KCOH - 3) * 2 * count, points // count), jnp.bfloat16),
            pltpu.SemaphoreType.DMA((6,)),
            pltpu.SemaphoreType.DMA((LEVELS,)),
            pltpu.SemaphoreType.DMA((2 * LEVELS + 1,)),
            pltpu.SemaphoreType.DMA((LEVELS,)),
            pltpu.SemaphoreType.DMA((LEVELS,)),
            pltpu.SemaphoreType.DMA,
            pltpu.SemaphoreType.DMA((2,)),
            pltpu.SemaphoreType.REGULAR,
        ],
        compiler_params=pltpu.CompilerParams(
            collective_id=0, has_side_effects=True, vmem_limit_bytes=60 << 20
        ),
    )(
        drift,
        blocked(strain_series),
        blocked(antenna),
        jnp.asarray(chirps),
        jnp.asarray(factors),
        jnp.asarray(dft_table(first_rows)),
        tracks.T,
    )
    return summed / segments


def solution(mesh):
    return jax.shard_map(
        functools.partial(local, mesh.shape["seg"]),
        mesh=mesh,
        in_specs=(
            P(("sky", "seg"), None, None),
            P(("sky", "seg"), None, None),
            P(("sky", "seg"), None),
            P(),
        ),
        out_specs=P("sky", "seg"),
        check_vma=False,
    )
```

```python
import functools
import math

import jax
import jax.numpy as jnp
import numpy as np
from jax import lax
from jax.experimental import pallas as pl
from jax.experimental.pallas import tpu as pltpu
from jax.sharding import PartitionSpec as P

DFT_ROWS = 256
BLK = 128
KCOH = 6
LEVELS = KCOH // 2
PAD = 8
HALO = 16
SUB = 8
HALVES = DFT_ROWS // BLK
MESH = pl.DeviceIdType.MESH

chirp_step = 3.0
tiny_eps = 1e-06


def dft_table(rows):
    index = np.arange(rows, dtype=np.int64)
    angle = np.float32(2.0 * math.pi / rows) * (index[:, None] * index[None, :] % rows).astype(np.float32)
    cos, sin = np.cos(angle), np.sin(angle)
    return np.block([[cos, sin], [-sin, cos]]).astype(jnp.bfloat16)


def twist_factors(points, first_rows):
    second_rows = points // first_rows
    inner = np.concatenate([SUB * np.arange(second_rows // SUB, dtype=np.int64), np.arange(SUB, dtype=np.int64)])
    outer = np.arange(first_rows, dtype=np.int64)
    angle = (2.0 * math.pi / points) * (inner[:, None] * outer[None, :] % points).astype(np.float64)
    return np.stack([np.cos(angle), np.sin(angle)]).astype(np.float32)


def chirp_table(points, first_rows):
    position = np.arange(points, dtype=np.float32) / np.float32(points)
    rate = (np.arange(LEVELS, KCOH, dtype=np.float32) - np.float32((KCOH - 1) / 2.0)) * np.float32(chirp_step)
    phases = (np.float32(2.0 * math.pi) * rate)[:, None] * (position * position)[None, :]
    both = np.stack([np.cos(phases), np.sin(phases)], 1).astype(np.float32)
    return np.swapaxes(both.reshape(LEVELS, 2, first_rows, points // first_rows), 2, 3).copy()


def kernel(
    count, drift_hbm, series_hbm, antenna_hbm, chirp_hbm, factors_hbm, table_hbm, tracks_hbm,
    out_ref, recv, last_picks,
    drift, series_in, series, antenna, chirp, factors, twist, table, tracks,
    strain, weights, weighted, spread, middle, spectra, padded,
    send, gather, total_far, from_far, picks, staged,
    load_sem, chirp_sem, send_sem, far_sem, near_sem, gather_sem, total_sem, late_sem,
):
    _, second_rows, first_rows = strain.shape
    halves = first_rows // BLK
    blocks = second_rows * halves // count
    half_count = count // 2
    early_count = half_count + half_count // 2
    late_count = count - early_count
    half_rows = second_rows // 2
    points = first_rows * second_rows
    sky = lax.axis_index("sky")
    me = lax.axis_index("seg")
    side = lax.div(me, half_count)
    place_in = lax.rem(me, half_count)
    far = (1 - side) * half_count
    near = side * half_count
    mirror = far + place_in

    loads = [
        pltpu.make_async_copy(source, target, load_sem.at[index])
        for index, (source, target) in enumerate([
            (series_hbm, series_in), (antenna_hbm, antenna), (table_hbm, table), (factors_hbm, factors), (drift_hbm, drift),
            (tracks_hbm, tracks),
        ])
    ]
    chirp_load = lambda level: pltpu.make_async_copy(chirp_hbm.at[level], chirp.at[level], chirp_sem.at[level])
    loads[0].start()
    loads[3].start()
    loads[1].start()
    chirp_load(0).start()
    for index in (4, 2, 5):
        loads[index].start()

    barrier = pltpu.get_barrier_semaphore()

    is_early = me < early_count

    def signal(semaphore, first, wide):
        def one(step, carry):
            peer = lax.rem(me + step, count) if wide else first + step
            pl.semaphore_signal(semaphore, inc=1, device_id=(sky, peer), device_id_type=MESH)
            return carry

        return one

    @pl.when(is_early)
    def _():
        lax.fori_loop(1, count, signal(barrier, 0, True), 0)

    @pl.when(jnp.logical_not(is_early))
    def _():
        lax.fori_loop(0, me - early_count, signal(barrier, early_count, False), 0)
        lax.fori_loop(me - early_count + 1, late_count, signal(barrier, early_count, False), 0)

    for which in range(2):
        padded[which, :PAD] = jnp.zeros((PAD, BLK), jnp.float32)
        padded[which, PAD + second_rows * halves :] = jnp.zeros((PAD, BLK), jnp.float32)
    send[1] = jnp.zeros(send.shape[1:], jnp.float32)

    @pl.when(jnp.logical_not(is_early))
    def _():
        pl.semaphore_wait(barrier, count - 1)
        lax.fori_loop(0, early_count, signal(late_sem, 0, False), 0)

    pieces = second_rows // BLK

    def turned(source, target):
        for which in range(2):
            for piece in range(pieces):
                lines = pl.ds(2 * piece + which, first_rows, stride=2 * pieces)
                target[which, piece * BLK : (piece + 1) * BLK, :] = source[lines, :].T

    def demodulate(level):
        for first in range(0, second_rows, HALO):
            rows = slice(first, first + HALO)
            chirp_cos, chirp_sin = chirp[level, 0, rows, :], chirp[level, 1, rows, :]
            real, imag = strain[0, rows, :], strain[1, rows, :]
            real_cos, imag_sin = real * chirp_cos, imag * chirp_sin
            imag_cos, real_sin = imag * chirp_cos, real * chirp_sin
            demods = ((real_cos + imag_sin, imag_cos - real_sin), (real_cos - imag_sin, imag_cos + real_sin))
            for kind in range(2):
                weight = weights[kind, rows, :]
                for upper in range(2):
                    start = (2 * upper + kind) * second_rows + first
                    for part in range(2):
                        lanes = slice((1 - part) * first_rows, (2 - part) * first_rows)
                        weighted[start : start + HALO, lanes] = (weight * demods[upper][part]).astype(jnp.bfloat16)

    loads[0].wait()
    series[...] = series_in[...].astype(jnp.float32)
    loads[3].wait()
    turned(series, strain)
    steps = second_rows // SUB
    step_cos, step_sin = factors[0, steps:, :], factors[1, steps:, :]
    for step in range(steps):
        base_cos, base_sin = factors[0, step : step + 1, :], factors[1, step : step + 1, :]
        twist[0, step * SUB : (step + 1) * SUB, :] = base_cos * step_cos - base_sin * step_sin
        twist[1, step * SUB : (step + 1) * SUB, :] = base_sin * step_cos + base_cos * step_sin
    loads[1].wait()
    turned(antenna, weights)
    chirp_load(0).wait()
    demodulate(0)

    def coefficients():
        sums = [0.0, 0.0, 0.0]
        for first in range(0, second_rows, HALO):
            rows = slice(first, first + HALO)
            weight_a, weight_b = weights[0, rows, :], weights[1, rows, :]
            sums = [held + value for held, value in zip(sums, (weight_a * weight_a, weight_b * weight_b, weight_a * weight_b))]
        aa, bb, ab = [jnp.sum(jnp.sum(held, axis=0, keepdims=True), axis=1, keepdims=True) / points for held in sums]
        aa, bb = aa + tiny_eps, bb + tiny_eps
        scale = 1.0 / (points * jnp.maximum(aa * bb - ab * ab, 0.1 * aa * bb))
        return bb * scale, aa * scale, 2.0 * ab * scale

    loads[4].wait()
    loads[2].wait()
    for level in range(1, LEVELS):
        chirp_load(level).start()

    def second_stage(coefs, start, size):
        coef_a, coef_b, coef_ab = coefs
        start = pl.multiple_of(start, HALO)
        lines = jnp.concatenate([table[pl.ds(start, size), :], table[pl.ds(second_rows + start, size), :]], axis=0)
        for which in range(4):
            spectra[which, : 2 * size] = jnp.dot(lines, middle[which], preferred_element_type=jnp.float32)
        for which in range(2):
            for first in range(0, size, HALO):
                real_rows, imag_rows = slice(first, first + HALO), slice(size + first, size + first + HALO)
                a_real, a_imag = spectra[2 * which, real_rows, :], spectra[2 * which, imag_rows, :]
                b_real, b_imag = spectra[2 * which + 1, real_rows, :], spectra[2 * which + 1, imag_rows, :]
                value = (
                    coef_a * (a_real * a_real + a_imag * a_imag)
                    + coef_b * (b_real * b_real + b_imag * b_imag)
                    - coef_ab * (a_real * b_real + a_imag * b_imag)
                )
                for half in range(halves):
                    lines = pl.ds(PAD + halves * (start + first) + half, HALO, stride=halves)
                    padded[which, lines, :] = value[:, half * BLK : (half + 1) * BLK]

    def place(level, first_device, devices_here):
        for which in (1, 0):
            shift = drift[0, (LEVELS + level) if which == 0 else (LEVELS - 1 - level)]
            channel = 2 * level + which
            if blocks % 8 == 0:
                devices = pl.ds(first_device, devices_here)
                value = padded[which, pl.ds(PAD + first_device * blocks - shift, devices_here * blocks), :]
                send[channel, devices] = value.reshape(devices_here, blocks, BLK) - send[1, devices]
            else:
                def one(step, carry, which=which, channel=channel, shift=shift):
                    peer = first_device + step
                    value = padded[which, pl.ds(PAD + peer * blocks - shift, blocks), :]
                    send[channel, peer] = value - send[1, peer]
                    return carry

                lax.fori_loop(0, devices_here, one, 0)

    def push(source, target, done, arrived, peer):
        pltpu.make_async_remote_copy(
            src_ref=source, dst_ref=target, send_sem=done, recv_sem=arrived, device_id=(sky, peer), device_id_type=MESH
        ).start()

    def ship_far(level, channels, first=0, last=half_count, ascending=False):
        def one(step, carry):
            peer = jnp.where(side == 0, half_count + (step if ascending else lax.rem(step + half_count // 2, half_count)), step)
            push(send.at[channels, peer], recv.at[channels, :, me], send_sem.at[level], far_sem.at[level], peer)
            return carry

        lax.fori_loop(first, last, one, 0)

    def ship_near(level):
        channels = pl.ds(2 * level, 2)

        def one(step, carry):
            peer = near + lax.rem(place_in + step, half_count)
            push(send.at[channels, peer], recv.at[channels, :, me], send_sem.at[LEVELS + level], near_sem.at[level], peer)
            return carry

        lax.fori_loop(1, half_count, one, 0)
        pltpu.make_async_copy(send.at[channels, me], recv.at[channels, :, me], near_sem.at[level]).start()

    def ship_base():
        def one(step, carry):
            other = lax.rem(place_in + step, half_count)
            push(send.at[1, far + other], gather.at[place_in], send_sem.at[2 * LEVELS], gather_sem, near + other)
            return carry

        lax.fori_loop(1, half_count, one, 0)
        pltpu.make_async_copy(send.at[1, mirror], gather.at[place_in], gather_sem).start()

    def one_level(level, carry):
        spread[...] = jnp.dot(weighted[...], table[...], preferred_element_type=jnp.float32)
        coefs = coefficients()
        for which in range(4):
            for first in range(0, second_rows, HALO):
                rows = slice(first, first + HALO)
                lines = slice(which * second_rows + first, which * second_rows + first + HALO)
                twist_cos, twist_sin = twist[0, rows, :], twist[1, rows, :]
                one_imag, one_real = spread[lines, :first_rows], spread[lines, first_rows:]
                middle[which, first : first + HALO, :] = (one_real * twist_cos + one_imag * twist_sin).astype(jnp.bfloat16)
                middle[which, second_rows + first : second_rows + first + HALO, :] = (
                    one_imag * twist_cos - one_real * twist_sin
                ).astype(jnp.bfloat16)

        first_row = (1 - side) * (half_rows - HALO)
        first_size = half_rows // 2 + 2 * HALO
        second_stage(coefs, first_row, first_size)
        place(level, far, half_count // 2)

        @pl.when(jnp.logical_and(level == 0, is_early))
        def _():
            pl.semaphore_wait(barrier, early_count - 1)

        @pl.when(level == 0)
        def _():
            ship_far(0, pl.ds(0, 1), 0, half_count // 2, ascending=True)

        second_stage(coefs, first_row + first_size, half_rows + HALO - first_size)
        place(level, far + half_count // 2, half_count // 2)

        @pl.when(jnp.logical_and(level == 0, side == 0))
        def _():
            pl.semaphore_wait(late_sem, late_count)

        @pl.when(level == 0)
        def _():
            ship_far(0, pl.ds(0, 1), half_count // 2, half_count, ascending=True)

        @pl.when(jnp.logical_and(level == 0, jnp.logical_and(side == 1, is_early)))
        def _():
            pl.semaphore_wait(late_sem, late_count)

        second_stage(coefs, side * (half_rows + HALO), half_rows - HALO)
        place(level, near, half_count)

        @pl.when(level == 0)
        def _():
            ship_base()

        ship_near(level)

        @pl.when(level > 0)
        def _():
            ship_far(level, pl.ds(2 * level, 2))

        @pl.when(level == LEVELS - 2)
        def _():
            pltpu.make_async_copy(gather, gather, gather_sem).wait()
            total_far[...] = jnp.sum(gather[...], axis=0)
            push(total_far, from_far, total_sem.at[0], total_sem.at[1], mirror)

        @pl.when(level < LEVELS - 1)
        def _():
            chirp_load(level + 1).wait()
            demodulate(level + 1)

        return carry

    lax.fori_loop(0, LEVELS, one_level, 0)

    far_devices, near_devices = pl.ds(pl.multiple_of(far, half_count), half_count), pl.ds(pl.multiple_of(near, half_count), half_count)
    await_bytes = lambda part, arrived: pltpu.make_async_copy(part, part, arrived).wait()

    channels = [channel for channel in range(KCOH) if channel != 1]
    names = tracks.shape[1]
    same = lax.broadcasted_iota(jnp.int32, (names, names), 0) == lax.broadcasted_iota(jnp.int32, (names, names), 1)
    loads[5].wait()
    for target, group in ((picks, channels[:-2]), (last_picks, channels[-2:])):
        chosen = []
        for channel in group:
            rate = LEVELS + channel // 2 if channel % 2 == 0 else LEVELS - 1 - channel // 2
            chosen += [jnp.where(tracks[...] == rate, 1.0, 0.0).astype(jnp.bfloat16)] * 2
        target[...] = lax.dot_general(
            jnp.where(same, 1.0, 0.0).astype(jnp.bfloat16), jnp.concatenate(chosen, axis=0), (((1,), (1,)), ((), ())),
            preferred_element_type=jnp.float32,
        ).astype(jnp.bfloat16)

    def arrive(level):
        pair = pl.ds(2 * level, 2)
        await_bytes(recv.at[pair, :, near_devices], near_sem.at[level])
        await_bytes(recv.at[pair if level else pl.ds(0, 1), :, far_devices], far_sem.at[level])

    def stage(step, channel):
        line = step * 2 * count
        for block in range(blocks):
            value = recv[channel, block]
            high = value.astype(jnp.bfloat16)
            lanes = slice(block * BLK, (block + 1) * BLK)
            staged[line : line + count, lanes] = high
            staged[line + count : line + 2 * count, lanes] = (value - high.astype(jnp.float32)).astype(jnp.bfloat16)

    for level in range(LEVELS - 1):
        arrive(level)
        for step, channel in enumerate(channels):
            if channel // 2 == level:
                stage(step, channel)
    await_bytes(from_far, total_sem.at[1])
    base = jnp.sum(recv[1, :, near_devices], axis=1) + from_far[...]
    width = halves * BLK
    parts = blocks // halves
    for part in range(parts):
        columns = slice(part * width, (part + 1) * width)
        line = jnp.concatenate([base[part * halves + half : part * halves + half + 1, :] for half in range(halves)], axis=1)
        out_ref[:, columns] = line + jnp.dot(
            picks[...], staged[:, columns], preferred_element_type=jnp.float32
        )
    arrive(LEVELS - 1)
    for level in range(LEVELS):
        pair = pl.ds(2 * level, 2)
        await_bytes(send.at[pair if level else pl.ds(0, 1), pl.ds(0, half_count)], send_sem.at[level])
        await_bytes(send.at[pair, pl.ds(0, half_count - 1)], send_sem.at[LEVELS + level])
    await_bytes(send.at[1, pl.ds(0, half_count - 1)], send_sem.at[2 * LEVELS])
    await_bytes(total_far, total_sem.at[0])


def finish(segments, partial_ref, recv_ref, picks_ref, out_hbm, summed, sem):
    _, blocks, _, lanes = recv_ref.shape
    parts = blocks // HALVES
    width = HALVES * lanes
    group = max(parts // 4, 1)
    copies = []
    for part in range(parts):
        columns = slice(part * width, (part + 1) * width)
        lines = []
        for channel in (KCOH - 2, KCOH - 1):
            value = jnp.concatenate([recv_ref[channel, part * HALVES + half] for half in range(HALVES)], axis=1)
            high = value.astype(jnp.bfloat16)
            lines += [high, (value - high.astype(jnp.float32)).astype(jnp.bfloat16)]
        total = partial_ref[:, columns] + jnp.dot(
            picks_ref[...], jnp.concatenate(lines, axis=0), preferred_element_type=jnp.float32
        )
        summed[:, columns] = total * (1.0 / segments)
        if (part + 1) % group == 0:
            done = slice((part + 1 - group) * width, (part + 1) * width)
            copies.append(pltpu.make_async_copy(summed.at[:, done], out_hbm.at[:, done], sem.at[len(copies)]))
            copies[-1].start()
    for copy in copies:
        copy.wait()


def local(count, strain_series, antenna, drift, tracks):
    points = strain_series.shape[2]
    first_rows, second_rows = DFT_ROWS, points // DFT_ROWS
    segments = tracks.shape[1]
    blocks = points // count // BLK
    blocked = lambda array: array.reshape(2, points // BLK, BLK).transpose(1, 0, 2).reshape(2 * points // BLK, BLK)
    hbm = pl.BlockSpec(memory_space=pl.ANY)
    vmem = pl.BlockSpec(memory_space=pltpu.VMEM)
    chirps = chirp_table(points, first_rows)
    factors = twist_factors(points, first_rows)
    block = (2 * points // BLK, BLK)
    partial, received, picks = pl.pallas_call(
        functools.partial(kernel, count),
        out_shape=(
            pltpu.VMEM((tracks.shape[0], points // count), jnp.float32),
            pltpu.VMEM((KCOH, blocks, count, BLK), jnp.float32),
            pltpu.VMEM((tracks.shape[0], 4 * count), jnp.bfloat16),
        ),
        in_specs=[hbm] * 7,
        out_specs=(vmem, vmem, vmem),
        scratch_shapes=[
            pltpu.SMEM(drift.shape, jnp.int32),
            pltpu.VMEM(block, jnp.bfloat16),
            pltpu.VMEM(block, jnp.float32),
            pltpu.VMEM(block, jnp.float32),
            pltpu.VMEM(chirps.shape, jnp.float32),
            pltpu.VMEM(factors.shape, jnp.float32),
            pltpu.VMEM((2, second_rows, first_rows), jnp.float32),
            pltpu.VMEM((2 * first_rows, 2 * first_rows), jnp.bfloat16),
            pltpu.VMEM((segments, tracks.shape[0]), jnp.int32),
            pltpu.VMEM((2, second_rows, first_rows), jnp.float32),
            pltpu.VMEM((2, second_rows, first_rows), jnp.float32),
            pltpu.VMEM((4 * second_rows, 2 * first_rows), jnp.bfloat16),
            pltpu.VMEM((4 * second_rows, 2 * first_rows), jnp.float32),
            pltpu.VMEM((4, 2 * second_rows, first_rows), jnp.bfloat16),
            pltpu.VMEM((4, second_rows + 2 * HALO, first_rows), jnp.float32),
            pltpu.VMEM((2, points // BLK + 2 * PAD, BLK), jnp.float32),
            pltpu.VMEM((KCOH, count, blocks, BLK), jnp.float32),
            pltpu.VMEM((count // 2, blocks, BLK), jnp.float32),
            pltpu.VMEM((blocks, BLK), jnp.float32),
            pltpu.VMEM((blocks, BLK), jnp.float32),
            pltpu.VMEM((tracks.shape[0], (KCOH - 3) * 2 * count), jnp.bfloat16),
            pltpu.VMEM(((KCOH - 3) * 2 * count, points // count), jnp.bfloat16),
            pltpu.SemaphoreType.DMA((6,)),
            pltpu.SemaphoreType.DMA((LEVELS,)),
            pltpu.SemaphoreType.DMA((2 * LEVELS + 1,)),
            pltpu.SemaphoreType.DMA((LEVELS,)),
            pltpu.SemaphoreType.DMA((LEVELS,)),
            pltpu.SemaphoreType.DMA,
            pltpu.SemaphoreType.DMA((2,)),
            pltpu.SemaphoreType.REGULAR,
        ],
        compiler_params=pltpu.CompilerParams(
            collective_id=0, has_side_effects=True, vmem_limit_bytes=60 << 20
        ),
    )(
        drift,
        blocked(strain_series),
        blocked(antenna),
        jnp.asarray(chirps),
        jnp.asarray(factors),
        jnp.asarray(dft_table(first_rows)),
        tracks.T,
    )
    parts = max(blocks // HALVES, 1)
    return pl.pallas_call(
        functools.partial(finish, segments),
        out_shape=jax.ShapeDtypeStruct(partial.shape, jnp.float32),
        in_specs=[vmem] * 3,
        out_specs=hbm,
        scratch_shapes=[pltpu.VMEM(partial.shape, jnp.float32), pltpu.SemaphoreType.DMA((min(parts, 8),))],
        compiler_params=pltpu.CompilerParams(vmem_limit_bytes=8 << 20),
    )(partial, received, picks)


def solution(mesh):
    return jax.shard_map(
        functools.partial(local, mesh.shape["seg"]),
        mesh=mesh,
        in_specs=(
            P(("sky", "seg"), None, None),
            P(("sky", "seg"), None, None),
            P(("sky", "seg"), None),
            P(),
        ),
        out_specs=P("sky", "seg"),
        check_vma=False,
    )
```

```python
import functools
import math

import jax
import jax.numpy as jnp
import numpy as np
from jax import lax
from jax.experimental import pallas as pl
from jax.experimental.pallas import tpu as pltpu
from jax.sharding import PartitionSpec as P

DFT_ROWS = 256
BLK = 128
KCOH = 6
LEVELS = KCOH // 2
PAD = 8
HALO = 16
SUB = 8
HALVES = DFT_ROWS // BLK
MESH = pl.DeviceIdType.MESH

chirp_step = 3.0
tiny_eps = 1e-06


def dft_table(rows):
    index = np.arange(rows, dtype=np.int64)
    angle = np.float32(2.0 * math.pi / rows) * (index[:, None] * index[None, :] % rows).astype(np.float32)
    cos, sin = np.cos(angle), np.sin(angle)
    return np.block([[cos, sin], [-sin, cos]]).astype(jnp.bfloat16)


def twist_factors(points, first_rows):
    second_rows = points // first_rows
    inner = np.concatenate([SUB * np.arange(second_rows // SUB, dtype=np.int64), np.arange(SUB, dtype=np.int64)])
    outer = np.arange(first_rows, dtype=np.int64)
    angle = (2.0 * math.pi / points) * (inner[:, None] * outer[None, :] % points).astype(np.float64)
    return np.stack([np.cos(angle), np.sin(angle)]).astype(np.float32)


def chirp_table(points, first_rows):
    position = np.arange(points, dtype=np.float32) / np.float32(points)
    rate = (np.arange(LEVELS, KCOH, dtype=np.float32) - np.float32((KCOH - 1) / 2.0)) * np.float32(chirp_step)
    phases = (np.float32(2.0 * math.pi) * rate)[:, None] * (position * position)[None, :]
    both = np.stack([np.cos(phases), np.sin(phases)], 1).astype(np.float32)
    return np.swapaxes(both.reshape(LEVELS, 2, first_rows, points // first_rows), 2, 3).copy()


def kernel(
    count, drift_hbm, series_hbm, antenna_hbm, chirp_hbm, factors_hbm, table_hbm, tracks_hbm,
    out_ref, recv, last_picks,
    drift, series_in, series, antenna, chirp, factors, twist, table, tracks,
    strain, weights, weighted, spread, middle, spectra, padded,
    send, gather, total_far, from_far, picks, staged,
    load_sem, chirp_sem, send_sem, far_sem, near_sem, gather_sem, total_sem, late_sem,
):
    _, second_rows, first_rows = strain.shape
    halves = first_rows // BLK
    blocks = second_rows * halves // count
    half_count = count // 2
    early_count = half_count + half_count // 2
    late_count = count - early_count
    half_rows = second_rows // 2
    points = first_rows * second_rows
    sky = lax.axis_index("sky")
    me = lax.axis_index("seg")
    side = lax.div(me, half_count)
    place_in = lax.rem(me, half_count)
    far = (1 - side) * half_count
    near = side * half_count
    mirror = far + place_in

    loads = [
        pltpu.make_async_copy(source, target, load_sem.at[index])
        for index, (source, target) in enumerate([
            (series_hbm, series_in), (antenna_hbm, antenna), (table_hbm, table), (factors_hbm, factors), (drift_hbm, drift),
            (tracks_hbm, tracks),
        ])
    ]
    chirp_load = lambda level: pltpu.make_async_copy(chirp_hbm.at[level], chirp.at[level], chirp_sem.at[level])
    loads[0].start()
    loads[3].start()
    loads[1].start()
    chirp_load(0).start()
    for index in (4, 2, 5):
        loads[index].start()

    barrier = pltpu.get_barrier_semaphore()

    is_early = me < early_count

    def signal(semaphore, first, wide):
        def one(step, carry):
            peer = lax.rem(me + step, count) if wide else first + step
            pl.semaphore_signal(semaphore, inc=1, device_id=(sky, peer), device_id_type=MESH)
            return carry

        return one

    @pl.when(is_early)
    def _():
        lax.fori_loop(1, count, signal(barrier, 0, True), 0)

    @pl.when(jnp.logical_not(is_early))
    def _():
        lax.fori_loop(0, me - early_count, signal(barrier, early_count, False), 0)
        lax.fori_loop(me - early_count + 1, late_count, signal(barrier, early_count, False), 0)

    for which in range(2):
        padded[which, :PAD] = jnp.zeros((PAD, BLK), jnp.float32)
        padded[which, PAD + second_rows * halves :] = jnp.zeros((PAD, BLK), jnp.float32)
    send[1] = jnp.zeros(send.shape[1:], jnp.float32)

    @pl.when(jnp.logical_not(is_early))
    def _():
        pl.semaphore_wait(barrier, count - 1)
        lax.fori_loop(0, early_count, signal(late_sem, 0, False), 0)

    pieces = second_rows // BLK

    def turned(source, target):
        for which in range(2):
            for piece in range(pieces):
                lines = pl.ds(2 * piece + which, first_rows, stride=2 * pieces)
                target[which, piece * BLK : (piece + 1) * BLK, :] = source[lines, :].T

    def demodulate(level):
        for first in range(0, second_rows, HALO):
            rows = slice(first, first + HALO)
            chirp_cos, chirp_sin = chirp[level, 0, rows, :], chirp[level, 1, rows, :]
            real, imag = strain[0, rows, :], strain[1, rows, :]
            real_cos, imag_sin = real * chirp_cos, imag * chirp_sin
            imag_cos, real_sin = imag * chirp_cos, real * chirp_sin
            demods = ((real_cos + imag_sin, imag_cos - real_sin), (real_cos - imag_sin, imag_cos + real_sin))
            for kind in range(2):
                weight = weights[kind, rows, :]
                for upper in range(2):
                    start = (2 * upper + kind) * second_rows + first
                    for part in range(2):
                        lanes = slice((1 - part) * first_rows, (2 - part) * first_rows)
                        weighted[start : start + HALO, lanes] = (weight * demods[upper][part]).astype(jnp.bfloat16)

    loads[0].wait()
    series[...] = series_in[...].astype(jnp.float32)
    loads[3].wait()
    turned(series, strain)
    steps = second_rows // SUB
    step_cos, step_sin = factors[0, steps:, :], factors[1, steps:, :]
    for step in range(steps):
        base_cos, base_sin = factors[0, step : step + 1, :], factors[1, step : step + 1, :]
        twist[0, step * SUB : (step + 1) * SUB, :] = base_cos * step_cos - base_sin * step_sin
        twist[1, step * SUB : (step + 1) * SUB, :] = base_sin * step_cos + base_cos * step_sin
    loads[1].wait()
    turned(antenna, weights)
    chirp_load(0).wait()
    demodulate(0)

    def coefficients():
        sums = [0.0, 0.0, 0.0]
        for first in range(0, second_rows, HALO):
            rows = slice(first, first + HALO)
            weight_a, weight_b = weights[0, rows, :], weights[1, rows, :]
            sums = [held + value for held, value in zip(sums, (weight_a * weight_a, weight_b * weight_b, weight_a * weight_b))]
        aa, bb, ab = [jnp.sum(jnp.sum(held, axis=0, keepdims=True), axis=1, keepdims=True) / points for held in sums]
        aa, bb = aa + tiny_eps, bb + tiny_eps
        scale = 1.0 / (points * jnp.maximum(aa * bb - ab * ab, 0.1 * aa * bb))
        return bb * scale, aa * scale, 2.0 * ab * scale

    loads[4].wait()
    loads[2].wait()
    for level in range(1, LEVELS):
        chirp_load(level).start()

    def second_stage(coefs, start, size):
        coef_a, coef_b, coef_ab = coefs
        start = pl.multiple_of(start, HALO)
        lines = jnp.concatenate([table[pl.ds(start, size), :], table[pl.ds(second_rows + start, size), :]], axis=0)
        for which in range(4):
            spectra[which, : 2 * size] = jnp.dot(lines, middle[which], preferred_element_type=jnp.float32)
        for which in range(2):
            for first in range(0, size, HALO):
                real_rows, imag_rows = slice(first, first + HALO), slice(size + first, size + first + HALO)
                a_real, a_imag = spectra[2 * which, real_rows, :], spectra[2 * which, imag_rows, :]
                b_real, b_imag = spectra[2 * which + 1, real_rows, :], spectra[2 * which + 1, imag_rows, :]
                value = (
                    coef_a * (a_real * a_real + a_imag * a_imag)
                    + coef_b * (b_real * b_real + b_imag * b_imag)
                    - coef_ab * (a_real * b_real + a_imag * b_imag)
                )
                for half in range(halves):
                    lines = pl.ds(PAD + halves * (start + first) + half, HALO, stride=halves)
                    padded[which, lines, :] = value[:, half * BLK : (half + 1) * BLK]

    def place(level, first_device, devices_here):
        for which in (1, 0):
            shift = drift[0, (LEVELS + level) if which == 0 else (LEVELS - 1 - level)]
            channel = 2 * level + which
            if blocks % 8 == 0:
                devices = pl.ds(first_device, devices_here)
                value = padded[which, pl.ds(PAD + first_device * blocks - shift, devices_here * blocks), :]
                send[channel, devices] = value.reshape(devices_here, blocks, BLK) - send[1, devices]
            else:
                def one(step, carry, which=which, channel=channel, shift=shift):
                    peer = first_device + step
                    value = padded[which, pl.ds(PAD + peer * blocks - shift, blocks), :]
                    send[channel, peer] = value - send[1, peer]
                    return carry

                lax.fori_loop(0, devices_here, one, 0)

    def push(source, target, done, arrived, peer):
        pltpu.make_async_remote_copy(
            src_ref=source, dst_ref=target, send_sem=done, recv_sem=arrived, device_id=(sky, peer), device_id_type=MESH
        ).start()

    def ship_far(level, channels, first=0, last=half_count, ascending=False):
        def one(step, carry):
            peer = jnp.where(side == 0, half_count + (step if ascending else lax.rem(step + half_count // 2, half_count)), step)
            push(send.at[channels, peer], recv.at[channels, :, me], send_sem.at[level], far_sem.at[level], peer)
            return carry

        lax.fori_loop(first, last, one, 0)

    def ship_near(level):
        channels = pl.ds(2 * level, 2)

        def one(step, carry):
            peer = near + lax.rem(place_in + step, half_count)
            push(send.at[channels, peer], recv.at[channels, :, me], send_sem.at[LEVELS + level], near_sem.at[level], peer)
            return carry

        lax.fori_loop(1, half_count, one, 0)
        pltpu.make_async_copy(send.at[channels, me], recv.at[channels, :, me], near_sem.at[level]).start()

    def ship_base():
        def one(step, carry):
            other = lax.rem(place_in + step, half_count)
            push(send.at[1, far + other], gather.at[place_in], send_sem.at[2 * LEVELS], gather_sem, near + other)
            return carry

        lax.fori_loop(1, half_count, one, 0)
        pltpu.make_async_copy(send.at[1, mirror], gather.at[place_in], gather_sem).start()

    def one_level(level, carry):
        spread[...] = jnp.dot(weighted[...], table[...], preferred_element_type=jnp.float32)
        coefs = coefficients()
        for which in range(4):
            for first in range(0, second_rows, HALO):
                rows = slice(first, first + HALO)
                lines = slice(which * second_rows + first, which * second_rows + first + HALO)
                twist_cos, twist_sin = twist[0, rows, :], twist[1, rows, :]
                one_imag, one_real = spread[lines, :first_rows], spread[lines, first_rows:]
                middle[which, first : first + HALO, :] = (one_real * twist_cos + one_imag * twist_sin).astype(jnp.bfloat16)
                middle[which, second_rows + first : second_rows + first + HALO, :] = (
                    one_imag * twist_cos - one_real * twist_sin
                ).astype(jnp.bfloat16)

        first_row = (1 - side) * (half_rows - HALO)
        first_size = half_rows // 2 + 2 * HALO
        second_stage(coefs, first_row, first_size)
        place(level, far, half_count // 2)

        @pl.when(jnp.logical_and(level == 0, is_early))
        def _():
            pl.semaphore_wait(barrier, early_count - 1)

        @pl.when(level == 0)
        def _():
            ship_far(0, pl.ds(0, 1), 0, half_count // 2, ascending=True)

        second_stage(coefs, first_row + first_size, half_rows + HALO - first_size)
        place(level, far + half_count // 2, half_count // 2)

        @pl.when(jnp.logical_and(level == 0, side == 0))
        def _():
            pl.semaphore_wait(late_sem, late_count)

        @pl.when(level == 0)
        def _():
            ship_far(0, pl.ds(0, 1), half_count // 2, half_count, ascending=True)

        second_stage(coefs, side * (half_rows + HALO), half_rows - HALO)
        place(level, near, half_count)

        @pl.when(jnp.logical_and(level == 0, jnp.logical_and(side == 1, is_early)))
        def _():
            pl.semaphore_wait(late_sem, late_count)

        @pl.when(level == 0)
        def _():
            ship_base()

        @pl.when(level == LEVELS - 1)
        def _():
            pltpu.make_async_copy(gather, gather, gather_sem).wait()
            total_far[...] = jnp.sum(gather[...], axis=0)
            push(total_far, from_far, total_sem.at[0], total_sem.at[1], mirror)

        ship_near(level)

        @pl.when(level > 0)
        def _():
            ship_far(level, pl.ds(2 * level, 2))

        @pl.when(level < LEVELS - 1)
        def _():
            chirp_load(level + 1).wait()
            demodulate(level + 1)

        return carry

    lax.fori_loop(0, LEVELS, one_level, 0)

    far_devices, near_devices = pl.ds(pl.multiple_of(far, half_count), half_count), pl.ds(pl.multiple_of(near, half_count), half_count)
    await_bytes = lambda part, arrived: pltpu.make_async_copy(part, part, arrived).wait()

    channels = [channel for channel in range(KCOH) if channel != 1]
    names = tracks.shape[1]
    same = lax.broadcasted_iota(jnp.int32, (names, names), 0) == lax.broadcasted_iota(jnp.int32, (names, names), 1)
    loads[5].wait()
    for target, group in ((picks, channels[:-2]), (last_picks, channels[-2:])):
        chosen = []
        for channel in group:
            rate = LEVELS + channel // 2 if channel % 2 == 0 else LEVELS - 1 - channel // 2
            chosen += [jnp.where(tracks[...] == rate, 1.0, 0.0).astype(jnp.bfloat16)] * 2
        target[...] = lax.dot_general(
            jnp.where(same, 1.0, 0.0).astype(jnp.bfloat16), jnp.concatenate(chosen, axis=0), (((1,), (1,)), ((), ())),
            preferred_element_type=jnp.float32,
        ).astype(jnp.bfloat16)

    def arrive(level):
        pair = pl.ds(2 * level, 2)
        await_bytes(recv.at[pair, :, near_devices], near_sem.at[level])
        await_bytes(recv.at[pair if level else pl.ds(0, 1), :, far_devices], far_sem.at[level])

    def stage(step, channel):
        line = step * 2 * count
        for block in range(blocks):
            value = recv[channel, block]
            high = value.astype(jnp.bfloat16)
            lanes = slice(block * BLK, (block + 1) * BLK)
            staged[line : line + count, lanes] = high
            staged[line + count : line + 2 * count, lanes] = (value - high.astype(jnp.float32)).astype(jnp.bfloat16)

    for level in range(LEVELS - 1):
        arrive(level)
        for step, channel in enumerate(channels):
            if channel // 2 == level:
                stage(step, channel)
    await_bytes(from_far, total_sem.at[1])
    base = jnp.sum(recv[1, :, near_devices], axis=1) + from_far[...]
    width = halves * BLK
    parts = blocks // halves
    for part in range(parts):
        columns = slice(part * width, (part + 1) * width)
        line = jnp.concatenate([base[part * halves + half : part * halves + half + 1, :] for half in range(halves)], axis=1)
        out_ref[:, columns] = line + jnp.dot(
            picks[...], staged[:, columns], preferred_element_type=jnp.float32
        )
    arrive(LEVELS - 1)
    for level in range(LEVELS):
        pair = pl.ds(2 * level, 2)
        await_bytes(send.at[pair if level else pl.ds(0, 1), pl.ds(0, half_count)], send_sem.at[level])
        await_bytes(send.at[pair, pl.ds(0, half_count - 1)], send_sem.at[LEVELS + level])
    await_bytes(send.at[1, pl.ds(0, half_count - 1)], send_sem.at[2 * LEVELS])
    await_bytes(total_far, total_sem.at[0])


def finish(segments, partial_ref, recv_ref, picks_ref, out_hbm, summed, sem):
    _, blocks, _, lanes = recv_ref.shape
    parts = blocks // HALVES
    width = HALVES * lanes
    group = max(parts // 4, 1)
    copies = []
    for part in range(parts):
        columns = slice(part * width, (part + 1) * width)
        lines = []
        for channel in (KCOH - 2, KCOH - 1):
            value = jnp.concatenate([recv_ref[channel, part * HALVES + half] for half in range(HALVES)], axis=1)
            high = value.astype(jnp.bfloat16)
            lines += [high, (value - high.astype(jnp.float32)).astype(jnp.bfloat16)]
        total = partial_ref[:, columns] + jnp.dot(
            picks_ref[...], jnp.concatenate(lines, axis=0), preferred_element_type=jnp.float32
        )
        summed[:, columns] = total * (1.0 / segments)
        if (part + 1) % group == 0:
            done = slice((part + 1 - group) * width, (part + 1) * width)
            copies.append(pltpu.make_async_copy(summed.at[:, done], out_hbm.at[:, done], sem.at[len(copies)]))
            copies[-1].start()
    for copy in copies:
        copy.wait()


def local(count, strain_series, antenna, drift, tracks):
    points = strain_series.shape[2]
    first_rows, second_rows = DFT_ROWS, points // DFT_ROWS
    segments = tracks.shape[1]
    blocks = points // count // BLK
    blocked = lambda array: array.reshape(2, points // BLK, BLK).transpose(1, 0, 2).reshape(2 * points // BLK, BLK)
    hbm = pl.BlockSpec(memory_space=pl.ANY)
    vmem = pl.BlockSpec(memory_space=pltpu.VMEM)
    chirps = chirp_table(points, first_rows)
    factors = twist_factors(points, first_rows)
    block = (2 * points // BLK, BLK)
    partial, received, picks = pl.pallas_call(
        functools.partial(kernel, count),
        out_shape=(
            pltpu.VMEM((tracks.shape[0], points // count), jnp.float32),
            pltpu.VMEM((KCOH, blocks, count, BLK), jnp.float32),
            pltpu.VMEM((tracks.shape[0], 4 * count), jnp.bfloat16),
        ),
        in_specs=[hbm] * 7,
        out_specs=(vmem, vmem, vmem),
        scratch_shapes=[
            pltpu.SMEM(drift.shape, jnp.int32),
            pltpu.VMEM(block, jnp.bfloat16),
            pltpu.VMEM(block, jnp.float32),
            pltpu.VMEM(block, jnp.float32),
            pltpu.VMEM(chirps.shape, jnp.float32),
            pltpu.VMEM(factors.shape, jnp.float32),
            pltpu.VMEM((2, second_rows, first_rows), jnp.float32),
            pltpu.VMEM((2 * first_rows, 2 * first_rows), jnp.bfloat16),
            pltpu.VMEM((segments, tracks.shape[0]), jnp.int32),
            pltpu.VMEM((2, second_rows, first_rows), jnp.float32),
            pltpu.VMEM((2, second_rows, first_rows), jnp.float32),
            pltpu.VMEM((4 * second_rows, 2 * first_rows), jnp.bfloat16),
            pltpu.VMEM((4 * second_rows, 2 * first_rows), jnp.float32),
            pltpu.VMEM((4, 2 * second_rows, first_rows), jnp.bfloat16),
            pltpu.VMEM((4, second_rows + 2 * HALO, first_rows), jnp.float32),
            pltpu.VMEM((2, points // BLK + 2 * PAD, BLK), jnp.float32),
            pltpu.VMEM((KCOH, count, blocks, BLK), jnp.float32),
            pltpu.VMEM((count // 2, blocks, BLK), jnp.float32),
            pltpu.VMEM((blocks, BLK), jnp.float32),
            pltpu.VMEM((blocks, BLK), jnp.float32),
            pltpu.VMEM((tracks.shape[0], (KCOH - 3) * 2 * count), jnp.bfloat16),
            pltpu.VMEM(((KCOH - 3) * 2 * count, points // count), jnp.bfloat16),
            pltpu.SemaphoreType.DMA((6,)),
            pltpu.SemaphoreType.DMA((LEVELS,)),
            pltpu.SemaphoreType.DMA((2 * LEVELS + 1,)),
            pltpu.SemaphoreType.DMA((LEVELS,)),
            pltpu.SemaphoreType.DMA((LEVELS,)),
            pltpu.SemaphoreType.DMA,
            pltpu.SemaphoreType.DMA((2,)),
            pltpu.SemaphoreType.REGULAR,
        ],
        compiler_params=pltpu.CompilerParams(
            collective_id=0, has_side_effects=True, vmem_limit_bytes=60 << 20
        ),
    )(
        drift,
        blocked(strain_series),
        blocked(antenna),
        jnp.asarray(chirps),
        jnp.asarray(factors),
        jnp.asarray(dft_table(first_rows)),
        tracks.T,
    )
    parts = max(blocks // HALVES, 1)
    return pl.pallas_call(
        functools.partial(finish, segments),
        out_shape=jax.ShapeDtypeStruct(partial.shape, jnp.float32),
        in_specs=[vmem] * 3,
        out_specs=hbm,
        scratch_shapes=[pltpu.VMEM(partial.shape, jnp.float32), pltpu.SemaphoreType.DMA((min(parts, 8),))],
        compiler_params=pltpu.CompilerParams(vmem_limit_bytes=8 << 20),
    )(partial, received, picks)


def solution(mesh):
    return jax.shard_map(
        functools.partial(local, mesh.shape["seg"]),
        mesh=mesh,
        in_specs=(
            P(("sky", "seg"), None, None),
            P(("sky", "seg"), None, None),
            P(("sky", "seg"), None),
            P(),
        ),
        out_specs=P("sky", "seg"),
        check_vma=False,
    )
```

```python
import functools
import math

import jax
import jax.numpy as jnp
import numpy as np
from jax import lax
from jax.experimental import pallas as pl
from jax.experimental.pallas import tpu as pltpu
from jax.sharding import PartitionSpec as P

DFT_ROWS = 256
BLK = 128
KCOH = 6
LEVELS = KCOH // 2
PAD = 8
HALO = 16
SUB = 8
HALVES = DFT_ROWS // BLK
MESH = pl.DeviceIdType.MESH

chirp_step = 3.0
tiny_eps = 1e-06


def dft_table(rows):
    index = np.arange(rows, dtype=np.int64)
    angle = np.float32(2.0 * math.pi / rows) * (index[:, None] * index[None, :] % rows).astype(np.float32)
    cos, sin = np.cos(angle), np.sin(angle)
    return np.block([[cos, sin], [-sin, cos]]).astype(jnp.bfloat16)


def twist_factors(points, first_rows):
    second_rows = points // first_rows
    inner = np.concatenate([SUB * np.arange(second_rows // SUB, dtype=np.int64), np.arange(SUB, dtype=np.int64)])
    outer = np.arange(first_rows, dtype=np.int64)
    angle = (2.0 * math.pi / points) * (inner[:, None] * outer[None, :] % points).astype(np.float64)
    return np.stack([np.cos(angle), np.sin(angle)]).astype(np.float32)


def chirp_table(points, first_rows):
    position = np.arange(points, dtype=np.float32) / np.float32(points)
    rate = (np.arange(LEVELS, KCOH, dtype=np.float32) - np.float32((KCOH - 1) / 2.0)) * np.float32(chirp_step)
    phases = (np.float32(2.0 * math.pi) * rate)[:, None] * (position * position)[None, :]
    both = np.stack([np.cos(phases), np.sin(phases)], 1).astype(np.float32)
    return np.swapaxes(both.reshape(LEVELS, 2, first_rows, points // first_rows), 2, 3).copy()


def kernel(
    count, drift_hbm, series_hbm, antenna_hbm, chirp_hbm, factors_hbm, table_hbm, tracks_hbm,
    out_ref, recv, last_picks,
    drift, series_in, series, antenna, chirp, factors, twist, table, tracks,
    strain, weights, weighted, spread, middle, spectra, padded,
    send, gather, total_far, from_far, picks, staged,
    load_sem, chirp_sem, send_sem, far_sem, near_sem, gather_sem, total_sem, late_sem,
):
    _, second_rows, first_rows = strain.shape
    halves = first_rows // BLK
    blocks = second_rows * halves // count
    half_count = count // 2
    early_count = half_count + half_count // 2
    late_count = count - early_count
    half_rows = second_rows // 2
    points = first_rows * second_rows
    sky = lax.axis_index("sky")
    me = lax.axis_index("seg")
    side = lax.div(me, half_count)
    place_in = lax.rem(me, half_count)
    far = (1 - side) * half_count
    near = side * half_count
    mirror = far + place_in

    loads = [
        pltpu.make_async_copy(source, target, load_sem.at[index])
        for index, (source, target) in enumerate([
            (series_hbm, series_in), (antenna_hbm, antenna), (table_hbm, table), (factors_hbm, factors), (drift_hbm, drift),
            (tracks_hbm, tracks),
        ])
    ]
    chirp_load = lambda level: pltpu.make_async_copy(chirp_hbm.at[level], chirp.at[level], chirp_sem.at[level])
    loads[0].start()
    loads[3].start()
    loads[1].start()
    chirp_load(0).start()
    for index in (4, 2, 5):
        loads[index].start()

    barrier = pltpu.get_barrier_semaphore()

    is_early = me < early_count

    def signal(semaphore, first, wide):
        def one(step, carry):
            peer = lax.rem(me + step, count) if wide else first + step
            pl.semaphore_signal(semaphore, inc=1, device_id=(sky, peer), device_id_type=MESH)
            return carry

        return one

    @pl.when(is_early)
    def _():
        lax.fori_loop(1, count, signal(barrier, 0, True), 0)

    @pl.when(jnp.logical_not(is_early))
    def _():
        lax.fori_loop(0, me - early_count, signal(barrier, early_count, False), 0)
        lax.fori_loop(me - early_count + 1, late_count, signal(barrier, early_count, False), 0)

    for which in range(2):
        padded[which, :PAD] = jnp.zeros((PAD, BLK), jnp.float32)
        padded[which, PAD + second_rows * halves :] = jnp.zeros((PAD, BLK), jnp.float32)
    send[1] = jnp.zeros(send.shape[1:], jnp.float32)

    @pl.when(jnp.logical_not(is_early))
    def _():
        pl.semaphore_wait(barrier, count - 1)
        lax.fori_loop(0, early_count, signal(late_sem, 0, False), 0)

    pieces = second_rows // BLK

    def turned(source, target):
        for which in range(2):
            for piece in range(pieces):
                lines = pl.ds(2 * piece + which, first_rows, stride=2 * pieces)
                target[which, piece * BLK : (piece + 1) * BLK, :] = source[lines, :].T

    def demodulate(level):
        for first in range(0, second_rows, HALO):
            rows = slice(first, first + HALO)
            chirp_cos, chirp_sin = chirp[level, 0, rows, :], chirp[level, 1, rows, :]
            real, imag = strain[0, rows, :], strain[1, rows, :]
            real_cos, imag_sin = real * chirp_cos, imag * chirp_sin
            imag_cos, real_sin = imag * chirp_cos, real * chirp_sin
            demods = ((real_cos + imag_sin, imag_cos - real_sin), (real_cos - imag_sin, imag_cos + real_sin))
            for kind in range(2):
                weight = weights[kind, rows, :]
                for upper in range(2):
                    start = (2 * upper + kind) * second_rows + first
                    for part in range(2):
                        lanes = slice((1 - part) * first_rows, (2 - part) * first_rows)
                        weighted[start : start + HALO, lanes] = (weight * demods[upper][part]).astype(jnp.bfloat16)

    loads[0].wait()
    series[...] = series_in[...].astype(jnp.float32)
    loads[3].wait()
    turned(series, strain)
    steps = second_rows // SUB
    step_cos, step_sin = factors[0, steps:, :], factors[1, steps:, :]
    for step in range(steps):
        base_cos, base_sin = factors[0, step : step + 1, :], factors[1, step : step + 1, :]
        twist[0, step * SUB : (step + 1) * SUB, :] = base_cos * step_cos - base_sin * step_sin
        twist[1, step * SUB : (step + 1) * SUB, :] = base_sin * step_cos + base_cos * step_sin
    loads[1].wait()
    turned(antenna, weights)
    chirp_load(0).wait()
    demodulate(0)

    def coefficients():
        sums = [0.0, 0.0, 0.0]
        for first in range(0, second_rows, HALO):
            rows = slice(first, first + HALO)
            weight_a, weight_b = weights[0, rows, :], weights[1, rows, :]
            sums = [held + value for held, value in zip(sums, (weight_a * weight_a, weight_b * weight_b, weight_a * weight_b))]
        aa, bb, ab = [jnp.sum(jnp.sum(held, axis=0, keepdims=True), axis=1, keepdims=True) / points for held in sums]
        aa, bb = aa + tiny_eps, bb + tiny_eps
        scale = 1.0 / (points * jnp.maximum(aa * bb - ab * ab, 0.1 * aa * bb))
        return bb * scale, aa * scale, 2.0 * ab * scale

    loads[4].wait()
    loads[2].wait()
    for level in range(1, LEVELS):
        chirp_load(level).start()

    def second_stage(coefs, start, size):
        coef_a, coef_b, coef_ab = coefs
        start = pl.multiple_of(start, HALO)
        lines = jnp.concatenate([table[pl.ds(start, size), :], table[pl.ds(second_rows + start, size), :]], axis=0)
        for which in range(4):
            spectra[which, : 2 * size] = jnp.dot(lines, middle[which], preferred_element_type=jnp.float32)
        for which in range(2):
            for first in range(0, size, HALO):
                real_rows, imag_rows = slice(first, first + HALO), slice(size + first, size + first + HALO)
                a_real, a_imag = spectra[2 * which, real_rows, :], spectra[2 * which, imag_rows, :]
                b_real, b_imag = spectra[2 * which + 1, real_rows, :], spectra[2 * which + 1, imag_rows, :]
                value = (
                    coef_a * (a_real * a_real + a_imag * a_imag)
                    + coef_b * (b_real * b_real + b_imag * b_imag)
                    - coef_ab * (a_real * b_real + a_imag * b_imag)
                )
                for half in range(halves):
                    lines = pl.ds(PAD + halves * (start + first) + half, HALO, stride=halves)
                    padded[which, lines, :] = value[:, half * BLK : (half + 1) * BLK]

    def place(level, first_device, devices_here):
        for which in (1, 0):
            shift = drift[0, (LEVELS + level) if which == 0 else (LEVELS - 1 - level)]
            channel = 2 * level + which
            if blocks % 8 == 0:
                devices = pl.ds(first_device, devices_here)
                value = padded[which, pl.ds(PAD + first_device * blocks - shift, devices_here * blocks), :]
                send[channel, devices] = value.reshape(devices_here, blocks, BLK) - send[1, devices]
            else:
                def one(step, carry, which=which, channel=channel, shift=shift):
                    peer = first_device + step
                    value = padded[which, pl.ds(PAD + peer * blocks - shift, blocks), :]
                    send[channel, peer] = value - send[1, peer]
                    return carry

                lax.fori_loop(0, devices_here, one, 0)

    def push(source, target, done, arrived, peer):
        pltpu.make_async_remote_copy(
            src_ref=source, dst_ref=target, send_sem=done, recv_sem=arrived, device_id=(sky, peer), device_id_type=MESH
        ).start()

    def ship_far(level, channels, first=0, last=half_count, ascending=False):
        def one(step, carry):
            peer = jnp.where(side == 0, half_count + (step if ascending else lax.rem(step + half_count // 2, half_count)), step)
            push(send.at[channels, peer], recv.at[channels, :, me], send_sem.at[level], far_sem.at[level], peer)
            return carry

        lax.fori_loop(first, last, one, 0)

    def ship_near(level):
        channels = pl.ds(2 * level, 2)

        def one(step, carry):
            peer = near + lax.rem(place_in + step, half_count)
            push(send.at[channels, peer], recv.at[channels, :, me], send_sem.at[LEVELS + level], near_sem.at[level], peer)
            return carry

        lax.fori_loop(1, half_count, one, 0)
        pltpu.make_async_copy(send.at[channels, me], recv.at[channels, :, me], near_sem.at[level]).start()

    def ship_base():
        def one(step, carry):
            other = lax.rem(place_in + step, half_count)
            push(send.at[1, far + other], gather.at[place_in], send_sem.at[2 * LEVELS], gather_sem, near + other)
            return carry

        lax.fori_loop(1, half_count, one, 0)
        pltpu.make_async_copy(send.at[1, mirror], gather.at[place_in], gather_sem).start()

    def one_level(level, carry):
        spread[...] = jnp.dot(weighted[...], table[...], preferred_element_type=jnp.float32)
        coefs = coefficients()
        for which in range(4):
            for first in range(0, second_rows, HALO):
                rows = slice(first, first + HALO)
                lines = slice(which * second_rows + first, which * second_rows + first + HALO)
                twist_cos, twist_sin = twist[0, rows, :], twist[1, rows, :]
                one_imag, one_real = spread[lines, :first_rows], spread[lines, first_rows:]
                middle[which, first : first + HALO, :] = (one_real * twist_cos + one_imag * twist_sin).astype(jnp.bfloat16)
                middle[which, second_rows + first : second_rows + first + HALO, :] = (
                    one_imag * twist_cos - one_real * twist_sin
                ).astype(jnp.bfloat16)

        first_row = (1 - side) * (half_rows - HALO)
        first_size = half_rows // 2 + 2 * HALO
        second_stage(coefs, first_row, first_size)
        place(level, far, half_count // 2)

        @pl.when(jnp.logical_and(level == 0, is_early))
        def _():
            pl.semaphore_wait(barrier, early_count - 1)

        @pl.when(level == 0)
        def _():
            ship_far(0, pl.ds(0, 1), 0, half_count // 2, ascending=True)

        second_stage(coefs, first_row + first_size, half_rows + HALO - first_size)
        place(level, far + half_count // 2, half_count // 2)

        @pl.when(jnp.logical_and(level == 0, side == 0))
        def _():
            pl.semaphore_wait(late_sem, late_count)

        @pl.when(level == 0)
        def _():
            ship_far(0, pl.ds(0, 1), half_count // 2, half_count, ascending=True)

        @pl.when(jnp.logical_and(level == 0, jnp.logical_and(side == 1, is_early)))
        def _():
            pl.semaphore_wait(late_sem, late_count)

        second_stage(coefs, side * (half_rows + HALO), half_rows - HALO)
        place(level, near, half_count)

        @pl.when(level == 0)
        def _():
            ship_base()

        ship_near(level)

        @pl.when(level > 0)
        def _():
            ship_far(level, pl.ds(2 * level, 2))

        @pl.when(level == LEVELS - 2)
        def _():
            pltpu.make_async_copy(gather, gather, gather_sem).wait()
            total_far[...] = jnp.sum(gather[...], axis=0)
            push(total_far, from_far, total_sem.at[0], total_sem.at[1], mirror)

        @pl.when(level < LEVELS - 1)
        def _():
            chirp_load(level + 1).wait()
            demodulate(level + 1)

        return carry

    lax.fori_loop(0, LEVELS, one_level, 0)

    far_devices, near_devices = pl.ds(pl.multiple_of(far, half_count), half_count), pl.ds(pl.multiple_of(near, half_count), half_count)
    await_bytes = lambda part, arrived: pltpu.make_async_copy(part, part, arrived).wait()

    channels = [channel for channel in range(KCOH) if channel != 1]
    names = tracks.shape[1]
    same = lax.broadcasted_iota(jnp.int32, (names, names), 0) == lax.broadcasted_iota(jnp.int32, (names, names), 1)
    loads[5].wait()
    for target, group in ((picks, channels[:-2]), (last_picks, channels[-2:])):
        chosen = []
        for channel in group:
            rate = LEVELS + channel // 2 if channel % 2 == 0 else LEVELS - 1 - channel // 2
            chosen += [jnp.where(tracks[...] == rate, 1.0, 0.0).astype(jnp.bfloat16)] * 2
        target[...] = lax.dot_general(
            jnp.where(same, 1.0, 0.0).astype(jnp.bfloat16), jnp.concatenate(chosen, axis=0), (((1,), (1,)), ((), ())),
            preferred_element_type=jnp.float32,
        ).astype(jnp.bfloat16)

    def arrive(level):
        pair = pl.ds(2 * level, 2)
        await_bytes(recv.at[pair, :, near_devices], near_sem.at[level])
        await_bytes(recv.at[pair if level else pl.ds(0, 1), :, far_devices], far_sem.at[level])

    def stage(step, channel):
        line = step * 2 * count
        for block in range(blocks):
            value = recv[channel, block]
            high = value.astype(jnp.bfloat16)
            lanes = slice(block * BLK, (block + 1) * BLK)
            staged[line : line + count, lanes] = high
            staged[line + count : line + 2 * count, lanes] = (value - high.astype(jnp.float32)).astype(jnp.bfloat16)

    for level in range(LEVELS - 1):
        arrive(level)
        for step, channel in enumerate(channels):
            if channel // 2 == level:
                stage(step, channel)
    await_bytes(from_far, total_sem.at[1])
    base = jnp.sum(recv[1, :, near_devices], axis=1) + from_far[...]
    width = halves * BLK
    parts = blocks // halves
    for part in range(parts):
        columns = slice(part * width, (part + 1) * width)
        line = jnp.concatenate([base[part * halves + half : part * halves + half + 1, :] for half in range(halves)], axis=1)
        out_ref[:, columns] = line + jnp.dot(
            picks[...], staged[:, columns], preferred_element_type=jnp.float32
        )
    for level in range(LEVELS):
        if level == LEVELS - 1:
            await_bytes(send.at[1, pl.ds(0, half_count - 1)], send_sem.at[2 * LEVELS])
            await_bytes(total_far, total_sem.at[0])
            arrive(level)
        pair = pl.ds(2 * level, 2)
        await_bytes(send.at[pair if level else pl.ds(0, 1), pl.ds(0, half_count)], send_sem.at[level])
        await_bytes(send.at[pair, pl.ds(0, half_count - 1)], send_sem.at[LEVELS + level])


def finish(segments, partial_ref, recv_ref, picks_ref, out_hbm, summed, sem):
    _, blocks, _, lanes = recv_ref.shape
    parts = blocks // HALVES
    width = HALVES * lanes
    group = max(parts // 4, 1)
    copies = []
    for part in range(parts):
        columns = slice(part * width, (part + 1) * width)
        lines = []
        for channel in (KCOH - 2, KCOH - 1):
            value = jnp.concatenate([recv_ref[channel, part * HALVES + half] for half in range(HALVES)], axis=1)
            high = value.astype(jnp.bfloat16)
            lines += [high, (value - high.astype(jnp.float32)).astype(jnp.bfloat16)]
        total = partial_ref[:, columns] + jnp.dot(
            picks_ref[...], jnp.concatenate(lines, axis=0), preferred_element_type=jnp.float32
        )
        summed[:, columns] = total * (1.0 / segments)
        if (part + 1) % group == 0:
            done = slice((part + 1 - group) * width, (part + 1) * width)
            copies.append(pltpu.make_async_copy(summed.at[:, done], out_hbm.at[:, done], sem.at[len(copies)]))
            copies[-1].start()
    for copy in copies:
        copy.wait()


def local(count, strain_series, antenna, drift, tracks):
    points = strain_series.shape[2]
    first_rows, second_rows = DFT_ROWS, points // DFT_ROWS
    segments = tracks.shape[1]
    blocks = points // count // BLK
    blocked = lambda array: array.reshape(2, points // BLK, BLK).transpose(1, 0, 2).reshape(2 * points // BLK, BLK)
    hbm = pl.BlockSpec(memory_space=pl.ANY)
    vmem = pl.BlockSpec(memory_space=pltpu.VMEM)
    chirps = chirp_table(points, first_rows)
    factors = twist_factors(points, first_rows)
    block = (2 * points // BLK, BLK)
    partial, received, picks = pl.pallas_call(
        functools.partial(kernel, count),
        out_shape=(
            pltpu.VMEM((tracks.shape[0], points // count), jnp.float32),
            pltpu.VMEM((KCOH, blocks, count, BLK), jnp.float32),
            pltpu.VMEM((tracks.shape[0], 4 * count), jnp.bfloat16),
        ),
        in_specs=[hbm] * 7,
        out_specs=(vmem, vmem, vmem),
        scratch_shapes=[
            pltpu.SMEM(drift.shape, jnp.int32),
            pltpu.VMEM(block, jnp.bfloat16),
            pltpu.VMEM(block, jnp.float32),
            pltpu.VMEM(block, jnp.float32),
            pltpu.VMEM(chirps.shape, jnp.float32),
            pltpu.VMEM(factors.shape, jnp.float32),
            pltpu.VMEM((2, second_rows, first_rows), jnp.float32),
            pltpu.VMEM((2 * first_rows, 2 * first_rows), jnp.bfloat16),
            pltpu.VMEM((segments, tracks.shape[0]), jnp.int32),
            pltpu.VMEM((2, second_rows, first_rows), jnp.float32),
            pltpu.VMEM((2, second_rows, first_rows), jnp.float32),
            pltpu.VMEM((4 * second_rows, 2 * first_rows), jnp.bfloat16),
            pltpu.VMEM((4 * second_rows, 2 * first_rows), jnp.float32),
            pltpu.VMEM((4, 2 * second_rows, first_rows), jnp.bfloat16),
            pltpu.VMEM((4, second_rows + 2 * HALO, first_rows), jnp.float32),
            pltpu.VMEM((2, points // BLK + 2 * PAD, BLK), jnp.float32),
            pltpu.VMEM((KCOH, count, blocks, BLK), jnp.float32),
            pltpu.VMEM((count // 2, blocks, BLK), jnp.float32),
            pltpu.VMEM((blocks, BLK), jnp.float32),
            pltpu.VMEM((blocks, BLK), jnp.float32),
            pltpu.VMEM((tracks.shape[0], (KCOH - 3) * 2 * count), jnp.bfloat16),
            pltpu.VMEM(((KCOH - 3) * 2 * count, points // count), jnp.bfloat16),
            pltpu.SemaphoreType.DMA((6,)),
            pltpu.SemaphoreType.DMA((LEVELS,)),
            pltpu.SemaphoreType.DMA((2 * LEVELS + 1,)),
            pltpu.SemaphoreType.DMA((LEVELS,)),
            pltpu.SemaphoreType.DMA((LEVELS,)),
            pltpu.SemaphoreType.DMA,
            pltpu.SemaphoreType.DMA((2,)),
            pltpu.SemaphoreType.REGULAR,
        ],
        compiler_params=pltpu.CompilerParams(
            collective_id=0, has_side_effects=True, vmem_limit_bytes=60 << 20
        ),
    )(
        drift,
        blocked(strain_series),
        blocked(antenna),
        jnp.asarray(chirps),
        jnp.asarray(factors),
        jnp.asarray(dft_table(first_rows)),
        tracks.T,
    )
    parts = max(blocks // HALVES, 1)
    return pl.pallas_call(
        functools.partial(finish, segments),
        out_shape=jax.ShapeDtypeStruct(partial.shape, jnp.float32),
        in_specs=[vmem] * 3,
        out_specs=hbm,
        scratch_shapes=[pltpu.VMEM(partial.shape, jnp.float32), pltpu.SemaphoreType.DMA((min(parts, 8),))],
        compiler_params=pltpu.CompilerParams(vmem_limit_bytes=8 << 20),
    )(partial, received, picks)


def solution(mesh):
    return jax.shard_map(
        functools.partial(local, mesh.shape["seg"]),
        mesh=mesh,
        in_specs=(
            P(("sky", "seg"), None, None),
            P(("sky", "seg"), None, None),
            P(("sky", "seg"), None),
            P(),
        ),
        out_specs=P("sky", "seg"),
        check_vma=False,
    )
```

```python
import functools
import math

import jax
import jax.numpy as jnp
import numpy as np
from jax import lax
from jax.experimental import pallas as pl
from jax.experimental.pallas import tpu as pltpu
from jax.sharding import PartitionSpec as P

DFT_ROWS = 256
BLK = 128
KCOH = 6
LEVELS = KCOH // 2
PAD = 8
HALO = 16
SUB = 8
HALVES = DFT_ROWS // BLK
MESH = pl.DeviceIdType.MESH

chirp_step = 3.0
tiny_eps = 1e-06


def dft_table(rows):
    index = np.arange(rows, dtype=np.int64)
    angle = np.float32(2.0 * math.pi / rows) * (index[:, None] * index[None, :] % rows).astype(np.float32)
    cos, sin = np.cos(angle), np.sin(angle)
    return np.block([[cos, sin], [-sin, cos]]).astype(jnp.bfloat16)


def twist_factors(points, first_rows):
    second_rows = points // first_rows
    inner = np.concatenate([SUB * np.arange(second_rows // SUB, dtype=np.int64), np.arange(SUB, dtype=np.int64)])
    outer = np.arange(first_rows, dtype=np.int64)
    angle = (2.0 * math.pi / points) * (inner[:, None] * outer[None, :] % points).astype(np.float64)
    return np.stack([np.cos(angle), np.sin(angle)]).astype(np.float32)


def chirp_table(points, first_rows):
    position = np.arange(points, dtype=np.float32) / np.float32(points)
    rate = (np.arange(LEVELS, KCOH, dtype=np.float32) - np.float32((KCOH - 1) / 2.0)) * np.float32(chirp_step)
    phases = (np.float32(2.0 * math.pi) * rate)[:, None] * (position * position)[None, :]
    both = np.stack([np.cos(phases), np.sin(phases)], 1).astype(np.float32)
    return np.swapaxes(both.reshape(LEVELS, 2, first_rows, points // first_rows), 2, 3).copy()


def kernel(
    count, drift_hbm, series_hbm, antenna_hbm, chirp_hbm, factors_hbm, table_hbm, tracks_hbm,
    out_ref, recv, last_picks,
    drift, series_in, series, antenna, chirp, factors, twist, table, tracks,
    strain, weights, weighted, spread, middle, spectra, padded,
    send, gather, total_far, from_far, picks, staged,
    load_sem, chirp_sem, send_sem, far_sem, near_sem, gather_sem, total_sem, late_sem,
):
    _, second_rows, first_rows = strain.shape
    halves = first_rows // BLK
    blocks = second_rows * halves // count
    half_count = count // 2
    early_count = half_count + half_count // 2
    late_count = count - early_count
    half_rows = second_rows // 2
    points = first_rows * second_rows
    sky = lax.axis_index("sky")
    me = lax.axis_index("seg")
    side = lax.div(me, half_count)
    place_in = lax.rem(me, half_count)
    far = (1 - side) * half_count
    near = side * half_count
    mirror = far + place_in

    loads = [
        pltpu.make_async_copy(source, target, load_sem.at[index])
        for index, (source, target) in enumerate([
            (series_hbm, series_in), (antenna_hbm, antenna), (table_hbm, table), (factors_hbm, factors), (drift_hbm, drift),
            (tracks_hbm, tracks),
        ])
    ]
    chirp_load = lambda level: pltpu.make_async_copy(chirp_hbm.at[level], chirp.at[level], chirp_sem.at[level])
    loads[0].start()
    loads[3].start()
    loads[1].start()
    chirp_load(0).start()
    for index in (4, 2, 5):
        loads[index].start()

    barrier = pltpu.get_barrier_semaphore()

    is_early = me < early_count

    def signal(semaphore, first, wide):
        def one(step, carry):
            peer = lax.rem(me + step, count) if wide else first + step
            pl.semaphore_signal(semaphore, inc=1, device_id=(sky, peer), device_id_type=MESH)
            return carry

        return one

    @pl.when(is_early)
    def _():
        lax.fori_loop(1, count, signal(barrier, 0, True), 0)

    @pl.when(jnp.logical_not(is_early))
    def _():
        lax.fori_loop(0, me - early_count, signal(barrier, early_count, False), 0)
        lax.fori_loop(me - early_count + 1, late_count, signal(barrier, early_count, False), 0)

    for which in range(2):
        padded[which, :PAD] = jnp.zeros((PAD, BLK), jnp.float32)
        padded[which, PAD + second_rows * halves :] = jnp.zeros((PAD, BLK), jnp.float32)
    send[1] = jnp.zeros(send.shape[1:], jnp.float32)

    @pl.when(jnp.logical_not(is_early))
    def _():
        pl.semaphore_wait(barrier, count - 1)
        lax.fori_loop(0, early_count, signal(late_sem, 0, False), 0)

    pieces = second_rows // BLK

    def turned(source, target):
        for which in range(2):
            for piece in range(pieces):
                lines = pl.ds(2 * piece + which, first_rows, stride=2 * pieces)
                target[which, piece * BLK : (piece + 1) * BLK, :] = source[lines, :].T

    def demodulate(level):
        for first in range(0, second_rows, HALO):
            rows = slice(first, first + HALO)
            chirp_cos, chirp_sin = chirp[level, 0, rows, :], chirp[level, 1, rows, :]
            real, imag = strain[0, rows, :], strain[1, rows, :]
            real_cos, imag_sin = real * chirp_cos, imag * chirp_sin
            imag_cos, real_sin = imag * chirp_cos, real * chirp_sin
            demods = ((real_cos + imag_sin, imag_cos - real_sin), (real_cos - imag_sin, imag_cos + real_sin))
            for kind in range(2):
                weight = weights[kind, rows, :]
                for upper in range(2):
                    start = (2 * upper + kind) * second_rows + first
                    for part in range(2):
                        lanes = slice((1 - part) * first_rows, (2 - part) * first_rows)
                        weighted[start : start + HALO, lanes] = (weight * demods[upper][part]).astype(jnp.bfloat16)

    loads[0].wait()
    series[...] = series_in[...].astype(jnp.float32)
    loads[3].wait()
    turned(series, strain)
    steps = second_rows // SUB
    step_cos, step_sin = factors[0, steps:, :], factors[1, steps:, :]
    for step in range(steps):
        base_cos, base_sin = factors[0, step : step + 1, :], factors[1, step : step + 1, :]
        twist[0, step * SUB : (step + 1) * SUB, :] = base_cos * step_cos - base_sin * step_sin
        twist[1, step * SUB : (step + 1) * SUB, :] = base_sin * step_cos + base_cos * step_sin
    loads[1].wait()
    turned(antenna, weights)
    chirp_load(0).wait()
    demodulate(0)

    def coefficients():
        sums = [0.0, 0.0, 0.0]
        for first in range(0, second_rows, HALO):
            rows = slice(first, first + HALO)
            weight_a, weight_b = weights[0, rows, :], weights[1, rows, :]
            sums = [held + value for held, value in zip(sums, (weight_a * weight_a, weight_b * weight_b, weight_a * weight_b))]
        aa, bb, ab = [jnp.sum(jnp.sum(held, axis=0, keepdims=True), axis=1, keepdims=True) / points for held in sums]
        aa, bb = aa + tiny_eps, bb + tiny_eps
        scale = 1.0 / (points * jnp.maximum(aa * bb - ab * ab, 0.1 * aa * bb))
        return bb * scale, aa * scale, 2.0 * ab * scale

    loads[4].wait()
    loads[2].wait()
    for level in range(1, LEVELS):
        chirp_load(level).start()

    def second_stage(coefs, start, size):
        coef_a, coef_b, coef_ab = coefs
        start = pl.multiple_of(start, HALO)
        lines = jnp.concatenate([table[pl.ds(start, size), :], table[pl.ds(second_rows + start, size), :]], axis=0)
        for which in range(4):
            spectra[which, : 2 * size] = jnp.dot(lines, middle[which], preferred_element_type=jnp.float32)
        for which in range(2):
            for first in range(0, size, HALO):
                real_rows, imag_rows = slice(first, first + HALO), slice(size + first, size + first + HALO)
                a_real, a_imag = spectra[2 * which, real_rows, :], spectra[2 * which, imag_rows, :]
                b_real, b_imag = spectra[2 * which + 1, real_rows, :], spectra[2 * which + 1, imag_rows, :]
                value = (
                    coef_a * (a_real * a_real + a_imag * a_imag)
                    + coef_b * (b_real * b_real + b_imag * b_imag)
                    - coef_ab * (a_real * b_real + a_imag * b_imag)
                )
                for half in range(halves):
                    lines = pl.ds(PAD + halves * (start + first) + half, HALO, stride=halves)
                    padded[which, lines, :] = value[:, half * BLK : (half + 1) * BLK]

    def place(level, first_device, devices_here):
        for which in (1, 0):
            shift = drift[0, (LEVELS + level) if which == 0 else (LEVELS - 1 - level)]
            channel = 2 * level + which
            if blocks % 8 == 0:
                devices = pl.ds(first_device, devices_here)
                value = padded[which, pl.ds(PAD + first_device * blocks - shift, devices_here * blocks), :]
                send[channel, devices] = value.reshape(devices_here, blocks, BLK) - send[1, devices]
            else:
                def one(step, carry, which=which, channel=channel, shift=shift):
                    peer = first_device + step
                    value = padded[which, pl.ds(PAD + peer * blocks - shift, blocks), :]
                    send[channel, peer] = value - send[1, peer]
                    return carry

                lax.fori_loop(0, devices_here, one, 0)

    def push(source, target, done, arrived, peer):
        pltpu.make_async_remote_copy(
            src_ref=source, dst_ref=target, send_sem=done, recv_sem=arrived, device_id=(sky, peer), device_id_type=MESH
        ).start()

    def ship_far(level, channels, first=0, last=half_count, ascending=False):
        def one(step, carry):
            peer = jnp.where(side == 0, half_count + (step if ascending else lax.rem(step + half_count // 2, half_count)), step)
            push(send.at[channels, peer], recv.at[channels, :, me], send_sem.at[level], far_sem.at[level], peer)
            return carry

        lax.fori_loop(first, last, one, 0)

    def ship_near(level):
        channels = pl.ds(2 * level, 2)

        def one(step, carry):
            peer = near + lax.rem(place_in + step, half_count)
            push(send.at[channels, peer], recv.at[channels, :, me], send_sem.at[LEVELS + level], near_sem.at[level], peer)
            return carry

        lax.fori_loop(1, half_count, one, 0)
        pltpu.make_async_copy(send.at[channels, me], recv.at[channels, :, me], near_sem.at[level]).start()

    def ship_base():
        def one(step, carry):
            other = lax.rem(place_in + step, half_count)
            push(send.at[1, far + other], gather.at[place_in], send_sem.at[2 * LEVELS], gather_sem, near + other)
            return carry

        lax.fori_loop(1, half_count, one, 0)
        pltpu.make_async_copy(send.at[1, mirror], gather.at[place_in], gather_sem).start()

    def one_level(level, carry):
        spread[...] = jnp.dot(weighted[...], table[...], preferred_element_type=jnp.float32)
        coefs = coefficients()
        for which in range(4):
            for first in range(0, second_rows, HALO):
                rows = slice(first, first + HALO)
                lines = slice(which * second_rows + first, which * second_rows + first + HALO)
                twist_cos, twist_sin = twist[0, rows, :], twist[1, rows, :]
                one_imag, one_real = spread[lines, :first_rows], spread[lines, first_rows:]
                middle[which, first : first + HALO, :] = (one_real * twist_cos + one_imag * twist_sin).astype(jnp.bfloat16)
                middle[which, second_rows + first : second_rows + first + HALO, :] = (
                    one_imag * twist_cos - one_real * twist_sin
                ).astype(jnp.bfloat16)

        first_row = (1 - side) * (half_rows - HALO)
        first_size = half_rows // 2 + 2 * HALO
        second_stage(coefs, first_row, first_size)
        place(level, far, half_count // 2)

        @pl.when(jnp.logical_and(level == 0, is_early))
        def _():
            pl.semaphore_wait(barrier, early_count - 1)

        @pl.when(level == 0)
        def _():
            ship_far(0, pl.ds(0, 1), 0, half_count // 2, ascending=True)

        second_stage(coefs, first_row + first_size, half_rows + HALO - first_size)
        place(level, far + half_count // 2, half_count // 2)

        @pl.when(jnp.logical_and(level == 0, side == 0))
        def _():
            pl.semaphore_wait(late_sem, late_count)

        @pl.when(level == 0)
        def _():
            ship_far(0, pl.ds(0, 1), half_count // 2, half_count, ascending=True)

        second_stage(coefs, side * (half_rows + HALO), half_rows - HALO)
        place(level, near, half_count)

        @pl.when(jnp.logical_and(level == 0, jnp.logical_and(side == 1, is_early)))
        def _():
            pl.semaphore_wait(late_sem, late_count)

        @pl.when(level == 0)
        def _():
            ship_base()

        ship_near(level)

        @pl.when(level > 0)
        def _():
            ship_far(level, pl.ds(2 * level, 2))

        @pl.when(level == LEVELS - 2)
        def _():
            pltpu.make_async_copy(gather, gather, gather_sem).wait()
            total_far[...] = jnp.sum(gather[...], axis=0)
            push(total_far, from_far, total_sem.at[0], total_sem.at[1], mirror)

        @pl.when(level < LEVELS - 1)
        def _():
            chirp_load(level + 1).wait()
            demodulate(level + 1)

        return carry

    lax.fori_loop(0, LEVELS, one_level, 0)

    far_devices, near_devices = pl.ds(pl.multiple_of(far, half_count), half_count), pl.ds(pl.multiple_of(near, half_count), half_count)
    await_bytes = lambda part, arrived: pltpu.make_async_copy(part, part, arrived).wait()

    channels = [channel for channel in range(KCOH) if channel != 1]
    names = tracks.shape[1]
    same = lax.broadcasted_iota(jnp.int32, (names, names), 0) == lax.broadcasted_iota(jnp.int32, (names, names), 1)
    loads[5].wait()
    for target, group in ((picks, channels[:-2]), (last_picks, channels[-2:])):
        chosen = []
        for channel in group:
            rate = LEVELS + channel // 2 if channel % 2 == 0 else LEVELS - 1 - channel // 2
            chosen += [jnp.where(tracks[...] == rate, 1.0, 0.0).astype(jnp.bfloat16)] * 2
        target[...] = lax.dot_general(
            jnp.where(same, 1.0, 0.0).astype(jnp.bfloat16), jnp.concatenate(chosen, axis=0), (((1,), (1,)), ((), ())),
            preferred_element_type=jnp.float32,
        ).astype(jnp.bfloat16)

    def arrive(level):
        pair = pl.ds(2 * level, 2)
        await_bytes(recv.at[pair, :, near_devices], near_sem.at[level])
        await_bytes(recv.at[pair if level else pl.ds(0, 1), :, far_devices], far_sem.at[level])

    def stage(step, channel):
        line = step * 2 * count
        for block in range(blocks):
            value = recv[channel, block]
            high = value.astype(jnp.bfloat16)
            lanes = slice(block * BLK, (block + 1) * BLK)
            staged[line : line + count, lanes] = high
            staged[line + count : line + 2 * count, lanes] = (value - high.astype(jnp.float32)).astype(jnp.bfloat16)

    for level in range(LEVELS - 1):
        arrive(level)
        for step, channel in enumerate(channels):
            if channel // 2 == level:
                stage(step, channel)
    await_bytes(from_far, total_sem.at[1])
    base = jnp.sum(recv[1, :, near_devices], axis=1) + from_far[...]
    width = halves * BLK
    parts = blocks // halves
    for part in range(parts):
        columns = slice(part * width, (part + 1) * width)
        line = jnp.concatenate([base[part * halves + half : part * halves + half + 1, :] for half in range(halves)], axis=1)
        out_ref[:, columns] = line + jnp.dot(
            picks[...], staged[:, columns], preferred_element_type=jnp.float32
        )
    arrive(LEVELS - 1)
    for level in range(LEVELS):
        pair = pl.ds(2 * level, 2)
        await_bytes(send.at[pair if level else pl.ds(0, 1), pl.ds(0, half_count)], send_sem.at[level])
        await_bytes(send.at[pair, pl.ds(0, half_count - 1)], send_sem.at[LEVELS + level])
    await_bytes(send.at[1, pl.ds(0, half_count - 1)], send_sem.at[2 * LEVELS])
    await_bytes(total_far, total_sem.at[0])


def finish(segments, partial_ref, recv_ref, picks_ref, out_hbm, summed, sem):
    _, blocks, _, lanes = recv_ref.shape
    parts = blocks // HALVES
    width = HALVES * lanes
    group = max(parts // 4, 1)
    copies = []
    for part in range(parts):
        columns = slice(part * width, (part + 1) * width)
        lines = []
        for channel in (KCOH - 2, KCOH - 1):
            value = jnp.concatenate([recv_ref[channel, part * HALVES + half] for half in range(HALVES)], axis=1)
            high = value.astype(jnp.bfloat16)
            lines += [high, (value - high.astype(jnp.float32)).astype(jnp.bfloat16)]
        total = partial_ref[:, columns] + jnp.dot(
            picks_ref[...], jnp.concatenate(lines, axis=0), preferred_element_type=jnp.float32
        )
        summed[:, columns] = total * (1.0 / segments)
        if (part + 1) % group == 0:
            done = slice((part + 1 - group) * width, (part + 1) * width)
            copies.append(pltpu.make_async_copy(summed.at[:, done], out_hbm.at[:, done], sem.at[len(copies)]))
            copies[-1].start()
    for copy in copies:
        copy.wait()


def local(count, strain_series, antenna, drift, tracks):
    points = strain_series.shape[2]
    first_rows, second_rows = DFT_ROWS, points // DFT_ROWS
    segments = tracks.shape[1]
    blocks = points // count // BLK
    blocked = lambda array: array.reshape(2, points // BLK, BLK).transpose(1, 0, 2).reshape(2 * points // BLK, BLK)
    hbm = pl.BlockSpec(memory_space=pl.ANY)
    vmem = pl.BlockSpec(memory_space=pltpu.VMEM)
    chirps = chirp_table(points, first_rows)
    factors = twist_factors(points, first_rows)
    block = (2 * points // BLK, BLK)
    partial, received, picks = pl.pallas_call(
        functools.partial(kernel, count),
        out_shape=(
            pltpu.VMEM((tracks.shape[0], points // count), jnp.float32),
            pltpu.VMEM((KCOH, blocks, count, BLK), jnp.float32),
            pltpu.VMEM((tracks.shape[0], 4 * count), jnp.bfloat16),
        ),
        in_specs=[hbm] * 7,
        out_specs=(vmem, vmem, vmem),
        scratch_shapes=[
            pltpu.SMEM(drift.shape, jnp.int32),
            pltpu.VMEM(block, jnp.bfloat16),
            pltpu.VMEM(block, jnp.float32),
            pltpu.VMEM(block, jnp.float32),
            pltpu.VMEM(chirps.shape, jnp.float32),
            pltpu.VMEM(factors.shape, jnp.float32),
            pltpu.VMEM((2, second_rows, first_rows), jnp.float32),
            pltpu.VMEM((2 * first_rows, 2 * first_rows), jnp.bfloat16),
            pltpu.VMEM((segments, tracks.shape[0]), jnp.int32),
            pltpu.VMEM((2, second_rows, first_rows), jnp.float32),
            pltpu.VMEM((2, second_rows, first_rows), jnp.float32),
            pltpu.VMEM((4 * second_rows, 2 * first_rows), jnp.bfloat16),
            pltpu.VMEM((4 * second_rows, 2 * first_rows), jnp.float32),
            pltpu.VMEM((4, 2 * second_rows, first_rows), jnp.bfloat16),
            pltpu.VMEM((4, second_rows + 2 * HALO, first_rows), jnp.float32),
            pltpu.VMEM((2, points // BLK + 2 * PAD, BLK), jnp.float32),
            pltpu.VMEM((KCOH, count, blocks, BLK), jnp.float32),
            pltpu.VMEM((count // 2, blocks, BLK), jnp.float32),
            pltpu.VMEM((blocks, BLK), jnp.float32),
            pltpu.VMEM((blocks, BLK), jnp.float32),
            pltpu.VMEM((tracks.shape[0], (KCOH - 3) * 2 * count), jnp.bfloat16),
            pltpu.VMEM(((KCOH - 3) * 2 * count, points // count), jnp.bfloat16),
            pltpu.SemaphoreType.DMA((6,)),
            pltpu.SemaphoreType.DMA((LEVELS,)),
            pltpu.SemaphoreType.DMA((2 * LEVELS + 1,)),
            pltpu.SemaphoreType.DMA((LEVELS,)),
            pltpu.SemaphoreType.DMA((LEVELS,)),
            pltpu.SemaphoreType.DMA,
            pltpu.SemaphoreType.DMA((2,)),
            pltpu.SemaphoreType.REGULAR,
        ],
        compiler_params=pltpu.CompilerParams(
            collective_id=0, has_side_effects=True, vmem_limit_bytes=60 << 20
        ),
    )(
        drift,
        blocked(strain_series),
        blocked(antenna),
        jnp.asarray(chirps),
        jnp.asarray(factors),
        jnp.asarray(dft_table(first_rows)),
        tracks.T,
    )
    parts = max(blocks // HALVES, 1)
    return pl.pallas_call(
        functools.partial(finish, segments),
        out_shape=jax.ShapeDtypeStruct(partial.shape, jnp.float32),
        in_specs=[vmem] * 3,
        out_specs=hbm,
        scratch_shapes=[pltpu.VMEM(partial.shape, jnp.float32), pltpu.SemaphoreType.DMA((min(parts, 8),))],
        compiler_params=pltpu.CompilerParams(vmem_limit_bytes=8 << 20),
    )(partial, received, picks)


def solution(mesh):
    return jax.shard_map(
        functools.partial(local, mesh.shape["seg"]),
        mesh=mesh,
        in_specs=(
            P(("sky", "seg"), None, None),
            P(("sky", "seg"), None, None),
            P(("sky", "seg"), None),
            P(),
        ),
        out_specs=P("sky", "seg"),
        check_vma=False,
    )
```
